32 devices in a mesh: seq: 8 (over y, x, core), fsdp: 4 (over z).
Axes of the slice: x: 2, y: 2, z: 4, core: 2. Of those that a mesh axis runs over, the one named last changes fastest.
Arguments:
- hidden_in: bfloat16 [4, 2048, 1024], P('fsdp', 'seq'), may hold values from -6 to 6
- cotangent: bfloat16 [4, 2048, 1024], P('fsdp', 'seq'), may hold values from -6 to 6
- doc_position: int32 [4, 2048], P('fsdp', 'seq'), may hold values from 0 to 2047, as said below
- norm_gains: float32 [2, 1024], P(None, ('seq', 'fsdp')), may hold values from 0.5 to 1.5
- conv_taps: float32 [3, 1024], P(None, ('seq', 'fsdp')), may hold values from -3 to 3
- in_proj: float32 [1024, 3072], P(('seq', 'fsdp')), may hold values from -0.1875 to 0.1875
- out_proj: float32 [1024, 1024], P(('seq', 'fsdp')), may hold values from -0.1875 to 0.1875
- gate_up: float32 [1024, 9216], P(('seq', 'fsdp')), may hold values from -0.1875 to 0.1875
- down_proj: float32 [4608, 1024], P(('seq', 'fsdp')), may hold values from -0.09375 to 0.09375
- first_gains: float32 [2, 1024], P(None, ('seq', 'fsdp')), may hold values from -56 to 56
- first_taps: float32 [3, 1024], P(None, ('seq', 'fsdp')), may hold values from -56 to 56
- first_in: float32 [1024, 3072], P(('seq', 'fsdp')), may hold values from -56 to 56
- first_out: float32 [1024, 1024], P(('seq', 'fsdp')), may hold values from -56 to 56
- first_gate_up: float32 [1024, 9216], P(('seq', 'fsdp')), may hold values from -14 to 14
- first_down: float32 [4608, 1024], P(('seq', 'fsdp')), may hold values from -32 to 32
- second_gains: float32 [2, 1024], P(None, ('seq', 'fsdp')), may hold values from 2.4576 to 24.576
- second_taps: float32 [3, 1024], P(None, ('seq', 'fsdp')), may hold values from 2.4576 to 24.576
- second_in: float32 [1024, 3072], P(('seq', 'fsdp')), may hold values from 2.4576 to 24.576
- second_out: float32 [1024, 1024], P(('seq', 'fsdp')), may hold values from 2.4576 to 24.576
- second_gate_up: float32 [1024, 9216], P(('seq', 'fsdp')), may hold values from 0.16384 to 1.6384
- second_down: float32 [4608, 1024], P(('seq', 'fsdp')), may hold values from 0.8192 to 8.192
Outputs:
- block_out: float32 [4, 2048, 1024], P('fsdp', 'seq')
- grad_hidden: float32 [4, 2048, 1024], P('fsdp', 'seq')
- grad_gains: float32 [2, 1024], P(None, ('seq', 'fsdp'))
- grad_taps: float32 [3, 1024], P(None, ('seq', 'fsdp'))
- grad_in: float32 [1024, 3072], P(('seq', 'fsdp'))
- grad_out: float32 [1024, 1024], P(('seq', 'fsdp'))
- grad_gate_up: float32 [1024, 9216], P(('seq', 'fsdp'))
- grad_down: float32 [4608, 1024], P(('seq', 'fsdp'))
- new_gains: float32 [2, 1024], P(None, ('seq', 'fsdp'))
- new_taps: float32 [3, 1024], P(None, ('seq', 'fsdp'))
- new_in: float32 [1024, 3072], P(('seq', 'fsdp'))
- new_out: float32 [1024, 1024], P(('seq', 'fsdp'))
- new_gate_up: float32 [1024, 9216], P(('seq', 'fsdp'))
- new_down: float32 [4608, 1024], P(('seq', 'fsdp'))
- next_first_gains: float32 [2, 1024], P(None, ('seq', 'fsdp'))
- next_first_taps: float32 [3, 1024], P(None, ('seq', 'fsdp'))
- next_first_in: float32 [1024, 3072], P(('seq', 'fsdp'))
- next_first_out: float32 [1024, 1024], P(('seq', 'fsdp'))
- next_first_gate_up: float32 [1024, 9216], P(('seq', 'fsdp'))
- next_first_down: float32 [4608, 1024], P(('seq', 'fsdp'))
- next_second_gains: float32 [2, 1024], P(None, ('seq', 'fsdp'))
- next_second_taps: float32 [3, 1024], P(None, ('seq', 'fsdp'))
- next_second_in: float32 [1024, 3072], P(('seq', 'fsdp'))
- next_second_out: float32 [1024, 1024], P(('seq', 'fsdp'))
- next_second_gate_up: float32 [1024, 9216], P(('seq', 'fsdp'))
- next_second_down: float32 [4608, 1024], P(('seq', 'fsdp'))
The draws below stay inside these ranges and needn't reach their ends.
Inputs may be any that keep to these rules, and one draw needn't show every extreme that they name: doc_position[s, t] is 0 where a packed document starts (always at t = 0) and doc_position[s, t - 1] + 1 elsewhere; sequence 0 holds a single document.
All inputs are finite; a program needn't handle non-finite values.
Results may differ from the reference program's by a relative error of at most 0.012.
The reference program's roundings to bfloat16 on the way (of `normed_one`, `gated_input`, `mixer_act`, `normed_two`, `ffn_act`, `grad_both`, `resid_cast` and `grad_proj`) count: a program that leaves them out, or rounds other values in their place, can miss the bound.
Values may be sent and summed in bfloat16 or wider, within the bound.
A program may use at most 256 MiB of HBM per device.

```python
import math
import jax
import jax.numpy as jnp
from jax import lax

D = 1024
FF = 4608
STEP = 3
SEQS = 4
LEN = 2048
TOKENS = 8192


def draw_doc_position(key, part):
    marks = jax.random.randint(key, (SEQS, LEN), 0, 32)
    places = jnp.broadcast_to(jnp.arange(LEN, dtype=jnp.int32), (SEQS, LEN))
    row_ids = jnp.broadcast_to(jnp.arange(SEQS, dtype=jnp.int32)[:, None], (SEQS, LEN))
    starts = jnp.logical_or(jnp.logical_and(marks == 0, row_ids > 0), places == 0)
    latest = lax.cummax(jnp.where(starts, places, 0), axis=1)
    return (places - latest).astype(jnp.int32)


def block_scale(stream_key, dims, split, low, top_value):
    def one(position, blocks):
        draws = jax.random.uniform(jax.random.fold_in(jax.random.fold_in(stream_key, 6), position), (blocks,), jnp.float32, low / len(split), top_value / len(split))
        return jnp.repeat(jnp.exp(draws), dims[position] // blocks).reshape((-1,) + (1,) * (len(dims) - position - 1))

    loudness = one(*split[0])
    for cut in split[1:]:
        loudness = loudness * one(*cut)
    return loudness


def centred(own_key, shape, scale, most, pieces=(), kind=jnp.bfloat16):
    values = scale * jax.random.normal(own_key, shape, jnp.float32)
    if pieces:
        values = values * block_scale(own_key, shape, pieces, -0.22, 0.18)
    return jnp.clip(values, -most, most).astype(kind)


def setup_inputs(seed: int = 0) -> dict:
    splits = jax.random.split(jax.random.key(seed), 22)
    return {
        "hidden_in": centred(splits[0], (SEQS, LEN, D), 1.0, 6.0, ((0, 4), (1, 8))),
        "cotangent": centred(splits[1], (SEQS, LEN, D), 1.0, 6.0, ((0, 4), (1, 8))),
        "doc_position": draw_doc_position(jax.random.fold_in(splits[21], 71), 0),
        "norm_gains": jnp.clip(1.0 + 0.1 * jax.random.normal(splits[3], (2, D), jnp.float32), 0.5, 1.5),
        "conv_taps": centred(splits[4], (3, D), 0.5, 3.0, ((1, 32),), jnp.float32),
        "in_proj": centred(splits[5], (D, 3 * D), D ** -0.5, 0.1875, ((0, 32),), jnp.float32),
        "out_proj": centred(splits[6], (D, D), D ** -0.5, 0.1875, ((0, 32),), jnp.float32),
        "gate_up": centred(splits[7], (D, 2 * FF), D ** -0.5, 0.1875, ((0, 32),), jnp.float32),
        "down_proj": centred(splits[8], (FF, D), FF ** -0.5, 0.09375, ((0, 32),), jnp.float32),
        "first_gains": centred(splits[9], (2, D), (0.1 * TOKENS ** 0.5), 56.0, ((1, 32),), jnp.float32),
        "first_taps": centred(splits[10], (3, D), (0.1 * TOKENS ** 0.5), 56.0, ((1, 32),), jnp.float32),
        "first_in": centred(splits[11], (D, 3 * D), (0.1 * TOKENS ** 0.5), 56.0, ((0, 32),), jnp.float32),
        "first_out": centred(splits[12], (D, D), (0.1 * TOKENS ** 0.5), 56.0, ((0, 32),), jnp.float32),
        "first_gate_up": centred(splits[13], (D, 2 * FF), (0.025 * TOKENS ** 0.5), 14.0, ((0, 32),), jnp.float32),
        "first_down": centred(splits[14], (FF, D), (0.06 * TOKENS ** 0.5), 32.0, ((0, 32),), jnp.float32),
        "second_gains": jnp.clip(jnp.exp(math.log(24.576) - 2.3025851 * jax.random.uniform(splits[15], (2, D), jnp.float32) ** block_scale(splits[15], (2, D), ((1, 32),), -0.2, 0.2)), 2.4576, 24.576),
        "second_taps": jnp.clip(jnp.exp(math.log(24.576) - 2.3025851 * jax.random.uniform(splits[16], (3, D), jnp.float32) ** block_scale(splits[16], (3, D), ((1, 32),), -0.2, 0.2)), 2.4576, 24.576),
        "second_in": jnp.clip(jnp.exp(math.log(24.576) - 2.3025851 * jax.random.uniform(splits[17], (D, 3 * D), jnp.float32) ** block_scale(splits[17], (D, 3 * D), ((0, 32),), -0.2, 0.2)), 2.4576, 24.576),
        "second_out": jnp.clip(jnp.exp(math.log(24.576) - 2.3025851 * jax.random.uniform(splits[18], (D, D), jnp.float32) ** block_scale(splits[18], (D, D), ((0, 32),), -0.2, 0.2)), 2.4576, 24.576),
        "second_gate_up": jnp.clip(jnp.exp(math.log(1.6384) - 2.3025851 * jax.random.uniform(splits[19], (D, 2 * FF), jnp.float32) ** block_scale(splits[19], (D, 2 * FF), ((0, 32),), -0.2, 0.2)), 0.16384, 1.6384),
        "second_down": jnp.clip(jnp.exp(math.log(8.192) - 2.3025852 * jax.random.uniform(splits[20], (FF, D), jnp.float32) ** block_scale(splits[20], (FF, D), ((0, 32),), -0.2, 0.2)), 0.8192, 8.192),
    }


NORM_EPS = 1e-05
BETA_ONE = 0.9
BETA_TWO = 0.999
ADAM_EPS = 1e-08
RATE_MATRIX = 0.005
RATE_VECTOR = 0.2
DECAY = 0.1

def matmul(left, right):
    return jnp.dot(left, right, preferred_element_type=jnp.float32)

def matmul_tn(left, right):
    return lax.dot_general(left, right, (((0,), (0,)), ((), ())), preferred_element_type=jnp.float32)

def matmul_nt(left, right):
    return lax.dot_general(left, right, (((1,), (1,)), ((), ())), preferred_element_type=jnp.float32)

def inverse_rms(values):
    return lax.rsqrt(lax.optimization_barrier(jnp.mean(values * values, axis=-1, keepdims=True)) + NORM_EPS)

def norm_backward(values, scale, gain, grad_normed):
    weighted = grad_normed * gain
    grad_gain = lax.optimization_barrier(jnp.sum(grad_normed * values * scale, axis=0))
    cubed = scale * scale * scale
    grad_values = scale * weighted - values * cubed * lax.optimization_barrier(jnp.mean(weighted * values, axis=-1, keepdims=True))
    return (grad_values, grad_gain)

def adamw_update(param, grad, first, second, rate, decay):
    first_new = BETA_ONE * first + (1.0 - BETA_ONE) * grad
    second_new = BETA_TWO * second + (1.0 - BETA_TWO) * grad * grad
    first_hat = first_new / (1.0 - BETA_ONE ** STEP)
    second_hat = second_new / (1.0 - BETA_TWO ** STEP)
    param_new = param - rate * (first_hat / (jnp.sqrt(second_hat) + ADAM_EPS) + decay * param)
    return (param_new, first_new, second_new)

def shift_down(values, amount):
    padding = jnp.zeros((amount, values.shape[1]), values.dtype)
    return jnp.concatenate([padding, values[:values.shape[0] - amount]], axis=0)

def shift_up(values, amount):
    padding = jnp.zeros((amount, values.shape[1]), values.dtype)
    return jnp.concatenate([values[amount:], padding], axis=0)

def one_row(params_b, row_in, row_cot, row_pos):
    gains_f = params_b[0].astype(jnp.float32)
    taps_f = params_b[1].astype(jnp.float32)
    in_b = params_b[2]
    out_b = params_b[3]
    gate_up_b = params_b[4]
    down_b = params_b[5]
    width = row_in.shape[1]
    hidden_units = gate_up_b.shape[1] // 2
    resid_one = row_in.astype(jnp.float32)
    scale_one = inverse_rms(resid_one)
    normed_one = (resid_one * scale_one * gains_f[0]).astype(jnp.bfloat16)
    projected = matmul(normed_one, in_b)
    b_branch = projected[:, :width]
    c_branch = projected[:, width:2 * width]
    x_branch = projected[:, 2 * width:]
    gated_input = (b_branch * x_branch).astype(jnp.bfloat16)
    gated_f = gated_input.astype(jnp.float32)
    mask_one = (row_pos >= 1).astype(jnp.float32)[:, None]
    mask_two = (row_pos >= 2).astype(jnp.float32)[:, None]
    prev_one = shift_down(gated_f, 1)
    prev_two = shift_down(gated_f, 2)
    conv_out = taps_f[0] * gated_f + mask_one * taps_f[1] * prev_one + mask_two * taps_f[2] * prev_two
    mixer_act = (c_branch * conv_out).astype(jnp.bfloat16)
    resid_two = resid_one + matmul(mixer_act, out_b)
    scale_two = inverse_rms(resid_two)
    normed_two = (resid_two * scale_two * gains_f[1]).astype(jnp.bfloat16)
    ffn_pre = matmul(normed_two, gate_up_b)
    gate_pre = ffn_pre[:, :hidden_units]
    up_pre = ffn_pre[:, hidden_units:]
    sigmoid_gate = jax.nn.sigmoid(gate_pre)
    silu_gate = gate_pre * sigmoid_gate
    ffn_act = (silu_gate * up_pre).astype(jnp.bfloat16)
    block_out = resid_two + matmul(ffn_act, down_b)
    grad_down = matmul_tn(ffn_act, row_cot)
    grad_act = matmul_nt(row_cot, down_b)
    grad_gate = grad_act * up_pre * sigmoid_gate * (1.0 + gate_pre * (1.0 - sigmoid_gate))
    grad_both = jnp.concatenate([grad_gate, grad_act * silu_gate], axis=1).astype(jnp.bfloat16)
    grad_gate_up = matmul_tn(normed_two, grad_both)
    grad_normed = matmul_nt(grad_both, gate_up_b)
    norm_part, gain_two_grad = norm_backward(resid_two, scale_two, gains_f[1], grad_normed)
    grad_resid = row_cot.astype(jnp.float32) + norm_part
    resid_cast = grad_resid.astype(jnp.bfloat16)
    grad_out = matmul_tn(mixer_act, resid_cast)
    grad_mixer = matmul_nt(resid_cast, out_b)
    grad_cbranch = grad_mixer * conv_out
    grad_conv = grad_mixer * c_branch
    masked_one = mask_one * grad_conv
    masked_two = mask_two * grad_conv
    grad_taps = jnp.stack([lax.optimization_barrier(jnp.sum(grad_conv * gated_f, axis=0)), lax.optimization_barrier(jnp.sum(masked_one * prev_one, axis=0)), lax.optimization_barrier(jnp.sum(masked_two * prev_two, axis=0))])
    grad_gated = taps_f[0] * grad_conv + taps_f[1] * shift_up(masked_one, 1) + taps_f[2] * shift_up(masked_two, 2)
    grad_proj = jnp.concatenate([grad_gated * x_branch, grad_cbranch, grad_gated * b_branch], axis=1).astype(jnp.bfloat16)
    grad_in = matmul_tn(normed_one, grad_proj)
    grad_normone = matmul_nt(grad_proj, in_b)
    first_part, gain_one_grad = norm_backward(resid_one, scale_one, gains_f[0], grad_normone)
    grad_hidden = grad_resid + first_part
    grad_gains = jnp.stack([gain_one_grad, gain_two_grad])
    row_grads = (grad_gains, grad_taps, grad_in, grad_out, grad_gate_up, grad_down)
    return (block_out, grad_hidden, row_grads)

def reference(hidden_in, cotangent, doc_position, norm_gains, conv_taps, in_proj, out_proj, gate_up, down_proj, first_gains, first_taps, first_in, first_out, first_gate_up, first_down, second_gains, second_taps, second_in, second_out, second_gate_up, second_down):
    params = (norm_gains, conv_taps, in_proj, out_proj, gate_up, down_proj)
    firsts = (first_gains, first_taps, first_in, first_out, first_gate_up, first_down)
    seconds = (second_gains, second_taps, second_in, second_out, second_gate_up, second_down)
    params_b = tuple((param.astype(jnp.bfloat16) for param in params))
    zero_grads = tuple((jnp.zeros(param.shape, jnp.float32) for param in params))

    def step_rows(totals, row_items):
        row_in, row_cot, row_pos = row_items
        row_out, row_grad, row_grads = one_row(params_b, row_in, row_cot, row_pos)
        summed = tuple((running + extra for running, extra in zip(totals, row_grads)))
        return (summed, (row_out, row_grad))
    totals, outputs = lax.scan(step_rows, zero_grads, (hidden_in, cotangent, doc_position))
    block_out, grad_hidden = outputs
    rates = (RATE_VECTOR, RATE_VECTOR, RATE_MATRIX, RATE_MATRIX, RATE_MATRIX, RATE_MATRIX)
    decays = (0.0, 0.0, DECAY, DECAY, DECAY, DECAY)
    updated = [adamw_update(params[index], totals[index], firsts[index], seconds[index], rates[index], decays[index]) for index in range(6)]
    return (block_out, grad_hidden, totals[0], totals[1], totals[2], totals[3], totals[4], totals[5], updated[0][0], updated[1][0], updated[2][0], updated[3][0], updated[4][0], updated[5][0], updated[0][1], updated[1][1], updated[2][1], updated[3][1], updated[4][1], updated[5][1], updated[0][2], updated[1][2], updated[2][2], updated[3][2], updated[4][2], updated[5][2])
```

```python
import functools

import jax
import jax.numpy as jnp
from jax import lax
from jax.experimental import pallas as pl
from jax.experimental.pallas import tpu as pltpu
from jax.sharding import Mesh
from jax.sharding import PartitionSpec as P

STEP = 3


NORM_EPS = 1e-05
BETA_ONE = 0.9
BETA_TWO = 0.999
ADAM_EPS = 1e-08
RATE_MATRIX = 0.005
RATE_VECTOR = 0.2
DECAY = 0.1
LANES = 128
MESH_ID = pl.DeviceIdType.MESH
SEQ = ("ring", "core")
ALL = ("ring", "core", "fsdp")


def snake(index):
    return 2 * (index // 2) + (index % 2 + index // 2) % 2


def halves(columns):
    first = (columns // 2 + LANES - 1) // LANES * LANES
    return (pl.ds(0, first), pl.ds(first, columns - first))


class Place:
    def __init__(self, chips, depth):
        self.chips, self.depth = chips, depth
        self.core = lax.axis_index("core")
        self.layer = lax.axis_index("fsdp")
        self.spot = snake(lax.axis_index("ring"))
        self.own = lax.axis_index("ring")
        self.right = self.device(snake((self.spot + 1) % chips), self.core, self.layer)
        self.left = self.device(snake((self.spot + chips - 1) % chips), self.core, self.layer)
        self.up = self.device(self.own, self.core, (self.layer + 1) % depth)
        self.down = self.device(self.own, self.core, (self.layer + depth - 1) % depth)
        self.sibling = self.device(self.own, 1 - self.core, self.layer)

    def device(self, ring, core, layer):
        return (ring, core, layer)

    def shard(self, spot, core, layer):
        return (snake(spot) * 2 + core) * self.depth + layer

    def greet(self):
        barrier = pltpu.get_barrier_semaphore()
        for device in (self.right, self.left, self.up, self.down, self.sibling):
            pl.semaphore_signal(barrier, inc=1, device_id=device, device_id_type=MESH_ID)
        pl.semaphore_wait(barrier, 5)


def gather_kernel(chips, depth, count, *refs):
    shards = refs[:count]
    wholes = refs[count : 2 * count]
    sent, from_sibling, from_below, from_ring, kept = refs[2 * count :]
    here = Place(chips, depth)
    here.greet()
    cuts = [halves(ref.shape[1]) for ref in shards]

    def block(which, shard):
        return wholes[which].at[shard]

    def piece_of(which, shard, way):
        return wholes[which].at[shard, :, cuts[which][way]]

    def send(source, target, which, arrived, device):
        pltpu.make_async_remote_copy(
            src_ref=source,
            dst_ref=target,
            send_sem=sent.at[which],
            recv_sem=arrived,
            device_id=device,
            device_id_type=MESH_ID,
        ).start()

    def awaited(ref, arrived):
        pltpu.make_async_copy(ref, ref, arrived).wait()

    own = here.shard(here.spot, here.core, here.layer)
    for which in range(count):
        send(shards[which], block(which, own), which, from_below.at[which, 0], here.up)
        for way in range(2):
            send(
                shards[which].at[:, cuts[which][way]],
                piece_of(which, own, way),
                which,
                from_ring.at[which, way, 0],
                (here.right, here.left)[way],
            )
        send(shards[which], block(which, own), which, from_sibling.at[which], here.sibling)
        pltpu.make_async_copy(shards[which], block(which, own), kept.at[which]).start()

    def around(hop, layer_step):
        layer = (here.layer + depth - layer_step) % depth
        for which in range(count):
            for way in range(2):
                away = (chips - hop, hop)[way]
                shard = here.shard((here.spot + away) % chips, here.core, layer)
                arrived = layer_step * (chips - 1) + hop - 1
                piece = piece_of(which, shard, way)
                awaited(piece, from_ring.at[which, way, arrived])
                if hop < chips - 1:
                    send(
                        piece,
                        piece,
                        which,
                        from_ring.at[which, way, arrived + 1],
                        (here.right, here.left)[way],
                    )
                send(piece, piece, which, from_sibling.at[which], here.sibling)

    def layer_arrives(layer_step):
        layer = (here.layer + depth - layer_step) % depth
        shard = here.shard(here.spot, here.core, layer)
        for which in range(count):
            whole = block(which, shard)
            awaited(whole, from_below.at[which, layer_step - 1])

            @pl.when(layer_step < depth - 1)
            def _():
                send(whole, whole, which, from_below.at[which, layer_step], here.up)

            for way in range(2):
                piece = piece_of(which, shard, way)
                send(
                    piece,
                    piece,
                    which,
                    from_ring.at[which, way, layer_step * (chips - 1)],
                    (here.right, here.left)[way],
                )
            send(whole, whole, which, from_sibling.at[which], here.sibling)

    @pl.loop(0, depth)
    def _(layer_step):
        for hop in range(1, chips - 1):
            around(hop, layer_step)

        @pl.when(layer_step < depth - 1)
        def _():
            layer_arrives(layer_step + 1)

        around(chips - 1, layer_step)

    shard_count = 2 * chips * depth
    for which in range(count):
        pltpu.make_async_copy(shards[which], block(which, own), kept.at[which]).wait()
        awaited(wholes[which].at[pl.ds(0, shard_count // 2)], from_sibling.at[which])
        awaited(wholes[which].at[pl.ds(0, shard_count - 1)], sent.at[which])


def gather(chips, depth, *shards):
    count = len(shards)
    steps = depth * (chips - 1)
    anywhere = pl.BlockSpec(memory_space=pl.ANY)
    shard_count = 2 * chips * depth
    wholes = pl.pallas_call(
        functools.partial(gather_kernel, chips, depth, count),
        out_shape=[jax.ShapeDtypeStruct((shard_count,) + x.shape, x.dtype) for x in shards],
        in_specs=[anywhere] * count,
        out_specs=[anywhere] * count,
        scratch_shapes=[
            pltpu.SemaphoreType.DMA((count,)),
            pltpu.SemaphoreType.DMA((count,)),
            pltpu.SemaphoreType.DMA((count, depth - 1)),
            pltpu.SemaphoreType.DMA((count, 2, steps)),
            pltpu.SemaphoreType.DMA((count,)),
        ],
        compiler_params=pltpu.CompilerParams(collective_id=0, has_side_effects=True),
        name="gather_weights",
    )(*shards)
    return [x.reshape(-1, x.shape[2]) for x in wholes]


def scatter_kernel(chips, depth, count, *refs):
    grads = refs[:count]
    owned = refs[count : 2 * count]
    rest = refs[2 * count :]
    theirs = rest[:count]
    staged = rest[count : 2 * count]
    ringed = rest[2 * count : 3 * count]
    layered = rest[3 * count : 4 * count]
    sent, loaded, from_sibling, from_below, from_ring = rest[4 * count :]
    here = Place(chips, depth)
    cuts = [halves(ref.shape[1]) for ref in owned]
    f32 = jnp.float32

    def place(hop, way):
        away = (chips - hop, hop)[way]
        return (here.spot + away) % chips

    def layer_of(layer_step):
        return (here.layer + 2 * depth - 1 - layer_step) % depth

    def slot_of(layer_step, hop):
        return layer_step * chips + hop - 1

    def load(which, slot, buffer, start):
        layer_step = slot // chips
        hop = slot % chips + 1
        for way, cut in enumerate(cuts[which]):
            shard = here.shard(place(hop, way), here.core, layer_of(layer_step))
            copy = pltpu.make_async_copy(
                grads[which].at[shard, :, cut],
                staged[which].at[buffer, :, cut],
                loaded.at[which, way, buffer],
            )
            copy.start() if start else copy.wait()

    def hand_over(which, slot):
        layer_step = slot // chips
        hop = slot % chips + 1
        for way, cut in enumerate(cuts[which]):
            shard = here.shard(place(hop, way), 1 - here.core, layer_of(layer_step))
            pltpu.make_async_remote_copy(
                src_ref=grads[which].at[shard, :, cut],
                dst_ref=theirs[which].at[slot, :, cut],
                send_sem=sent.at[which],
                recv_sem=from_sibling.at[which, way, slot],
                device_id=here.sibling,
                device_id_type=MESH_ID,
            ).start()

    slots = chips * depth
    for which in range(count):
        load(which, jnp.int32(0), jnp.int32(0), True)
    here.greet()

    @pl.loop(0, slots)
    def _(slot):
        for which in range(count):
            hand_over(which, slot)

    def got(ref, semaphore):
        pltpu.make_async_copy(ref, ref, semaphore).wait()

    def step(layer_step, hop):
        slot = slot_of(layer_step, hop)
        buffer = slot % 2

        @pl.when(slot + 1 < slots)
        def _():
            for which in range(count):
                load(which, slot + 1, (slot + 1) % 2, True)

        for which in range(count):
            load(which, slot, buffer, False)
            if hop == chips:
                @pl.when(layer_step > 0)
                def _():
                    ref = layered[which].at[layer_step - 1]
                    got(ref, from_below.at[which, layer_step - 1])

            for way, cut in enumerate(cuts[which]):
                mine = theirs[which].at[slot, :, cut]
                got(mine, from_sibling.at[which, way, slot])
                total = mine[...].astype(f32) + staged[which][buffer, :, cut].astype(f32)
                if hop > 1:
                    index = layer_step * (chips - 1) + hop - 2
                    arrived = ringed[which].at[index, :, cut]
                    got(arrived, from_ring.at[which, way, index])
                    total = total + arrived[...].astype(f32)
                if hop < chips:
                    index = layer_step * (chips - 1) + hop - 1
                    mine[...] = total.astype(mine.dtype)
                    pltpu.make_async_remote_copy(
                        src_ref=mine,
                        dst_ref=ringed[which].at[index, :, cut],
                        send_sem=sent.at[which],
                        recv_sem=from_ring.at[which, way, index],
                        device_id=(here.right, here.left)[way],
                        device_id_type=MESH_ID,
                    ).start()
                else:
                    owned[which][:, cut] = total

            if hop == chips:
                @pl.when(layer_step > 0)
                def _():
                    owned[which][...] += layered[which][layer_step - 1].astype(f32)

                @pl.when(layer_step < depth - 1)
                def _():
                    mine = theirs[which].at[slot]
                    mine[...] = owned[which][...].astype(mine.dtype)
                    pltpu.make_async_remote_copy(
                        src_ref=mine,
                        dst_ref=layered[which].at[layer_step],
                        send_sem=sent.at[which],
                        recv_sem=from_below.at[which, layer_step],
                        device_id=here.up,
                        device_id_type=MESH_ID,
                    ).start()

    @pl.loop(0, depth)
    def _(layer_step):
        for hop in range(1, chips + 1):
            step(layer_step, hop)

    for which in range(count):
        most = grads[which].at[pl.ds(0, 2 * slots - 1)]
        pltpu.make_async_copy(most, most, sent.at[which]).wait()


def scatter(chips, depth, *grads):
    count = len(grads)
    slots = chips * depth
    steps = depth * (chips - 1)
    grads = [g.reshape(2 * slots, -1, g.shape[1]) for g in grads]
    anywhere = pl.BlockSpec(memory_space=pl.ANY)
    inner = pl.BlockSpec(memory_space=pltpu.VMEM)

    def room(leading):
        return [pltpu.VMEM((leading,) + g.shape[1:], g.dtype) for g in grads]

    return pl.pallas_call(
        functools.partial(scatter_kernel, chips, depth, count),
        out_shape=[jax.ShapeDtypeStruct(g.shape[1:], jnp.float32) for g in grads],
        in_specs=[anywhere] * count,
        out_specs=[inner] * count,
        scratch_shapes=room(slots)
        + room(2)
        + room(steps)
        + room(depth - 1)
        + [
            pltpu.SemaphoreType.DMA((count,)),
            pltpu.SemaphoreType.DMA((count, 2, 2)),
            pltpu.SemaphoreType.DMA((count, 2, slots)),
            pltpu.SemaphoreType.DMA((count, depth - 1)),
            pltpu.SemaphoreType.DMA((count, 2, steps)),
        ],
        compiler_params=pltpu.CompilerParams(
            collective_id=1, has_side_effects=True, vmem_limit_bytes=56 << 20
        ),
        name="scatter_gradients",
    )(*grads)


def from_behind(value, axis, steps):
    count = lax.axis_size(axis)
    first, last = (max(0, -steps), min(count, count - steps))
    return lax.ppermute(value, axis, [(source, source + steps) for source in range(first, last)])


def matmul(left, right):
    return jnp.dot(left, right, preferred_element_type=jnp.float32)


def matmul_tn(left, right):
    return lax.dot_general(
        left, right, (((0,), (0,)), ((), ())), preferred_element_type=jnp.float32
    )


def matmul_nt(left, right):
    return lax.dot_general(
        left, right, (((1,), (1,)), ((), ())), preferred_element_type=jnp.float32
    )


def inverse_rms(values):
    return lax.rsqrt(jnp.mean(values * values, axis=-1, keepdims=True) + NORM_EPS)


def norm_backward(values, scale, gain, grad_normed):
    weighted = grad_normed * gain
    grad_gain = jnp.sum(grad_normed * values * scale, axis=0)
    cubed = scale * scale * scale
    grad_values = scale * weighted - values * cubed * jnp.mean(
        weighted * values, axis=-1, keepdims=True
    )
    return (grad_values, grad_gain)


def adamw_update(param, grad, first, second, rate, decay):
    first_new = BETA_ONE * first + (1.0 - BETA_ONE) * grad
    second_new = BETA_TWO * second + (1.0 - BETA_TWO) * grad * grad
    first_hat = first_new / (1.0 - BETA_ONE**STEP)
    second_hat = second_new / (1.0 - BETA_TWO**STEP)
    param_new = param - rate * (first_hat / (jnp.sqrt(second_hat) + ADAM_EPS) + decay * param)
    return (param_new, first_new, second_new)


def local(
    hidden_in,
    cotangent,
    doc_position,
    norm_gains,
    conv_taps,
    in_proj,
    out_proj,
    gate_up,
    down_proj,
    first_gains,
    first_taps,
    first_in,
    first_out,
    first_gate_up,
    first_down,
    second_gains,
    second_taps,
    second_in,
    second_out,
    second_gate_up,
    second_down,
):
    half = jnp.bfloat16
    single = jnp.float32
    row_count, length, width = hidden_in.shape
    tok_count = row_count * length
    chips, depth = lax.axis_size("ring"), lax.axis_size("fsdp")
    in_width = in_proj.shape[1]
    out_width = out_proj.shape[1]
    vectors = jnp.concatenate([norm_gains, conv_taps], axis=0).T.astype(half)
    packed = jnp.concatenate(
        [
            in_proj.astype(half),
            out_proj.astype(half),
            jnp.pad(vectors, ((0, 0), (0, LANES - vectors.shape[1]))),
            gate_up.astype(half),
        ],
        axis=1,
    )
    packed_full, down_full = gather(chips, depth, packed, down_proj.astype(half))
    in_full = packed_full[:, :in_width]
    out_full = packed_full[:, in_width : in_width + out_width]
    vector_start = in_width + out_width
    vectors_full = packed_full[:, vector_start : vector_start + LANES].astype(single).T
    mixer_full = (None, None, in_full, out_full)
    gains_f = vectors_full[:2]
    taps_f = vectors_full[2:5]
    resid_one = hidden_in.reshape(tok_count, width).astype(single)
    scale_one = inverse_rms(resid_one)
    normed_one = (resid_one * scale_one * gains_f[0]).astype(half)
    projected = matmul(normed_one, mixer_full[2])
    b_branch = projected[:, :width]
    c_branch = projected[:, width : 2 * width]
    x_branch = projected[:, 2 * width :]
    gated_input = (b_branch * x_branch).astype(half)
    gated_rows = gated_input.reshape(row_count, length, width)
    carried = from_behind(gated_rows[:, length - 2 :, :], SEQ, 1)
    extended = jnp.concatenate([carried, gated_rows], axis=1).astype(single)
    gated_f = extended[:, 2:].reshape(tok_count, width)
    prev_one = extended[:, 1 : length + 1].reshape(tok_count, width)
    prev_two = extended[:, :length].reshape(tok_count, width)
    positions = doc_position.reshape(tok_count)
    mask_one = (positions >= 1).astype(single)[:, None]
    mask_two = (positions >= 2).astype(single)[:, None]
    conv_out = (
        taps_f[0] * gated_f + mask_one * taps_f[1] * prev_one + mask_two * taps_f[2] * prev_two
    )
    mixer_act = (c_branch * conv_out).astype(half)
    resid_two = resid_one + matmul(mixer_act, mixer_full[3])
    scale_two = inverse_rms(resid_two)
    normed_two = (resid_two * scale_two * gains_f[1]).astype(half)
    ffn_full = (packed_full[:, vector_start + LANES :], down_full)
    hidden_units = ffn_full[0].shape[1] // 2
    ffn_pre = matmul(normed_two, ffn_full[0])
    gate_pre = ffn_pre[:, :hidden_units]
    up_pre = ffn_pre[:, hidden_units:]
    sigmoid_gate = jax.nn.sigmoid(gate_pre)
    silu_gate = gate_pre * sigmoid_gate
    ffn_act = (silu_gate * up_pre).astype(half)
    block_out = resid_two + matmul(ffn_act, ffn_full[1])
    cot_rows = cotangent.reshape(tok_count, width)
    grad_act = matmul_nt(cot_rows, ffn_full[1])
    grad_gate = grad_act * up_pre * sigmoid_gate * (1.0 + gate_pre * (1.0 - sigmoid_gate))
    grad_both = jnp.concatenate([grad_gate, grad_act * silu_gate], axis=1).astype(half)
    grad_normed = matmul_nt(grad_both, ffn_full[0])
    grad_down = matmul_tn(ffn_act, cot_rows)
    grad_gate_up = matmul_tn(normed_two, grad_both)
    norm_part, gain_two_grad = norm_backward(resid_two, scale_two, gains_f[1], grad_normed)
    grad_resid = cot_rows.astype(single) + norm_part
    resid_cast = grad_resid.astype(half)
    grad_mixer = matmul_nt(resid_cast, mixer_full[3])
    grad_cbranch = grad_mixer * conv_out
    grad_conv = grad_mixer * c_branch
    masked_one = mask_one * grad_conv
    masked_two = mask_two * grad_conv
    grad_taps = jnp.stack(
        [
            jnp.sum(grad_conv * gated_f, axis=0),
            jnp.sum(masked_one * prev_one, axis=0),
            jnp.sum(masked_two * prev_two, axis=0),
        ]
    )
    one_rows = masked_one.reshape(row_count, length, width)
    two_rows = masked_two.reshape(row_count, length, width)
    leading = from_behind((one_rows[:, :2, :], two_rows[:, :2, :]), SEQ, -1)
    ext_one = jnp.concatenate([one_rows, leading[0]], axis=1)
    ext_two = jnp.concatenate([two_rows, leading[1]], axis=1)
    next_one = ext_one[:, 1 : length + 1].reshape(tok_count, width)
    next_two = ext_two[:, 2 : length + 2].reshape(tok_count, width)
    grad_gated = taps_f[0] * grad_conv + taps_f[1] * next_one + taps_f[2] * next_two
    grad_proj = jnp.concatenate(
        [grad_gated * x_branch, grad_cbranch, grad_gated * b_branch], axis=1
    ).astype(half)
    grad_normone = matmul_nt(grad_proj, mixer_full[2])
    first_part, gain_one_grad = norm_backward(resid_one, scale_one, gains_f[0], grad_normone)
    grad_hidden = grad_resid + first_part
    grad_gains = jnp.stack([gain_one_grad, gain_two_grad])
    grad_in = matmul_tn(normed_one, grad_proj)
    grad_out = matmul_tn(mixer_act, resid_cast)
    vector_grads = jnp.concatenate([grad_gains, grad_taps], axis=0)
    vector_count = vector_grads.shape[0]
    grad_sent = jnp.concatenate(
        [
            grad_in.astype(half),
            grad_out.astype(half),
            jnp.pad(vector_grads.T, ((0, 0), (0, LANES - vector_count))).astype(half),
            grad_gate_up.astype(half),
        ],
        axis=1,
    )
    grad_owned, down_owned = scatter(chips, depth, grad_sent, grad_down.astype(half))
    vector_owned = grad_owned[:, vector_start : vector_start + vector_count].T
    owned = (
        vector_owned[:2],
        vector_owned[2:],
        grad_owned[:, :in_width],
        grad_owned[:, in_width:vector_start],
        grad_owned[:, vector_start + LANES :],
        down_owned,
    )
    params = (norm_gains, conv_taps, in_proj, out_proj, gate_up, down_proj)
    firsts = (first_gains, first_taps, first_in, first_out, first_gate_up, first_down)
    seconds = (second_gains, second_taps, second_in, second_out, second_gate_up, second_down)
    rates = (RATE_VECTOR, RATE_VECTOR, RATE_MATRIX, RATE_MATRIX, RATE_MATRIX, RATE_MATRIX)
    decays = (0.0, 0.0, DECAY, DECAY, DECAY, DECAY)
    updated = [
        adamw_update(
            params[index], owned[index], firsts[index], seconds[index], rates[index], decays[index]
        )
        for index in range(6)
    ]
    out_rows = block_out.reshape(row_count, length, width)
    grad_rows = grad_hidden.reshape(row_count, length, width)
    return (
        out_rows,
        grad_rows,
        owned[0],
        owned[1],
        owned[2],
        owned[3],
        owned[4],
        owned[5],
        updated[0][0],
        updated[1][0],
        updated[2][0],
        updated[3][0],
        updated[4][0],
        updated[5][0],
        updated[0][1],
        updated[1][1],
        updated[2][1],
        updated[3][1],
        updated[4][1],
        updated[5][1],
        updated[0][2],
        updated[1][2],
        updated[2][2],
        updated[3][2],
        updated[4][2],
        updated[5][2],
    )


def solution(mesh):
    tokens, depth = mesh.devices.shape
    chip_mesh = Mesh(mesh.devices.reshape(tokens // 2, 2, depth), ALL)
    in_specs = (
        P("fsdp", SEQ, None),
        P("fsdp", SEQ, None),
        P("fsdp", SEQ),
        P(None, ALL),
        P(None, ALL),
        P(ALL, None),
        P(ALL, None),
        P(ALL, None),
        P(ALL, None),
        P(None, ALL),
        P(None, ALL),
        P(ALL, None),
        P(ALL, None),
        P(ALL, None),
        P(ALL, None),
        P(None, ALL),
        P(None, ALL),
        P(ALL, None),
        P(ALL, None),
        P(ALL, None),
        P(ALL, None),
    )
    out_specs = (
        P("fsdp", SEQ, None),
        P("fsdp", SEQ, None),
        P(None, ALL),
        P(None, ALL),
        P(ALL, None),
        P(ALL, None),
        P(ALL, None),
        P(ALL, None),
        P(None, ALL),
        P(None, ALL),
        P(ALL, None),
        P(ALL, None),
        P(ALL, None),
        P(ALL, None),
        P(None, ALL),
        P(None, ALL),
        P(ALL, None),
        P(ALL, None),
        P(ALL, None),
        P(ALL, None),
        P(None, ALL),
        P(None, ALL),
        P(ALL, None),
        P(ALL, None),
        P(ALL, None),
        P(ALL, None),
    )
    return jax.shard_map(local, mesh=chip_mesh, in_specs=in_specs, out_specs=out_specs, check_vma=False)
```

```python
import functools

import jax
import jax.numpy as jnp
from jax import lax
from jax.experimental import pallas as pl
from jax.experimental.pallas import tpu as pltpu
from jax.sharding import Mesh
from jax.sharding import PartitionSpec as P

STEP = 3


NORM_EPS = 1e-05
BETA_ONE = 0.9
BETA_TWO = 0.999
ADAM_EPS = 1e-08
RATE_MATRIX = 0.005
RATE_VECTOR = 0.2
DECAY = 0.1
LANES = 128
MESH_ID = pl.DeviceIdType.MESH
SEQ = ("ring", "core")
ALL = ("ring", "core", "fsdp")


def snake(index):
    return 2 * (index // 2) + (index % 2 + index // 2) % 2


def halves(columns):
    first = (columns // 2 + LANES - 1) // LANES * LANES
    return (pl.ds(0, first), pl.ds(first, columns - first))


class Place:
    def __init__(self, chips, depth):
        self.chips, self.depth = chips, depth
        self.core = lax.axis_index("core")
        self.layer = lax.axis_index("fsdp")
        self.spot = snake(lax.axis_index("ring"))
        self.own = lax.axis_index("ring")
        self.right = self.device(snake((self.spot + 1) % chips), self.core, self.layer)
        self.left = self.device(snake((self.spot + chips - 1) % chips), self.core, self.layer)
        self.up = self.device(self.own, self.core, (self.layer + 1) % depth)
        self.down = self.device(self.own, self.core, (self.layer + depth - 1) % depth)
        self.sibling = self.device(self.own, 1 - self.core, self.layer)

    def device(self, ring, core, layer):
        return (ring, core, layer)

    def shard(self, spot, core, layer):
        return (snake(spot) * 2 + core) * self.depth + layer

    def greet(self):
        barrier = pltpu.get_barrier_semaphore()
        for device in (self.right, self.left, self.up, self.down, self.sibling):
            pl.semaphore_signal(barrier, inc=1, device_id=device, device_id_type=MESH_ID)
        pl.semaphore_wait(barrier, 5)


def gather_kernel(chips, depth, count, *refs):
    shards = refs[:count]
    wholes = refs[count : 2 * count]
    sent, from_sibling, from_below, from_ring, kept = refs[2 * count :]
    here = Place(chips, depth)
    here.greet()
    cuts = [halves(ref.shape[1]) for ref in shards]

    def block(which, shard):
        return wholes[which].at[shard]

    def piece_of(which, shard, way):
        return wholes[which].at[shard, :, cuts[which][way]]

    def send(source, target, which, arrived, device):
        pltpu.make_async_remote_copy(
            src_ref=source,
            dst_ref=target,
            send_sem=sent.at[which],
            recv_sem=arrived,
            device_id=device,
            device_id_type=MESH_ID,
        ).start()

    def awaited(ref, arrived):
        pltpu.make_async_copy(ref, ref, arrived).wait()

    own = here.shard(here.spot, here.core, here.layer)
    for which in range(count):
        send(shards[which], block(which, own), which, from_below.at[which, 0], here.up)
        for way in range(2):
            send(
                shards[which].at[:, cuts[which][way]],
                piece_of(which, own, way),
                which,
                from_ring.at[which, way, 0],
                (here.right, here.left)[way],
            )
        send(shards[which], block(which, own), which, from_sibling.at[which], here.sibling)
        pltpu.make_async_copy(shards[which], block(which, own), kept.at[which]).start()

    def around(hop, layer_step):
        layer = (here.layer + depth - layer_step) % depth
        for which in range(count):
            for way in range(2):
                away = (chips - hop, hop)[way]
                shard = here.shard((here.spot + away) % chips, here.core, layer)
                arrived = layer_step * (chips - 1) + hop - 1
                piece = piece_of(which, shard, way)
                awaited(piece, from_ring.at[which, way, arrived])
                if hop < chips - 1:
                    send(
                        piece,
                        piece,
                        which,
                        from_ring.at[which, way, arrived + 1],
                        (here.right, here.left)[way],
                    )
                send(piece, piece, which, from_sibling.at[which], here.sibling)

    def layer_arrives(layer_step):
        layer = (here.layer + depth - layer_step) % depth
        shard = here.shard(here.spot, here.core, layer)
        for which in range(count):
            whole = block(which, shard)
            awaited(whole, from_below.at[which, layer_step - 1])

            @pl.when(layer_step < depth - 1)
            def _():
                send(whole, whole, which, from_below.at[which, layer_step], here.up)

            for way in range(2):
                piece = piece_of(which, shard, way)
                send(
                    piece,
                    piece,
                    which,
                    from_ring.at[which, way, layer_step * (chips - 1)],
                    (here.right, here.left)[way],
                )
            send(whole, whole, which, from_sibling.at[which], here.sibling)

    @pl.loop(0, depth)
    def _(layer_step):
        for hop in range(1, chips - 1):
            around(hop, layer_step)

        @pl.when(layer_step < depth - 1)
        def _():
            layer_arrives(layer_step + 1)

        around(chips - 1, layer_step)

    shard_count = 2 * chips * depth
    for which in range(count):
        pltpu.make_async_copy(shards[which], block(which, own), kept.at[which]).wait()
        awaited(wholes[which].at[pl.ds(0, shard_count // 2)], from_sibling.at[which])
        awaited(wholes[which].at[pl.ds(0, shard_count - 1)], sent.at[which])


def gather(chips, depth, *shards):
    count = len(shards)
    steps = depth * (chips - 1)
    anywhere = pl.BlockSpec(memory_space=pl.ANY)
    shard_count = 2 * chips * depth
    wholes = pl.pallas_call(
        functools.partial(gather_kernel, chips, depth, count),
        out_shape=[jax.ShapeDtypeStruct((shard_count,) + x.shape, x.dtype) for x in shards],
        in_specs=[anywhere] * count,
        out_specs=[anywhere] * count,
        scratch_shapes=[
            pltpu.SemaphoreType.DMA((count,)),
            pltpu.SemaphoreType.DMA((count,)),
            pltpu.SemaphoreType.DMA((count, depth - 1)),
            pltpu.SemaphoreType.DMA((count, 2, steps)),
            pltpu.SemaphoreType.DMA((count,)),
        ],
        compiler_params=pltpu.CompilerParams(collective_id=0, has_side_effects=True),
        name="gather_weights",
    )(*shards)
    return [x.reshape(-1, x.shape[2]) for x in wholes]


def scatter_kernel(chips, depth, count, *refs):
    grads = refs[:count]
    owned = refs[count : 2 * count]
    rest = refs[2 * count :]
    theirs = rest[:count]
    staged = rest[count : 2 * count]
    ringed = rest[2 * count : 3 * count]
    layered = rest[3 * count : 4 * count]
    sent, loaded, from_sibling, from_below, from_ring = rest[4 * count :]
    here = Place(chips, depth)
    cuts = [halves(ref.shape[1]) for ref in owned]
    f32 = jnp.float32

    def place(hop, way):
        away = (chips - hop, hop)[way]
        return (here.spot + away) % chips

    def layer_of(layer_step):
        return (here.layer + 2 * depth - 1 - layer_step) % depth

    def slot_of(layer_step, hop):
        return layer_step * chips + hop - 1

    def load(which, layer_step, hop, start):
        for way, cut in enumerate(cuts[which]):
            shard = here.shard(place(hop, way), here.core, layer_of(layer_step))
            copy = pltpu.make_async_copy(
                grads[which].at[shard, :, cut],
                staged[which].at[hop - 1, :, cut],
                loaded.at[which, way, hop - 1],
            )
            copy.start() if start else copy.wait()

    def hand_over(which, slot):
        layer_step = slot // chips
        hop = slot % chips + 1
        for way, cut in enumerate(cuts[which]):
            shard = here.shard(place(hop, way), 1 - here.core, layer_of(layer_step))
            pltpu.make_async_remote_copy(
                src_ref=grads[which].at[shard, :, cut],
                dst_ref=theirs[which].at[slot, :, cut],
                send_sem=sent.at[which],
                recv_sem=from_sibling.at[which, way, slot],
                device_id=here.sibling,
                device_id_type=MESH_ID,
            ).start()

    slots = chips * depth
    for hop in range(1, chips + 1):
        for which in range(count):
            load(which, 0, hop, True)
    here.greet()

    @pl.loop(0, slots)
    def _(slot):
        for which in range(count):
            hand_over(which, slot)

    def got(ref, semaphore):
        pltpu.make_async_copy(ref, ref, semaphore).wait()

    def step(layer_step, hop):
        slot = slot_of(layer_step, hop)
        for which in range(count):
            load(which, layer_step, hop, False)
            if hop == chips:
                @pl.when(layer_step > 0)
                def _():
                    ref = layered[which].at[layer_step - 1]
                    got(ref, from_below.at[which, layer_step - 1])

            for way, cut in enumerate(cuts[which]):
                mine = theirs[which].at[slot, :, cut]
                got(mine, from_sibling.at[which, way, slot])
                total = mine[...].astype(f32) + staged[which][hop - 1, :, cut].astype(f32)
                if hop > 1:
                    index = layer_step * (chips - 1) + hop - 2
                    arrived = ringed[which].at[index, :, cut]
                    got(arrived, from_ring.at[which, way, index])
                    total = total + arrived[...].astype(f32)
                if hop < chips:
                    index = layer_step * (chips - 1) + hop - 1
                    mine[...] = total.astype(mine.dtype)
                    pltpu.make_async_remote_copy(
                        src_ref=mine,
                        dst_ref=ringed[which].at[index, :, cut],
                        send_sem=sent.at[which],
                        recv_sem=from_ring.at[which, way, index],
                        device_id=(here.right, here.left)[way],
                        device_id_type=MESH_ID,
                    ).start()
                else:
                    owned[which][:, cut] = total

            if hop == chips:
                @pl.when(layer_step > 0)
                def _():
                    owned[which][...] += layered[which][layer_step - 1].astype(f32)

                @pl.when(layer_step < depth - 1)
                def _():
                    mine = theirs[which].at[slot]
                    mine[...] = owned[which][...].astype(mine.dtype)
                    pltpu.make_async_remote_copy(
                        src_ref=mine,
                        dst_ref=layered[which].at[layer_step],
                        send_sem=sent.at[which],
                        recv_sem=from_below.at[which, layer_step],
                        device_id=here.up,
                        device_id_type=MESH_ID,
                    ).start()

        @pl.when(layer_step < depth - 1)
        def _():
            for which in range(count):
                load(which, layer_step + 1, hop, True)

    step(0, 1)

    @pl.loop(0, depth)
    def _(layer_step):
        for hop in range(2, chips):
            step(layer_step, hop)

        @pl.when(layer_step < depth - 1)
        def _():
            step(layer_step + 1, 1)

        step(layer_step, chips)

    for which in range(count):
        most = grads[which].at[pl.ds(0, 2 * slots - 1)]
        pltpu.make_async_copy(most, most, sent.at[which]).wait()


def scatter(chips, depth, *grads):
    count = len(grads)
    slots = chips * depth
    steps = depth * (chips - 1)
    grads = [g.reshape(2 * slots, -1, g.shape[1]) for g in grads]
    anywhere = pl.BlockSpec(memory_space=pl.ANY)
    inner = pl.BlockSpec(memory_space=pltpu.VMEM)

    def room(leading):
        return [pltpu.VMEM((leading,) + g.shape[1:], g.dtype) for g in grads]

    return pl.pallas_call(
        functools.partial(scatter_kernel, chips, depth, count),
        out_shape=[jax.ShapeDtypeStruct(g.shape[1:], jnp.float32) for g in grads],
        in_specs=[anywhere] * count,
        out_specs=[inner] * count,
        scratch_shapes=room(slots)
        + room(chips)
        + room(steps)
        + room(depth - 1)
        + [
            pltpu.SemaphoreType.DMA((count,)),
            pltpu.SemaphoreType.DMA((count, 2, chips)),
            pltpu.SemaphoreType.DMA((count, 2, slots)),
            pltpu.SemaphoreType.DMA((count, depth - 1)),
            pltpu.SemaphoreType.DMA((count, 2, steps)),
        ],
        compiler_params=pltpu.CompilerParams(
            collective_id=1, has_side_effects=True, vmem_limit_bytes=56 << 20
        ),
        name="scatter_gradients",
    )(*grads)


def from_behind(value, axis, steps):
    count = lax.axis_size(axis)
    first, last = (max(0, -steps), min(count, count - steps))
    return lax.ppermute(value, axis, [(source, source + steps) for source in range(first, last)])


def matmul(left, right):
    return jnp.dot(left, right, preferred_element_type=jnp.float32)


def matmul_tn(left, right):
    return lax.dot_general(
        left, right, (((0,), (0,)), ((), ())), preferred_element_type=jnp.float32
    )


def matmul_nt(left, right):
    return lax.dot_general(
        left, right, (((1,), (1,)), ((), ())), preferred_element_type=jnp.float32
    )


def inverse_rms(values):
    return lax.rsqrt(jnp.mean(values * values, axis=-1, keepdims=True) + NORM_EPS)


def norm_backward(values, scale, gain, grad_normed):
    weighted = grad_normed * gain
    grad_gain = jnp.sum(grad_normed * values * scale, axis=0)
    cubed = scale * scale * scale
    grad_values = scale * weighted - values * cubed * jnp.mean(
        weighted * values, axis=-1, keepdims=True
    )
    return (grad_values, grad_gain)


def adamw_update(param, grad, first, second, rate, decay):
    first_new = BETA_ONE * first + (1.0 - BETA_ONE) * grad
    second_new = BETA_TWO * second + (1.0 - BETA_TWO) * grad * grad
    first_hat = first_new / (1.0 - BETA_ONE**STEP)
    second_hat = second_new / (1.0 - BETA_TWO**STEP)
    param_new = param - rate * (first_hat / (jnp.sqrt(second_hat) + ADAM_EPS) + decay * param)
    return (param_new, first_new, second_new)


def adamw_kernel(*refs):
    grads, state, outs = refs[:5], refs[5:23], refs[23:]
    vectors = grads[0][...].T
    found = [vectors[:2], vectors[2:5]] + [ref[...] for ref in grads[1:]]
    for index, grad in enumerate(found):
        rate, decay = (RATE_VECTOR, 0.0) if index < 2 else (RATE_MATRIX, DECAY)
        param, first, second = (state[6 * kind + index][...] for kind in range(3))
        new = adamw_update(param, grad, first, second, rate, decay)
        for kind, value in enumerate((grad,) + new):
            outs[6 * kind + index][...] = value


def adamw(grads, params, firsts, seconds):
    inner = pl.BlockSpec(memory_space=pltpu.VMEM)
    return pl.pallas_call(
        adamw_kernel,
        out_shape=[jax.ShapeDtypeStruct(p.shape, p.dtype) for p in params] * 4,
        in_specs=[inner] * 23,
        out_specs=[inner] * 24,
        compiler_params=pltpu.CompilerParams(vmem_limit_bytes=48 << 20),
        name="adamw",
    )(*grads, *params, *firsts, *seconds)


def local(
    hidden_in,
    cotangent,
    doc_position,
    norm_gains,
    conv_taps,
    in_proj,
    out_proj,
    gate_up,
    down_proj,
    first_gains,
    first_taps,
    first_in,
    first_out,
    first_gate_up,
    first_down,
    second_gains,
    second_taps,
    second_in,
    second_out,
    second_gate_up,
    second_down,
):
    half = jnp.bfloat16
    single = jnp.float32
    row_count, length, width = hidden_in.shape
    tok_count = row_count * length
    chips, depth = lax.axis_size("ring"), lax.axis_size("fsdp")
    in_width = in_proj.shape[1]
    out_width = out_proj.shape[1]
    vectors = jnp.concatenate([norm_gains, conv_taps], axis=0).T.astype(half)
    packed = jnp.concatenate(
        [
            in_proj.astype(half),
            out_proj.astype(half),
            jnp.pad(vectors, ((0, 0), (0, LANES - vectors.shape[1]))),
            gate_up.astype(half),
        ],
        axis=1,
    )
    packed_full, down_full = gather(chips, depth, packed, down_proj.astype(half))
    in_full = packed_full[:, :in_width]
    out_full = packed_full[:, in_width : in_width + out_width]
    vector_start = in_width + out_width
    vectors_full = packed_full[:, vector_start : vector_start + LANES].astype(single).T
    mixer_full = (None, None, in_full, out_full)
    gains_f = vectors_full[:2]
    taps_f = vectors_full[2:5]
    resid_one = hidden_in.reshape(tok_count, width).astype(single)
    scale_one = inverse_rms(resid_one)
    normed_one = (resid_one * scale_one * gains_f[0]).astype(half)
    projected = matmul(normed_one, mixer_full[2])
    b_branch = projected[:, :width]
    c_branch = projected[:, width : 2 * width]
    x_branch = projected[:, 2 * width :]
    gated_input = (b_branch * x_branch).astype(half)
    gated_rows = gated_input.reshape(row_count, length, width)
    carried = from_behind(gated_rows[:, length - 2 :, :], SEQ, 1)
    extended = jnp.concatenate([carried, gated_rows], axis=1).astype(single)
    gated_f = extended[:, 2:].reshape(tok_count, width)
    prev_one = extended[:, 1 : length + 1].reshape(tok_count, width)
    prev_two = extended[:, :length].reshape(tok_count, width)
    positions = doc_position.reshape(tok_count)
    mask_one = (positions >= 1).astype(single)[:, None]
    mask_two = (positions >= 2).astype(single)[:, None]
    conv_out = (
        taps_f[0] * gated_f + mask_one * taps_f[1] * prev_one + mask_two * taps_f[2] * prev_two
    )
    mixer_act = (c_branch * conv_out).astype(half)
    resid_two = resid_one + matmul(mixer_act, mixer_full[3])
    scale_two = inverse_rms(resid_two)
    normed_two = (resid_two * scale_two * gains_f[1]).astype(half)
    ffn_full = (packed_full[:, vector_start + LANES :], down_full)
    hidden_units = ffn_full[0].shape[1] // 2
    ffn_pre = matmul(normed_two, ffn_full[0])
    gate_pre = ffn_pre[:, :hidden_units]
    up_pre = ffn_pre[:, hidden_units:]
    sigmoid_gate = jax.nn.sigmoid(gate_pre)
    silu_gate = gate_pre * sigmoid_gate
    ffn_act = (silu_gate * up_pre).astype(half)
    block_out = resid_two + matmul(ffn_act, ffn_full[1])
    cot_rows = cotangent.reshape(tok_count, width)
    grad_act = matmul_nt(cot_rows, ffn_full[1])
    grad_gate = grad_act * up_pre * sigmoid_gate * (1.0 + gate_pre * (1.0 - sigmoid_gate))
    grad_both = jnp.concatenate([grad_gate, grad_act * silu_gate], axis=1).astype(half)
    grad_normed = matmul_nt(grad_both, ffn_full[0])
    grad_down = matmul_tn(ffn_act, cot_rows)
    down_owned = lax.psum_scatter(
        grad_down.astype(half), ALL, scatter_dimension=0, tiled=True
    ).astype(single)
    grad_gate_up = matmul_tn(normed_two, grad_both)
    norm_part, gain_two_grad = norm_backward(resid_two, scale_two, gains_f[1], grad_normed)
    grad_resid = cot_rows.astype(single) + norm_part
    resid_cast = grad_resid.astype(half)
    grad_mixer = matmul_nt(resid_cast, mixer_full[3])
    grad_cbranch = grad_mixer * conv_out
    grad_conv = grad_mixer * c_branch
    masked_one = mask_one * grad_conv
    masked_two = mask_two * grad_conv
    grad_taps = jnp.stack(
        [
            jnp.sum(grad_conv * gated_f, axis=0),
            jnp.sum(masked_one * prev_one, axis=0),
            jnp.sum(masked_two * prev_two, axis=0),
        ]
    )
    one_rows = masked_one.reshape(row_count, length, width)
    two_rows = masked_two.reshape(row_count, length, width)
    leading = from_behind((one_rows[:, :2, :], two_rows[:, :2, :]), SEQ, -1)
    ext_one = jnp.concatenate([one_rows, leading[0]], axis=1)
    ext_two = jnp.concatenate([two_rows, leading[1]], axis=1)
    next_one = ext_one[:, 1 : length + 1].reshape(tok_count, width)
    next_two = ext_two[:, 2 : length + 2].reshape(tok_count, width)
    grad_gated = taps_f[0] * grad_conv + taps_f[1] * next_one + taps_f[2] * next_two
    grad_proj = jnp.concatenate(
        [grad_gated * x_branch, grad_cbranch, grad_gated * b_branch], axis=1
    ).astype(half)
    grad_normone = matmul_nt(grad_proj, mixer_full[2])
    first_part, gain_one_grad = norm_backward(resid_one, scale_one, gains_f[0], grad_normone)
    grad_hidden = grad_resid + first_part
    grad_gains = jnp.stack([gain_one_grad, gain_two_grad])
    grad_in = matmul_tn(normed_one, grad_proj)
    grad_out = matmul_tn(mixer_act, resid_cast)
    vector_grads = jnp.concatenate([grad_gains, grad_taps], axis=0)
    vector_count = vector_grads.shape[0]
    vector_columns = jnp.pad(vector_grads.T, ((0, 0), (0, LANES - vector_count))).astype(half)
    grad_side = jnp.concatenate([vector_columns, grad_out.astype(half)], axis=1)
    gate_owned, in_owned, side_owned = scatter(
        chips, depth, grad_gate_up.astype(half), grad_in.astype(half), grad_side
    )
    params = (norm_gains, conv_taps, in_proj, out_proj, gate_up, down_proj)
    firsts = (first_gains, first_taps, first_in, first_out, first_gate_up, first_down)
    seconds = (second_gains, second_taps, second_in, second_out, second_gate_up, second_down)
    owned = (side_owned[:, :LANES], in_owned, side_owned[:, LANES:], gate_owned, down_owned)
    results = adamw(owned, params, firsts, seconds)
    out_rows = block_out.reshape(row_count, length, width)
    grad_rows = grad_hidden.reshape(row_count, length, width)
    return (
        out_rows,
        grad_rows,
        *results,
    )


def solution(mesh):
    tokens, depth = mesh.devices.shape
    chip_mesh = Mesh(mesh.devices.reshape(tokens // 2, 2, depth), ALL)
    in_specs = (
        P("fsdp", SEQ, None),
        P("fsdp", SEQ, None),
        P("fsdp", SEQ),
        P(None, ALL),
        P(None, ALL),
        P(ALL, None),
        P(ALL, None),
        P(ALL, None),
        P(ALL, None),
        P(None, ALL),
        P(None, ALL),
        P(ALL, None),
        P(ALL, None),
        P(ALL, None),
        P(ALL, None),
        P(None, ALL),
        P(None, ALL),
        P(ALL, None),
        P(ALL, None),
        P(ALL, None),
        P(ALL, None),
    )
    out_specs = (
        P("fsdp", SEQ, None),
        P("fsdp", SEQ, None),
        P(None, ALL),
        P(None, ALL),
        P(ALL, None),
        P(ALL, None),
        P(ALL, None),
        P(ALL, None),
        P(None, ALL),
        P(None, ALL),
        P(ALL, None),
        P(ALL, None),
        P(ALL, None),
        P(ALL, None),
        P(None, ALL),
        P(None, ALL),
        P(ALL, None),
        P(ALL, None),
        P(ALL, None),
        P(ALL, None),
        P(None, ALL),
        P(None, ALL),
        P(ALL, None),
        P(ALL, None),
        P(ALL, None),
        P(ALL, None),
    )
    return jax.shard_map(local, mesh=chip_mesh, in_specs=in_specs, out_specs=out_specs, check_vma=False)
```

```python
import functools

import jax
import jax.numpy as jnp
from jax import lax
from jax.experimental import pallas as pl
from jax.experimental.pallas import tpu as pltpu
from jax.sharding import Mesh
from jax.sharding import PartitionSpec as P

STEP = 3


NORM_EPS = 1e-05
BETA_ONE = 0.9
BETA_TWO = 0.999
ADAM_EPS = 1e-08
RATE_MATRIX = 0.005
RATE_VECTOR = 0.2
DECAY = 0.1
LANES = 128
VMEM_SCATTER = 46 << 20
MESH_ID = pl.DeviceIdType.MESH
SEQ = ("ring", "core")
ALL = ("ring", "core", "fsdp")


def snake(index):
    return 2 * (index // 2) + (index % 2 + index // 2) % 2


def halves(columns):
    first = (columns // 2 + LANES - 1) // LANES * LANES
    return (pl.ds(0, first), pl.ds(first, columns - first))


class Place:
    def __init__(self, chips, depth):
        self.chips, self.depth = chips, depth
        self.core = lax.axis_index("core")
        self.layer = lax.axis_index("fsdp")
        self.spot = snake(lax.axis_index("ring"))
        self.own = lax.axis_index("ring")
        self.right = self.device(snake((self.spot + 1) % chips), self.core, self.layer)
        self.left = self.device(snake((self.spot + chips - 1) % chips), self.core, self.layer)
        self.up = self.device(self.own, self.core, (self.layer + 1) % depth)
        self.down = self.device(self.own, self.core, (self.layer + depth - 1) % depth)
        self.sibling = self.device(self.own, 1 - self.core, self.layer)

    def device(self, ring, core, layer):
        return (ring, core, layer)

    def shard(self, spot, core, layer):
        return (snake(spot) * 2 + core) * self.depth + layer

    def greet(self):
        barrier = pltpu.get_barrier_semaphore()
        for device in (self.right, self.left, self.up, self.down, self.sibling):
            pl.semaphore_signal(barrier, inc=1, device_id=device, device_id_type=MESH_ID)
        pl.semaphore_wait(barrier, 5)


def gather_kernel(chips, depth, count, *refs):
    shards = refs[:count]
    wholes = refs[count : 2 * count]
    sent, from_sibling, from_below, from_ring, kept, late_ring, late_below = refs[2 * count :]
    here = Place(chips, depth)
    here.greet()
    late = count - 1
    cuts = [halves(ref.shape[1]) for ref in shards]

    def block(which, shard):
        return wholes[which].at[shard]

    def piece_of(which, shard, way):
        return wholes[which].at[shard, :, cuts[which][way]]

    def send(source, target, which, arrived, device):
        pltpu.make_async_remote_copy(
            src_ref=source,
            dst_ref=target,
            send_sem=sent.at[which],
            recv_sem=arrived,
            device_id=device,
            device_id_type=MESH_ID,
        ).start()

    def awaited(ref, arrived):
        pltpu.make_async_copy(ref, ref, arrived).wait()

    own = here.shard(here.spot, here.core, here.layer)
    for which in range(late):
        send(shards[which], block(which, own), which, from_below.at[which, 0], here.up)
        for way in range(2):
            send(
                shards[which].at[:, cuts[which][way]],
                piece_of(which, own, way),
                which,
                from_ring.at[which, way, 0],
                (here.right, here.left)[way],
            )
    for way in range(2):
        part = shards[late].at[:, cuts[late][way]]
        piece = piece_of(late, own, way)
        send(part, piece, late, late_ring.at[way, 0], (here.right, here.left)[way])
        send(part, piece, late, late_below.at[way, 0], here.up)
    for which in range(count):
        send(shards[which], block(which, own), which, from_sibling.at[which], here.sibling)
        pltpu.make_async_copy(shards[which], block(which, own), kept.at[which]).start()

    def late_around(hop):
        for way in range(2):
            away = (chips - hop, hop)[way]
            piece = piece_of(late, here.shard((here.spot + away) % chips, here.core, here.layer), way)
            awaited(piece, late_ring.at[way, hop - 1])
            if hop < chips - 1:
                send(piece, piece, late, late_ring.at[way, hop], (here.right, here.left)[way])
            send(piece, piece, late, late_below.at[way, hop], here.up)
            send(piece, piece, late, from_sibling.at[late], here.sibling)

    def late_layer(layer_step, hop):
        layer = (here.layer + depth - layer_step) % depth
        for way in range(2):
            away = (chips - hop, hop)[way]
            piece = piece_of(late, here.shard((here.spot + away) % chips, here.core, layer), way)
            awaited(piece, late_below.at[way, (layer_step - 1) * chips + hop])

            @pl.when(layer_step < depth - 1)
            def _():
                send(piece, piece, late, late_below.at[way, layer_step * chips + hop], here.up)

            send(piece, piece, late, from_sibling.at[late], here.sibling)

    def late_step(layer_step, hop):
        if hop > 0:
            @pl.when(layer_step == 0)
            def _():
                late_around(hop)

        @pl.when(layer_step > 0)
        def _():
            late_layer(layer_step, hop)

    def around(hop, layer_step):
        layer = (here.layer + depth - layer_step) % depth
        for which in range(late):
            for way in range(2):
                away = (chips - hop, hop)[way]
                shard = here.shard((here.spot + away) % chips, here.core, layer)
                arrived = layer_step * (chips - 1) + hop - 1
                piece = piece_of(which, shard, way)
                awaited(piece, from_ring.at[which, way, arrived])
                if hop < chips - 1:
                    send(
                        piece,
                        piece,
                        which,
                        from_ring.at[which, way, arrived + 1],
                        (here.right, here.left)[way],
                    )
                send(piece, piece, which, from_sibling.at[which], here.sibling)

    def layer_arrives(layer_step):
        layer = (here.layer + depth - layer_step) % depth
        shard = here.shard(here.spot, here.core, layer)
        for which in range(late):
            whole = block(which, shard)
            awaited(whole, from_below.at[which, layer_step - 1])

            @pl.when(layer_step < depth - 1)
            def _():
                send(whole, whole, which, from_below.at[which, layer_step], here.up)

            for way in range(2):
                piece = piece_of(which, shard, way)
                send(
                    piece,
                    piece,
                    which,
                    from_ring.at[which, way, layer_step * (chips - 1)],
                    (here.right, here.left)[way],
                )
            send(whole, whole, which, from_sibling.at[which], here.sibling)

    @pl.loop(0, depth)
    def _(layer_step):
        late_step(layer_step, 0)
        for hop in range(1, chips - 1):
            around(hop, layer_step)
            late_step(layer_step, hop)

        @pl.when(layer_step < depth - 1)
        def _():
            layer_arrives(layer_step + 1)

        around(chips - 1, layer_step)
        late_step(layer_step, chips - 1)

    shard_count = 2 * chips * depth
    for which in range(count):
        pltpu.make_async_copy(shards[which], block(which, own), kept.at[which]).wait()
        awaited(wholes[which].at[pl.ds(0, shard_count // 2)], from_sibling.at[which])
        awaited(wholes[which].at[pl.ds(0, shard_count - 1)], sent.at[which])


def gather(chips, depth, *shards):
    count = len(shards)
    steps = depth * (chips - 1)
    anywhere = pl.BlockSpec(memory_space=pl.ANY)
    shard_count = 2 * chips * depth
    wholes = pl.pallas_call(
        functools.partial(gather_kernel, chips, depth, count),
        out_shape=[jax.ShapeDtypeStruct((shard_count,) + x.shape, x.dtype) for x in shards],
        in_specs=[anywhere] * count,
        out_specs=[anywhere] * count,
        scratch_shapes=[
            pltpu.SemaphoreType.DMA((count,)),
            pltpu.SemaphoreType.DMA((count,)),
            pltpu.SemaphoreType.DMA((count, depth - 1)),
            pltpu.SemaphoreType.DMA((count, 2, steps)),
            pltpu.SemaphoreType.DMA((count,)),
            pltpu.SemaphoreType.DMA((2, chips - 1)),
            pltpu.SemaphoreType.DMA((2, chips * (depth - 1))),
        ],
        compiler_params=pltpu.CompilerParams(collective_id=0, has_side_effects=True),
        name="gather_weights",
    )(*shards)
    return [x.reshape(-1, x.shape[2]) for x in wholes]


def scatter_kernel(chips, depth, count, *refs):
    grads = refs[:count]
    owned = refs[count : 2 * count]
    rest = refs[2 * count :]
    theirs = rest[:count]
    staged = rest[count : 2 * count]
    ringed = rest[2 * count : 3 * count]
    layered = rest[3 * count : 4 * count]
    sent, loaded, from_sibling, from_below, from_ring, late_below = rest[4 * count :]
    here = Place(chips, depth)
    late = count - 1
    cuts = [halves(ref.shape[1]) for ref in owned]
    f32 = jnp.float32

    def place(hop, way):
        away = (chips - hop, hop)[way]
        return (here.spot + away) % chips

    def layer_of(layer_step):
        return (here.layer + 2 * depth - 1 - layer_step) % depth

    def slot_of(layer_step, hop):
        return layer_step * chips + hop - 1

    def load(which, layer_step, hop, start):
        for way, cut in enumerate(cuts[which]):
            shard = here.shard(place(hop, way), here.core, layer_of(layer_step))
            copy = pltpu.make_async_copy(
                grads[which].at[shard, :, cut],
                staged[which].at[hop - 1, :, cut],
                loaded.at[which, way, hop - 1],
            )
            copy.start() if start else copy.wait()

    def hand_over(which, slot):
        layer_step = slot // chips
        hop = slot % chips + 1
        for way, cut in enumerate(cuts[which]):
            shard = here.shard(place(hop, way), 1 - here.core, layer_of(layer_step))
            pltpu.make_async_remote_copy(
                src_ref=grads[which].at[shard, :, cut],
                dst_ref=theirs[which].at[slot, :, cut],
                send_sem=sent.at[which],
                recv_sem=from_sibling.at[which, way, slot],
                device_id=here.sibling,
                device_id_type=MESH_ID,
            ).start()

    slots = chips * depth
    for hop in range(1, chips + 1):
        for which in range(count):
            load(which, 0, hop, True)
    here.greet()

    @pl.loop(0, slots)
    def _(slot):
        for which in range(count):
            hand_over(which, slot)

    def got(ref, semaphore):
        pltpu.make_async_copy(ref, ref, semaphore).wait()

    def step(layer_step, hop):
        slot = slot_of(layer_step, hop)
        for which in range(late):
            load(which, layer_step, hop, False)
            if hop == chips:
                @pl.when(layer_step > 0)
                def _():
                    ref = layered[which].at[layer_step - 1]
                    got(ref, from_below.at[which, layer_step - 1])

            for way, cut in enumerate(cuts[which]):
                mine = theirs[which].at[slot, :, cut]
                got(mine, from_sibling.at[which, way, slot])
                total = mine[...].astype(f32) + staged[which][hop - 1, :, cut].astype(f32)
                if hop > 1:
                    index = layer_step * (chips - 1) + hop - 2
                    arrived = ringed[which].at[index, :, cut]
                    got(arrived, from_ring.at[which, way, index])
                    total = total + arrived[...].astype(f32)
                if hop < chips:
                    index = layer_step * (chips - 1) + hop - 1
                    mine[...] = total.astype(mine.dtype)
                    pltpu.make_async_remote_copy(
                        src_ref=mine,
                        dst_ref=ringed[which].at[index, :, cut],
                        send_sem=sent.at[which],
                        recv_sem=from_ring.at[which, way, index],
                        device_id=(here.right, here.left)[way],
                        device_id_type=MESH_ID,
                    ).start()
                else:
                    owned[which][:, cut] = total

            if hop == chips:
                @pl.when(layer_step > 0)
                def _():
                    owned[which][...] += layered[which][layer_step - 1].astype(f32)

                @pl.when(layer_step < depth - 1)
                def _():
                    mine = theirs[which].at[slot]
                    mine[...] = owned[which][...].astype(mine.dtype)
                    pltpu.make_async_remote_copy(
                        src_ref=mine,
                        dst_ref=layered[which].at[layer_step],
                        send_sem=sent.at[which],
                        recv_sem=from_below.at[which, layer_step],
                        device_id=here.up,
                        device_id_type=MESH_ID,
                    ).start()

        @pl.when(layer_step < depth - 1)
        def _():
            for which in range(late):
                load(which, layer_step + 1, hop, True)

    def late_step(layer_step, hop):
        slot = slot_of(layer_step, hop)
        load(late, layer_step, hop, False)
        for way, cut in enumerate(cuts[late]):
            mine = theirs[late].at[slot, :, cut]
            got(mine, from_sibling.at[late, way, slot])
            total = mine[...].astype(f32) + staged[late][hop - 1, :, cut].astype(f32)
            mine[...] = total.astype(mine.dtype)

            @pl.when(layer_step > 0)
            def _():
                before = slot_of(layer_step - 1, hop)
                arrived = layered[late].at[before, :, cut]
                got(arrived, late_below.at[way, before])
                both = total + arrived[...].astype(f32)
                mine[...] = both.astype(mine.dtype)

            @pl.when(layer_step < depth - 1)
            def _():
                pltpu.make_async_remote_copy(
                    src_ref=mine,
                    dst_ref=layered[late].at[slot, :, cut],
                    send_sem=sent.at[late],
                    recv_sem=late_below.at[way, slot],
                    device_id=here.up,
                    device_id_type=MESH_ID,
                ).start()

            @pl.when(layer_step == depth - 1)
            def _():
                around = mine[...].astype(f32)
                if hop > 1:
                    arrived = ringed[late].at[hop - 2, :, cut]
                    got(arrived, from_ring.at[late, way, hop - 2])
                    around = around + arrived[...].astype(f32)
                if hop < chips:
                    mine[...] = around.astype(mine.dtype)
                    pltpu.make_async_remote_copy(
                        src_ref=mine,
                        dst_ref=ringed[late].at[hop - 1, :, cut],
                        send_sem=sent.at[late],
                        recv_sem=from_ring.at[late, way, hop - 1],
                        device_id=(here.right, here.left)[way],
                        device_id_type=MESH_ID,
                    ).start()
                else:
                    owned[late][:, cut] = around

        @pl.when(layer_step < depth - 1)
        def _():
            load(late, layer_step + 1, hop, True)

    step(0, 1)

    @pl.loop(0, depth)
    def _(layer_step):
        late_step(layer_step, 1)
        for hop in range(2, chips):
            step(layer_step, hop)
            late_step(layer_step, hop)

        @pl.when(layer_step < depth - 1)
        def _():
            step(layer_step + 1, 1)

        late_step(layer_step, chips)
        step(layer_step, chips)

    for which in range(count):
        most = grads[which].at[pl.ds(0, 2 * slots - 1)]
        pltpu.make_async_copy(most, most, sent.at[which]).wait()


def scatter(chips, depth, *grads):
    count = len(grads)
    slots = chips * depth
    steps = depth * (chips - 1)
    grads = [g.reshape(2 * slots, -1, g.shape[1]) for g in grads]
    anywhere = pl.BlockSpec(memory_space=pl.ANY)
    inner = pl.BlockSpec(memory_space=pltpu.VMEM)

    def room(most, last):
        leading = [most] * (count - 1) + [last]
        return [pltpu.VMEM((n,) + g.shape[1:], g.dtype) for n, g in zip(leading, grads)]

    return pl.pallas_call(
        functools.partial(scatter_kernel, chips, depth, count),
        out_shape=[jax.ShapeDtypeStruct(g.shape[1:], jnp.float32) for g in grads],
        in_specs=[anywhere] * count,
        out_specs=[inner] * count,
        scratch_shapes=room(slots, slots)
        + room(chips, chips)
        + room(steps, chips - 1)
        + room(depth - 1, chips * (depth - 1))
        + [
            pltpu.SemaphoreType.DMA((count,)),
            pltpu.SemaphoreType.DMA((count, 2, chips)),
            pltpu.SemaphoreType.DMA((count, 2, slots)),
            pltpu.SemaphoreType.DMA((count, depth - 1)),
            pltpu.SemaphoreType.DMA((count, 2, steps)),
            pltpu.SemaphoreType.DMA((2, chips * (depth - 1))),
        ],
        compiler_params=pltpu.CompilerParams(
            collective_id=1, has_side_effects=True, vmem_limit_bytes=VMEM_SCATTER
        ),
        name="scatter_gradients",
    )(*grads)


def from_behind(value, axis, steps):
    count = lax.axis_size(axis)
    first, last = (max(0, -steps), min(count, count - steps))
    return lax.ppermute(value, axis, [(source, source + steps) for source in range(first, last)])


def matmul(left, right):
    return jnp.dot(left, right, preferred_element_type=jnp.float32)


def matmul_tn(left, right):
    return lax.dot_general(
        left, right, (((0,), (0,)), ((), ())), preferred_element_type=jnp.float32
    )


def matmul_nt(left, right):
    return lax.dot_general(
        left, right, (((1,), (1,)), ((), ())), preferred_element_type=jnp.float32
    )


def inverse_rms(values):
    return lax.rsqrt(jnp.mean(values * values, axis=-1, keepdims=True) + NORM_EPS)


def norm_backward(values, scale, gain, grad_normed):
    weighted = grad_normed * gain
    grad_gain = jnp.sum(grad_normed * values * scale, axis=0)
    cubed = scale * scale * scale
    grad_values = scale * weighted - values * cubed * jnp.mean(
        weighted * values, axis=-1, keepdims=True
    )
    return (grad_values, grad_gain)


def adamw_update(param, grad, first, second, rate, decay):
    first_new = BETA_ONE * first + (1.0 - BETA_ONE) * grad
    second_new = BETA_TWO * second + (1.0 - BETA_TWO) * grad * grad
    first_hat = first_new / (1.0 - BETA_ONE**STEP)
    second_hat = second_new / (1.0 - BETA_TWO**STEP)
    param_new = param - rate * (first_hat / (jnp.sqrt(second_hat) + ADAM_EPS) + decay * param)
    return (param_new, first_new, second_new)


def adamw_kernel(*refs):
    grads, state, outs = refs[:5], refs[5:23], refs[23:]
    vectors = grads[0][...].T
    found = [vectors[:2], vectors[2:5]] + [ref[...] for ref in grads[1:]]
    for index, grad in enumerate(found):
        rate, decay = (RATE_VECTOR, 0.0) if index < 2 else (RATE_MATRIX, DECAY)
        param, first, second = (state[6 * kind + index][...] for kind in range(3))
        new = adamw_update(param, grad, first, second, rate, decay)
        for kind, value in enumerate((grad,) + new):
            outs[6 * kind + index][...] = value


def adamw(grads, params, firsts, seconds):
    inner = pl.BlockSpec(memory_space=pltpu.VMEM)
    return pl.pallas_call(
        adamw_kernel,
        out_shape=[jax.ShapeDtypeStruct(p.shape, p.dtype) for p in params] * 4,
        in_specs=[inner] * 23,
        out_specs=[inner] * 24,
        compiler_params=pltpu.CompilerParams(vmem_limit_bytes=48 << 20),
        name="adamw",
    )(*grads, *params, *firsts, *seconds)


def local(
    hidden_in,
    cotangent,
    doc_position,
    norm_gains,
    conv_taps,
    in_proj,
    out_proj,
    gate_up,
    down_proj,
    first_gains,
    first_taps,
    first_in,
    first_out,
    first_gate_up,
    first_down,
    second_gains,
    second_taps,
    second_in,
    second_out,
    second_gate_up,
    second_down,
):
    half = jnp.bfloat16
    single = jnp.float32
    row_count, length, width = hidden_in.shape
    tok_count = row_count * length
    chips, depth = lax.axis_size("ring"), lax.axis_size("fsdp")
    in_width = in_proj.shape[1]
    out_width = out_proj.shape[1]
    vectors = jnp.concatenate([norm_gains, conv_taps], axis=0).T.astype(half)
    packed = jnp.concatenate(
        [
            in_proj.astype(half),
            out_proj.astype(half),
            jnp.pad(vectors, ((0, 0), (0, LANES - vectors.shape[1]))),
            gate_up.astype(half),
        ],
        axis=1,
    )
    packed_full, down_full = gather(chips, depth, packed, down_proj.astype(half))
    in_full = packed_full[:, :in_width]
    out_full = packed_full[:, in_width : in_width + out_width]
    vector_start = in_width + out_width
    vectors_full = packed_full[:, vector_start : vector_start + LANES].astype(single).T
    mixer_full = (None, None, in_full, out_full)
    gains_f = vectors_full[:2]
    taps_f = vectors_full[2:5]
    resid_one = hidden_in.reshape(tok_count, width).astype(single)
    scale_one = inverse_rms(resid_one)
    normed_one = (resid_one * scale_one * gains_f[0]).astype(half)
    projected = matmul(normed_one, mixer_full[2])
    b_branch = projected[:, :width]
    c_branch = projected[:, width : 2 * width]
    x_branch = projected[:, 2 * width :]
    gated_input = (b_branch * x_branch).astype(half)
    gated_rows = gated_input.reshape(row_count, length, width)
    carried = from_behind(gated_rows[:, length - 2 :, :], SEQ, 1)
    extended = jnp.concatenate([carried, gated_rows], axis=1).astype(single)
    gated_f = extended[:, 2:].reshape(tok_count, width)
    prev_one = extended[:, 1 : length + 1].reshape(tok_count, width)
    prev_two = extended[:, :length].reshape(tok_count, width)
    positions = doc_position.reshape(tok_count)
    mask_one = (positions >= 1).astype(single)[:, None]
    mask_two = (positions >= 2).astype(single)[:, None]
    conv_out = (
        taps_f[0] * gated_f + mask_one * taps_f[1] * prev_one + mask_two * taps_f[2] * prev_two
    )
    mixer_act = (c_branch * conv_out).astype(half)
    resid_two = resid_one + matmul(mixer_act, mixer_full[3])
    scale_two = inverse_rms(resid_two)
    normed_two = (resid_two * scale_two * gains_f[1]).astype(half)
    ffn_full = (packed_full[:, vector_start + LANES :], down_full)
    hidden_units = ffn_full[0].shape[1] // 2
    ffn_pre = matmul(normed_two, ffn_full[0])
    gate_pre = ffn_pre[:, :hidden_units]
    up_pre = ffn_pre[:, hidden_units:]
    sigmoid_gate = jax.nn.sigmoid(gate_pre)
    silu_gate = gate_pre * sigmoid_gate
    ffn_act = (silu_gate * up_pre).astype(half)
    block_out = resid_two + matmul(ffn_act, ffn_full[1])
    cot_rows = cotangent.reshape(tok_count, width)
    grad_act = matmul_nt(cot_rows, ffn_full[1])
    grad_gate = grad_act * up_pre * sigmoid_gate * (1.0 + gate_pre * (1.0 - sigmoid_gate))
    grad_both = jnp.concatenate([grad_gate, grad_act * silu_gate], axis=1).astype(half)
    grad_normed = matmul_nt(grad_both, ffn_full[0])
    grad_down = matmul_tn(ffn_act, cot_rows)
    grad_gate_up = matmul_tn(normed_two, grad_both)
    norm_part, gain_two_grad = norm_backward(resid_two, scale_two, gains_f[1], grad_normed)
    grad_resid = cot_rows.astype(single) + norm_part
    resid_cast = grad_resid.astype(half)
    grad_mixer = matmul_nt(resid_cast, mixer_full[3])
    grad_cbranch = grad_mixer * conv_out
    grad_conv = grad_mixer * c_branch
    masked_one = mask_one * grad_conv
    masked_two = mask_two * grad_conv
    grad_taps = jnp.stack(
        [
            jnp.sum(grad_conv * gated_f, axis=0),
            jnp.sum(masked_one * prev_one, axis=0),
            jnp.sum(masked_two * prev_two, axis=0),
        ]
    )
    one_rows = masked_one.reshape(row_count, length, width)
    two_rows = masked_two.reshape(row_count, length, width)
    leading = from_behind((one_rows[:, :2, :], two_rows[:, :2, :]), SEQ, -1)
    ext_one = jnp.concatenate([one_rows, leading[0]], axis=1)
    ext_two = jnp.concatenate([two_rows, leading[1]], axis=1)
    next_one = ext_one[:, 1 : length + 1].reshape(tok_count, width)
    next_two = ext_two[:, 2 : length + 2].reshape(tok_count, width)
    grad_gated = taps_f[0] * grad_conv + taps_f[1] * next_one + taps_f[2] * next_two
    grad_proj = jnp.concatenate(
        [grad_gated * x_branch, grad_cbranch, grad_gated * b_branch], axis=1
    ).astype(half)
    grad_normone = matmul_nt(grad_proj, mixer_full[2])
    first_part, gain_one_grad = norm_backward(resid_one, scale_one, gains_f[0], grad_normone)
    grad_hidden = grad_resid + first_part
    grad_gains = jnp.stack([gain_one_grad, gain_two_grad])
    grad_in = matmul_tn(normed_one, grad_proj)
    grad_out = matmul_tn(mixer_act, resid_cast)
    vector_grads = jnp.concatenate([grad_gains, grad_taps], axis=0)
    vector_count = vector_grads.shape[0]
    vector_columns = jnp.pad(vector_grads.T, ((0, 0), (0, LANES - vector_count))).astype(half)
    grad_side = jnp.concatenate([vector_columns, grad_out.astype(half)], axis=1)
    gate_owned, in_owned, side_owned, down_owned = scatter(
        chips,
        depth,
        grad_gate_up.astype(half),
        grad_in.astype(half),
        grad_side,
        grad_down.astype(half),
    )
    params = (norm_gains, conv_taps, in_proj, out_proj, gate_up, down_proj)
    firsts = (first_gains, first_taps, first_in, first_out, first_gate_up, first_down)
    seconds = (second_gains, second_taps, second_in, second_out, second_gate_up, second_down)
    owned = (side_owned[:, :LANES], in_owned, side_owned[:, LANES:], gate_owned, down_owned)
    results = adamw(owned, params, firsts, seconds)
    out_rows = block_out.reshape(row_count, length, width)
    grad_rows = grad_hidden.reshape(row_count, length, width)
    return (
        out_rows,
        grad_rows,
        *results,
    )


def solution(mesh):
    tokens, depth = mesh.devices.shape
    chip_mesh = Mesh(mesh.devices.reshape(tokens // 2, 2, depth), ALL)
    in_specs = (
        P("fsdp", SEQ, None),
        P("fsdp", SEQ, None),
        P("fsdp", SEQ),
        P(None, ALL),
        P(None, ALL),
        P(ALL, None),
        P(ALL, None),
        P(ALL, None),
        P(ALL, None),
        P(None, ALL),
        P(None, ALL),
        P(ALL, None),
        P(ALL, None),
        P(ALL, None),
        P(ALL, None),
        P(None, ALL),
        P(None, ALL),
        P(ALL, None),
        P(ALL, None),
        P(ALL, None),
        P(ALL, None),
    )
    out_specs = (
        P("fsdp", SEQ, None),
        P("fsdp", SEQ, None),
        P(None, ALL),
        P(None, ALL),
        P(ALL, None),
        P(ALL, None),
        P(ALL, None),
        P(ALL, None),
        P(None, ALL),
        P(None, ALL),
        P(ALL, None),
        P(ALL, None),
        P(ALL, None),
        P(ALL, None),
        P(None, ALL),
        P(None, ALL),
        P(ALL, None),
        P(ALL, None),
        P(ALL, None),
        P(ALL, None),
        P(None, ALL),
        P(None, ALL),
        P(ALL, None),
        P(ALL, None),
        P(ALL, None),
        P(ALL, None),
    )
    return jax.shard_map(local, mesh=chip_mesh, in_specs=in_specs, out_specs=out_specs, check_vma=False)
```

```python
import functools

import jax
import jax.numpy as jnp
from jax import lax
from jax.experimental import pallas as pl
from jax.experimental.pallas import tpu as pltpu
from jax.sharding import Mesh
from jax.sharding import PartitionSpec as P

STEP = 3


NORM_EPS = 1e-05
BETA_ONE = 0.9
BETA_TWO = 0.999
ADAM_EPS = 1e-08
RATE_MATRIX = 0.005
RATE_VECTOR = 0.2
DECAY = 0.1
LANES = 128
VMEM_SCATTER = 46 << 20
UNIT_TILE = 512
MESH_ID = pl.DeviceIdType.MESH
SEQ = ("ring", "core")
ALL = ("ring", "core", "fsdp")


def snake(index):
    return 2 * (index // 2) + (index % 2 + index // 2) % 2


def halves(columns):
    first = (columns // 2 + LANES - 1) // LANES * LANES
    return (pl.ds(0, first), pl.ds(first, columns - first))


class Place:
    def __init__(self, chips, depth):
        self.chips, self.depth = chips, depth
        self.core = lax.axis_index("core")
        self.layer = lax.axis_index("fsdp")
        self.spot = snake(lax.axis_index("ring"))
        self.own = lax.axis_index("ring")
        self.right = self.device(snake((self.spot + 1) % chips), self.core, self.layer)
        self.left = self.device(snake((self.spot + chips - 1) % chips), self.core, self.layer)
        self.up = self.device(self.own, self.core, (self.layer + 1) % depth)
        self.down = self.device(self.own, self.core, (self.layer + depth - 1) % depth)
        self.sibling = self.device(self.own, 1 - self.core, self.layer)

    def device(self, ring, core, layer):
        return (ring, core, layer)

    def shard(self, spot, core, layer):
        return (snake(spot) * 2 + core) * self.depth + layer

    def greet(self):
        for device in (self.right, self.left, self.up, self.down, self.sibling):
            pl.semaphore_signal(
                pltpu.get_barrier_semaphore(), inc=1, device_id=device, device_id_type=MESH_ID
            )

    def await_greetings(self):
        pl.semaphore_wait(pltpu.get_barrier_semaphore(), 5)


def gather_kernel(chips, depth, groups, *refs):
    count, inputs = len(groups), sum(groups)
    wholes = refs[inputs : inputs + count]
    shards = refs[inputs + count : inputs + 2 * count]
    sent, from_sibling, from_below, from_ring, kept, late_ring, late_below = refs[
        inputs + 2 * count :
    ]
    here = Place(chips, depth)
    here.greet()
    taken = 0
    for shard, members in zip(shards, groups):
        start = 0
        for member in refs[taken : taken + members]:
            shard[:, start : start + member.shape[1]] = member[...].astype(shard.dtype)
            start += member.shape[1]
        taken += members
    here.await_greetings()
    late = count - 1
    cuts = [halves(ref.shape[1]) for ref in shards]

    def block(which, shard):
        return wholes[which].at[shard]

    def piece_of(which, shard, way):
        return wholes[which].at[shard, :, cuts[which][way]]

    def send(source, target, which, arrived, device):
        pltpu.make_async_remote_copy(
            src_ref=source,
            dst_ref=target,
            send_sem=sent.at[which],
            recv_sem=arrived,
            device_id=device,
            device_id_type=MESH_ID,
        ).start()

    def awaited(ref, arrived):
        pltpu.make_async_copy(ref, ref, arrived).wait()

    own = here.shard(here.spot, here.core, here.layer)
    for which in range(late):
        send(shards[which], block(which, own), which, from_below.at[which, 0], here.up)
        for way in range(2):
            send(
                shards[which].at[:, cuts[which][way]],
                piece_of(which, own, way),
                which,
                from_ring.at[which, way, 0],
                (here.right, here.left)[way],
            )
    for way in range(2):
        part = shards[late].at[:, cuts[late][way]]
        piece = piece_of(late, own, way)
        send(part, piece, late, late_ring.at[way, 0], (here.right, here.left)[way])
        send(part, piece, late, late_below.at[way, 0], here.up)
    for which in range(count):
        send(shards[which], block(which, own), which, from_sibling.at[which], here.sibling)
        pltpu.make_async_copy(shards[which], block(which, own), kept.at[which]).start()

    def late_around(hop):
        for way in range(2):
            away = (chips - hop, hop)[way]
            piece = piece_of(late, here.shard((here.spot + away) % chips, here.core, here.layer), way)
            awaited(piece, late_ring.at[way, hop - 1])
            if hop < chips - 1:
                send(piece, piece, late, late_ring.at[way, hop], (here.right, here.left)[way])
            send(piece, piece, late, late_below.at[way, hop], here.up)
            send(piece, piece, late, from_sibling.at[late], here.sibling)

    def late_layer(layer_step, hop):
        layer = (here.layer + depth - layer_step) % depth
        for way in range(2):
            away = (chips - hop, hop)[way]
            piece = piece_of(late, here.shard((here.spot + away) % chips, here.core, layer), way)
            awaited(piece, late_below.at[way, (layer_step - 1) * chips + hop])

            @pl.when(layer_step < depth - 1)
            def _():
                send(piece, piece, late, late_below.at[way, layer_step * chips + hop], here.up)

            send(piece, piece, late, from_sibling.at[late], here.sibling)

    def late_step(layer_step, hop):
        if hop > 0:
            @pl.when(layer_step == 0)
            def _():
                late_around(hop)

        @pl.when(layer_step > 0)
        def _():
            late_layer(layer_step, hop)

    def around(hop, layer_step):
        layer = (here.layer + depth - layer_step) % depth
        for which in range(late):
            for way in range(2):
                away = (chips - hop, hop)[way]
                shard = here.shard((here.spot + away) % chips, here.core, layer)
                arrived = layer_step * (chips - 1) + hop - 1
                piece = piece_of(which, shard, way)
                awaited(piece, from_ring.at[which, way, arrived])
                if hop < chips - 1:
                    send(
                        piece,
                        piece,
                        which,
                        from_ring.at[which, way, arrived + 1],
                        (here.right, here.left)[way],
                    )
                send(piece, piece, which, from_sibling.at[which], here.sibling)

    def layer_arrives(layer_step):
        layer = (here.layer + depth - layer_step) % depth
        shard = here.shard(here.spot, here.core, layer)
        for which in range(late):
            whole = block(which, shard)
            awaited(whole, from_below.at[which, layer_step - 1])

            @pl.when(layer_step < depth - 1)
            def _():
                send(whole, whole, which, from_below.at[which, layer_step], here.up)

            for way in range(2):
                piece = piece_of(which, shard, way)
                send(
                    piece,
                    piece,
                    which,
                    from_ring.at[which, way, layer_step * (chips - 1)],
                    (here.right, here.left)[way],
                )
            send(whole, whole, which, from_sibling.at[which], here.sibling)

    @pl.loop(0, depth)
    def _(layer_step):
        late_step(layer_step, 0)
        for hop in range(1, chips - 1):
            around(hop, layer_step)
            late_step(layer_step, hop)

        @pl.when(layer_step < depth - 1)
        def _():
            layer_arrives(layer_step + 1)

        around(chips - 1, layer_step)
        late_step(layer_step, chips - 1)

    shard_count = 2 * chips * depth
    for which in range(count):
        pltpu.make_async_copy(shards[which], block(which, own), kept.at[which]).wait()
        awaited(wholes[which].at[pl.ds(0, shard_count // 2)], from_sibling.at[which])
        awaited(wholes[which].at[pl.ds(0, shard_count - 1)], sent.at[which])


def gather(chips, depth, *groups):
    count = len(groups)
    steps = depth * (chips - 1)
    shard_count = 2 * chips * depth
    shapes = [(g[0].shape[0], sum(x.shape[1] for x in g)) for g in groups]
    half = jnp.bfloat16
    return pl.pallas_call(
        functools.partial(gather_kernel, chips, depth, [len(g) for g in groups]),
        out_shape=[jax.ShapeDtypeStruct((shard_count,) + shape, half) for shape in shapes],
        in_specs=[pl.BlockSpec(memory_space=pltpu.VMEM)] * sum(len(g) for g in groups),
        out_specs=[pl.BlockSpec(memory_space=pl.ANY)] * count,
        scratch_shapes=[pltpu.VMEM(shape, half) for shape in shapes]
        + [
            pltpu.SemaphoreType.DMA((count,)),
            pltpu.SemaphoreType.DMA((count,)),
            pltpu.SemaphoreType.DMA((count, depth - 1)),
            pltpu.SemaphoreType.DMA((count, 2, steps)),
            pltpu.SemaphoreType.DMA((count,)),
            pltpu.SemaphoreType.DMA((2, chips - 1)),
            pltpu.SemaphoreType.DMA((2, chips * (depth - 1))),
        ],
        compiler_params=pltpu.CompilerParams(
            collective_id=0, has_side_effects=True, vmem_limit_bytes=16 << 20
        ),
        name="gather_weights",
    )(*[x for g in groups for x in g])


def scatter_kernel(chips, depth, count, *refs):
    grads = refs[:count]
    owned = refs[count : 2 * count]
    rest = refs[2 * count :]
    theirs = rest[:count]
    staged = rest[count : 2 * count]
    ringed = rest[2 * count : 3 * count]
    layered = rest[3 * count : 4 * count]
    sent, loaded, from_sibling, from_below, from_ring, late_below = rest[4 * count :]
    here = Place(chips, depth)
    late = count - 1
    cuts = [halves(ref.shape[1]) for ref in owned]
    f32 = jnp.float32

    def part(which, shard, way):
        if len(grads[which].shape) == 4:
            return grads[which].at[way, shard]
        return grads[which].at[shard, :, cuts[which][way]]

    def place(hop, way):
        away = (chips - hop, hop)[way]
        return (here.spot + away) % chips

    def layer_of(layer_step):
        return (here.layer + 2 * depth - 1 - layer_step) % depth

    def slot_of(layer_step, hop):
        return layer_step * chips + hop - 1

    def load(which, layer_step, hop, start):
        for way, cut in enumerate(cuts[which]):
            shard = here.shard(place(hop, way), here.core, layer_of(layer_step))
            copy = pltpu.make_async_copy(
                part(which, shard, way),
                staged[which].at[hop - 1, :, cut],
                loaded.at[which, way, hop - 1],
            )
            copy.start() if start else copy.wait()

    def hand_over(which, slot):
        layer_step = slot // chips
        hop = slot % chips + 1
        for way, cut in enumerate(cuts[which]):
            shard = here.shard(place(hop, way), 1 - here.core, layer_of(layer_step))
            pltpu.make_async_remote_copy(
                src_ref=part(which, shard, way),
                dst_ref=theirs[which].at[slot, :, cut],
                send_sem=sent.at[which],
                recv_sem=from_sibling.at[which, way, slot],
                device_id=here.sibling,
                device_id_type=MESH_ID,
            ).start()

    slots = chips * depth
    for hop in range(1, chips + 1):
        for which in range(count):
            load(which, 0, hop, True)
    here.greet()
    here.await_greetings()

    @pl.loop(0, slots)
    def _(slot):
        for which in range(count):
            hand_over(which, slot)

    def got(ref, semaphore):
        pltpu.make_async_copy(ref, ref, semaphore).wait()

    def step(layer_step, hop):
        slot = slot_of(layer_step, hop)
        for which in range(late):
            load(which, layer_step, hop, False)
            if hop == chips:
                @pl.when(layer_step > 0)
                def _():
                    ref = layered[which].at[layer_step - 1]
                    got(ref, from_below.at[which, layer_step - 1])

            for way, cut in enumerate(cuts[which]):
                mine = theirs[which].at[slot, :, cut]
                got(mine, from_sibling.at[which, way, slot])
                total = mine[...].astype(f32) + staged[which][hop - 1, :, cut].astype(f32)
                if hop > 1:
                    index = layer_step * (chips - 1) + hop - 2
                    arrived = ringed[which].at[index, :, cut]
                    got(arrived, from_ring.at[which, way, index])
                    total = total + arrived[...].astype(f32)
                if hop < chips:
                    index = layer_step * (chips - 1) + hop - 1
                    mine[...] = total.astype(mine.dtype)
                    pltpu.make_async_remote_copy(
                        src_ref=mine,
                        dst_ref=ringed[which].at[index, :, cut],
                        send_sem=sent.at[which],
                        recv_sem=from_ring.at[which, way, index],
                        device_id=(here.right, here.left)[way],
                        device_id_type=MESH_ID,
                    ).start()
                else:
                    owned[which][:, cut] = total

            if hop == chips:
                @pl.when(layer_step > 0)
                def _():
                    owned[which][...] += layered[which][layer_step - 1].astype(f32)

                @pl.when(layer_step < depth - 1)
                def _():
                    mine = theirs[which].at[slot]
                    mine[...] = owned[which][...].astype(mine.dtype)
                    pltpu.make_async_remote_copy(
                        src_ref=mine,
                        dst_ref=layered[which].at[layer_step],
                        send_sem=sent.at[which],
                        recv_sem=from_below.at[which, layer_step],
                        device_id=here.up,
                        device_id_type=MESH_ID,
                    ).start()

        @pl.when(layer_step < depth - 1)
        def _():
            for which in range(late):
                load(which, layer_step + 1, hop, True)

    def late_step(layer_step, hop):
        slot = slot_of(layer_step, hop)
        load(late, layer_step, hop, False)
        for way, cut in enumerate(cuts[late]):
            mine = theirs[late].at[slot, :, cut]
            got(mine, from_sibling.at[late, way, slot])
            total = mine[...].astype(f32) + staged[late][hop - 1, :, cut].astype(f32)
            mine[...] = total.astype(mine.dtype)

            @pl.when(layer_step > 0)
            def _():
                before = slot_of(layer_step - 1, hop)
                arrived = layered[late].at[before, :, cut]
                got(arrived, late_below.at[way, before])
                both = total + arrived[...].astype(f32)
                mine[...] = both.astype(mine.dtype)

            @pl.when(layer_step < depth - 1)
            def _():
                pltpu.make_async_remote_copy(
                    src_ref=mine,
                    dst_ref=layered[late].at[slot, :, cut],
                    send_sem=sent.at[late],
                    recv_sem=late_below.at[way, slot],
                    device_id=here.up,
                    device_id_type=MESH_ID,
                ).start()

            @pl.when(layer_step == depth - 1)
            def _():
                around = mine[...].astype(f32)
                if hop > 1:
                    arrived = ringed[late].at[hop - 2, :, cut]
                    got(arrived, from_ring.at[late, way, hop - 2])
                    around = around + arrived[...].astype(f32)
                if hop < chips:
                    mine[...] = around.astype(mine.dtype)
                    pltpu.make_async_remote_copy(
                        src_ref=mine,
                        dst_ref=ringed[late].at[hop - 1, :, cut],
                        send_sem=sent.at[late],
                        recv_sem=from_ring.at[late, way, hop - 1],
                        device_id=(here.right, here.left)[way],
                        device_id_type=MESH_ID,
                    ).start()
                else:
                    owned[late][:, cut] = around

        @pl.when(layer_step < depth - 1)
        def _():
            load(late, layer_step + 1, hop, True)

    step(0, 1)

    @pl.loop(0, depth)
    def _(layer_step):
        late_step(layer_step, 1)
        for hop in range(2, chips):
            step(layer_step, hop)
            late_step(layer_step, hop)

        @pl.when(layer_step < depth - 1)
        def _():
            step(layer_step + 1, 1)

        late_step(layer_step, chips)
        step(layer_step, chips)

    for which in range(count):
        some = pl.ds(0, 2 * slots - 1)
        most = grads[which].at[:, some] if len(grads[which].shape) == 4 else grads[which].at[some]
        pltpu.make_async_copy(most, most, sent.at[which]).wait()


def scatter(chips, depth, *grads):
    count = len(grads)
    slots = chips * depth
    steps = depth * (chips - 1)
    shapes = [
        (g.shape[1], g.shape[2]) if g.ndim == 3 else (g.shape[2], 2 * g.shape[3]) for g in grads
    ]
    anywhere = pl.BlockSpec(memory_space=pl.ANY)
    inner = pl.BlockSpec(memory_space=pltpu.VMEM)

    def room(most, last):
        leading = [most] * (count - 1) + [last]
        return [pltpu.VMEM((n,) + x, jnp.bfloat16) for n, x in zip(leading, shapes)]

    return pl.pallas_call(
        functools.partial(scatter_kernel, chips, depth, count),
        out_shape=[jax.ShapeDtypeStruct(x, jnp.float32) for x in shapes],
        in_specs=[anywhere] * count,
        out_specs=[inner] * count,
        scratch_shapes=room(slots, slots)
        + room(chips, chips)
        + room(steps, chips - 1)
        + room(depth - 1, chips * (depth - 1))
        + [
            pltpu.SemaphoreType.DMA((count,)),
            pltpu.SemaphoreType.DMA((count, 2, chips)),
            pltpu.SemaphoreType.DMA((count, 2, slots)),
            pltpu.SemaphoreType.DMA((count, depth - 1)),
            pltpu.SemaphoreType.DMA((count, 2, steps)),
            pltpu.SemaphoreType.DMA((2, chips * (depth - 1))),
        ],
        compiler_params=pltpu.CompilerParams(
            collective_id=1, has_side_effects=True, vmem_limit_bytes=VMEM_SCATTER
        ),
        name="scatter_gradients",
    )(*grads)


def from_behind(value, axis, steps):
    count = lax.axis_size(axis)
    first, last = (max(0, -steps), min(count, count - steps))
    return lax.ppermute(value, axis, [(source, source + steps) for source in range(first, last)])


def matmul(left, right):
    return jnp.dot(left, right, preferred_element_type=jnp.float32)


def matmul_tn(left, right):
    return lax.dot_general(
        left, right, (((0,), (0,)), ((), ())), preferred_element_type=jnp.float32
    )


def matmul_nt(left, right):
    return lax.dot_general(
        left, right, (((1,), (1,)), ((), ())), preferred_element_type=jnp.float32
    )


def inverse_rms(values):
    return lax.rsqrt(jnp.mean(values * values, axis=-1, keepdims=True) + NORM_EPS)


def norm_backward(values, scale, gain, grad_normed):
    weighted = grad_normed * gain
    grad_gain = jnp.sum(grad_normed * values * scale, axis=0)
    cubed = scale * scale * scale
    grad_values = scale * weighted - values * cubed * jnp.mean(
        weighted * values, axis=-1, keepdims=True
    )
    return (grad_values, grad_gain)


def adamw_update(param, grad, first, second, rate, decay):
    first_new = BETA_ONE * first + (1.0 - BETA_ONE) * grad
    second_new = BETA_TWO * second + (1.0 - BETA_TWO) * grad * grad
    first_hat = first_new / (1.0 - BETA_ONE**STEP)
    second_hat = second_new / (1.0 - BETA_TWO**STEP)
    param_new = param - rate * (first_hat / (jnp.sqrt(second_hat) + ADAM_EPS) + decay * param)
    return (param_new, first_new, second_new)


def adamw_kernel(*refs):
    grads, state, outs = refs[:4], refs[4:22], refs[22:]
    side, lanes, width = grads[0], outs[0].shape[1], outs[3].shape[1]
    vectors = side[:8, width:]
    found = [vectors[:2, :lanes], vectors[2:5, :lanes], grads[1][...], side[:, :width]]
    found += [ref[...] for ref in grads[2:]]
    for index, grad in enumerate(found):
        rate, decay = (RATE_VECTOR, 0.0) if index < 2 else (RATE_MATRIX, DECAY)
        param, first, second = (state[6 * kind + index][...] for kind in range(3))
        new = adamw_update(param, grad, first, second, rate, decay)
        for kind, value in enumerate((grad,) + new):
            outs[6 * kind + index][...] = value


def adamw(grads, params, firsts, seconds):
    inner = pl.BlockSpec(memory_space=pltpu.VMEM)
    return pl.pallas_call(
        adamw_kernel,
        out_shape=[jax.ShapeDtypeStruct(p.shape, p.dtype) for p in params] * 4,
        in_specs=[inner] * 22,
        out_specs=[inner] * 24,
        compiler_params=pltpu.CompilerParams(vmem_limit_bytes=48 << 20),
        name="adamw",
    )(*grads, *params, *firsts, *seconds)


def feed_forward_kernel(
    normed, turned, resid, cot, gate, up, down, out, grad_normed, grad_down, grad_gate_up
):
    half = jnp.bfloat16

    @pl.when(pl.program_id(0) == 0)
    def _():
        out[...] = resid[...]
        grad_normed[...] = jnp.zeros_like(grad_normed)

    gate_pre = matmul(normed[...], gate[...])
    up_pre = matmul(normed[...], up[...])
    grad_act = matmul_nt(cot[...], down[...])
    sigmoid_gate = jax.nn.sigmoid(gate_pre)
    silu_gate = gate_pre * sigmoid_gate
    act = (silu_gate * up_pre).astype(half)
    grad_gate = grad_act * up_pre * sigmoid_gate * (1.0 + gate_pre * (1.0 - sigmoid_gate))
    grad_gate = grad_gate.astype(half)
    grad_up = (grad_act * silu_gate).astype(half)
    out[...] += matmul(act, down[...])
    grad_normed[...] += matmul_nt(grad_gate, gate[...]) + matmul_nt(grad_up, up[...])
    grad_down[...] = matmul_tn(act, cot[...]).astype(half)
    grad_gate_up[0] = matmul(turned[...], grad_gate).astype(half)
    grad_gate_up[1] = matmul(turned[...], grad_up).astype(half)


def feed_forward(normed, resid, cot, packed, down):
    tokens, width = normed.shape
    units = down.shape[0]
    tile = UNIT_TILE
    tiles = units // tile
    half, single = jnp.bfloat16, jnp.float32

    def fixed(rows, columns):
        return pl.BlockSpec((rows, columns), lambda i: (0, 0))

    flops = 2 * tokens * width * units * 9
    return pl.pallas_call(
        feed_forward_kernel,
        grid=(tiles,),
        out_shape=[
            jax.ShapeDtypeStruct((tokens, width), single),
            jax.ShapeDtypeStruct((tokens, width), single),
            jax.ShapeDtypeStruct((units, width), half),
            jax.ShapeDtypeStruct((2, width, units), half),
        ],
        in_specs=[
            fixed(tokens, width),
            fixed(width, tokens),
            fixed(tokens, width),
            fixed(tokens, width),
            pl.BlockSpec((width, tile), lambda i: (0, i)),
            pl.BlockSpec((width, tile), lambda i: (0, i + tiles)),
            pl.BlockSpec((tile, width), lambda i: (i, 0)),
        ],
        out_specs=[
            fixed(tokens, width),
            fixed(tokens, width),
            pl.BlockSpec((tile, width), lambda i: (i, 0)),
            pl.BlockSpec((2, width, tile), lambda i: (0, 0, i)),
        ],
        compiler_params=pltpu.CompilerParams(vmem_limit_bytes=48 << 20),
        cost_estimate=pl.CostEstimate(
            flops=flops, bytes_accessed=12 * width * units, transcendentals=tokens * units
        ),
        name="feed_forward",
    )(normed, normed.T, resid, cot, packed, packed, down)


def local(
    hidden_in,
    cotangent,
    doc_position,
    norm_gains,
    conv_taps,
    in_proj,
    out_proj,
    gate_up,
    down_proj,
    first_gains,
    first_taps,
    first_in,
    first_out,
    first_gate_up,
    first_down,
    second_gains,
    second_taps,
    second_in,
    second_out,
    second_gate_up,
    second_down,
):
    half = jnp.bfloat16
    single = jnp.float32
    row_count, length, width = hidden_in.shape
    tok_count = row_count * length
    chips, depth = lax.axis_size("ring"), lax.axis_size("fsdp")
    in_width = in_proj.shape[1]
    out_width = out_proj.shape[1]
    rows, unit_columns = gate_up.shape
    shards = 2 * chips * depth
    vectors = jnp.concatenate([norm_gains, conv_taps], axis=0)
    vector_count, lanes = vectors.shape
    corner = ((0, rows - vector_count), (0, LANES - lanes))
    packed_shards, down_shards = gather(
        chips, depth, (gate_up, in_proj, out_proj, jnp.pad(vectors, corner)), (down_proj,)
    )
    packed_full = packed_shards.reshape(width, -1)
    down_full = down_shards.reshape(-1, width)
    out_start = unit_columns + in_width
    in_full = packed_full[:, unit_columns:out_start]
    out_full = packed_full[:, out_start : out_start + out_width]
    vectors_full = packed_shards[:, :vector_count, -LANES:][:, :, :lanes].astype(single)
    vectors_full = vectors_full.transpose(1, 0, 2).reshape(vector_count, width)
    mixer_full = (None, None, in_full, out_full)
    gains_f = vectors_full[:2]
    taps_f = vectors_full[2:5]
    resid_one = hidden_in.reshape(tok_count, width).astype(single)
    scale_one = inverse_rms(resid_one)
    normed_one = (resid_one * scale_one * gains_f[0]).astype(half)
    projected = matmul(normed_one, mixer_full[2])
    b_branch = projected[:, :width]
    c_branch = projected[:, width : 2 * width]
    x_branch = projected[:, 2 * width :]
    gated_input = (b_branch * x_branch).astype(half)
    gated_rows = gated_input.reshape(row_count, length, width)
    carried = from_behind(gated_rows[:, length - 2 :, :], SEQ, 1)
    extended = jnp.concatenate([carried, gated_rows], axis=1).astype(single)
    gated_f = extended[:, 2:].reshape(tok_count, width)
    prev_one = extended[:, 1 : length + 1].reshape(tok_count, width)
    prev_two = extended[:, :length].reshape(tok_count, width)
    positions = doc_position.reshape(tok_count)
    mask_one = (positions >= 1).astype(single)[:, None]
    mask_two = (positions >= 2).astype(single)[:, None]
    conv_out = (
        taps_f[0] * gated_f + mask_one * taps_f[1] * prev_one + mask_two * taps_f[2] * prev_two
    )
    mixer_act = (c_branch * conv_out).astype(half)
    resid_two = resid_one + matmul(mixer_act, mixer_full[3])
    scale_two = inverse_rms(resid_two)
    normed_two = (resid_two * scale_two * gains_f[1]).astype(half)
    cot_rows = cotangent.reshape(tok_count, width)
    block_out, grad_normed, grad_down, grad_gate_up = feed_forward(
        normed_two, resid_two, cot_rows, packed_full, down_full
    )
    norm_part, gain_two_grad = norm_backward(resid_two, scale_two, gains_f[1], grad_normed)
    grad_resid = cot_rows.astype(single) + norm_part
    resid_cast = grad_resid.astype(half)
    grad_mixer = matmul_nt(resid_cast, mixer_full[3])
    grad_cbranch = grad_mixer * conv_out
    grad_conv = grad_mixer * c_branch
    masked_one = mask_one * grad_conv
    masked_two = mask_two * grad_conv
    grad_taps = jnp.stack(
        [
            jnp.sum(grad_conv * gated_f, axis=0),
            jnp.sum(masked_one * prev_one, axis=0),
            jnp.sum(masked_two * prev_two, axis=0),
        ]
    )
    one_rows = masked_one.reshape(row_count, length, width)
    two_rows = masked_two.reshape(row_count, length, width)
    leading = from_behind((one_rows[:, :2, :], two_rows[:, :2, :]), SEQ, -1)
    ext_one = jnp.concatenate([one_rows, leading[0]], axis=1)
    ext_two = jnp.concatenate([two_rows, leading[1]], axis=1)
    next_one = ext_one[:, 1 : length + 1].reshape(tok_count, width)
    next_two = ext_two[:, 2 : length + 2].reshape(tok_count, width)
    grad_gated = taps_f[0] * grad_conv + taps_f[1] * next_one + taps_f[2] * next_two
    grad_proj = jnp.concatenate(
        [grad_gated * x_branch, grad_cbranch, grad_gated * b_branch], axis=1
    ).astype(half)
    grad_normone = matmul_nt(grad_proj, mixer_full[2])
    first_part, gain_one_grad = norm_backward(resid_one, scale_one, gains_f[0], grad_normone)
    grad_hidden = grad_resid + first_part
    grad_gains = jnp.stack([gain_one_grad, gain_two_grad])
    grad_in = matmul_tn(normed_one, grad_proj)
    grad_out = matmul_tn(mixer_act, resid_cast)
    vector_grads = jnp.concatenate([grad_gains, grad_taps], axis=0)
    vector_shards = vector_grads.reshape(vector_count, shards, lanes).transpose(1, 0, 2)
    vector_shards = jnp.pad(vector_shards.astype(half), ((0, 0),) + corner)
    grad_side = jnp.concatenate(
        [grad_out.astype(half).reshape(shards, rows, out_width), vector_shards], axis=2
    )
    gate_owned, in_owned, side_owned, down_owned = scatter(
        chips,
        depth,
        grad_gate_up.reshape(2, shards, rows, -1),
        grad_in.astype(half).reshape(shards, rows, in_width),
        grad_side,
        grad_down.reshape(shards, -1, width),
    )
    params = (norm_gains, conv_taps, in_proj, out_proj, gate_up, down_proj)
    firsts = (first_gains, first_taps, first_in, first_out, first_gate_up, first_down)
    seconds = (second_gains, second_taps, second_in, second_out, second_gate_up, second_down)
    owned = (side_owned, in_owned, gate_owned, down_owned)
    results = adamw(owned, params, firsts, seconds)
    out_rows = block_out.reshape(row_count, length, width)
    grad_rows = grad_hidden.reshape(row_count, length, width)
    return (
        out_rows,
        grad_rows,
        *results,
    )


def solution(mesh):
    tokens, depth = mesh.devices.shape
    chip_mesh = Mesh(mesh.devices.reshape(tokens // 2, 2, depth), ALL)
    in_specs = (
        P("fsdp", SEQ, None),
        P("fsdp", SEQ, None),
        P("fsdp", SEQ),
        P(None, ALL),
        P(None, ALL),
        P(ALL, None),
        P(ALL, None),
        P(ALL, None),
        P(ALL, None),
        P(None, ALL),
        P(None, ALL),
        P(ALL, None),
        P(ALL, None),
        P(ALL, None),
        P(ALL, None),
        P(None, ALL),
        P(None, ALL),
        P(ALL, None),
        P(ALL, None),
        P(ALL, None),
        P(ALL, None),
    )
    out_specs = (
        P("fsdp", SEQ, None),
        P("fsdp", SEQ, None),
        P(None, ALL),
        P(None, ALL),
        P(ALL, None),
        P(ALL, None),
        P(ALL, None),
        P(ALL, None),
        P(None, ALL),
        P(None, ALL),
        P(ALL, None),
        P(ALL, None),
        P(ALL, None),
        P(ALL, None),
        P(None, ALL),
        P(None, ALL),
        P(ALL, None),
        P(ALL, None),
        P(ALL, None),
        P(ALL, None),
        P(None, ALL),
        P(None, ALL),
        P(ALL, None),
        P(ALL, None),
        P(ALL, None),
        P(ALL, None),
    )
    return jax.shard_map(local, mesh=chip_mesh, in_specs=in_specs, out_specs=out_specs, check_vma=False)
```

```python
import functools

import jax
import jax.numpy as jnp
from jax import lax
from jax.experimental import pallas as pl
from jax.experimental.pallas import tpu as pltpu
from jax.sharding import Mesh
from jax.sharding import PartitionSpec as P

STEP = 3


NORM_EPS = 1e-05
BETA_ONE = 0.9
BETA_TWO = 0.999
ADAM_EPS = 1e-08
RATE_MATRIX = 0.005
RATE_VECTOR = 0.2
DECAY = 0.1
LANES = 128
VMEM_SCATTER = 46 << 20
VMEM_GATHER = 60 << 20
UNIT_TILE = 512
MESH_ID = pl.DeviceIdType.MESH
SEQ = ("ring", "core")
ALL = ("ring", "core", "fsdp")


def snake(index):
    return 2 * (index // 2) + (index % 2 + index // 2) % 2


def halves(columns):
    first = (columns // 2 + LANES - 1) // LANES * LANES
    return (pl.ds(0, first), pl.ds(first, columns - first))


class Place:
    def __init__(self, chips, depth):
        self.chips, self.depth = chips, depth
        self.core = lax.axis_index("core")
        self.layer = lax.axis_index("fsdp")
        self.spot = snake(lax.axis_index("ring"))
        self.own = lax.axis_index("ring")
        self.right = self.device(snake((self.spot + 1) % chips), self.core, self.layer)
        self.left = self.device(snake((self.spot + chips - 1) % chips), self.core, self.layer)
        self.up = self.device(self.own, self.core, (self.layer + 1) % depth)
        self.down = self.device(self.own, self.core, (self.layer + depth - 1) % depth)
        self.sibling = self.device(self.own, 1 - self.core, self.layer)

    def device(self, ring, core, layer):
        return (ring, core, layer)

    def shard(self, spot, core, layer):
        return (snake(spot) * 2 + core) * self.depth + layer

    def greet(self):
        for device in (self.right, self.left, self.up, self.down, self.sibling):
            pl.semaphore_signal(
                pltpu.get_barrier_semaphore(), inc=1, device_id=device, device_id_type=MESH_ID
            )

    def await_greetings(self):
        pl.semaphore_wait(pltpu.get_barrier_semaphore(), 5)


def gather_kernel(chips, depth, groups, *refs):
    count, inputs = len(groups), sum(groups)
    wholes = refs[inputs : inputs + count]
    shards = refs[inputs + count : inputs + 2 * count]
    wide = refs[inputs + 2 * count : 2 * inputs + 2 * count]
    loaded, sent, from_sibling, from_below, from_ring, kept, late_ring, late_below = refs[
        2 * inputs + 2 * count :
    ]
    loads = [
        pltpu.make_async_copy(refs[index], wide[index], loaded.at[index])
        for index in range(inputs)
    ]
    for load in loads:
        load.start()
    here = Place(chips, depth)
    here.greet()
    for load in loads:
        load.wait()
    taken = 0
    for shard, members in zip(shards, groups):
        start = 0
        for member in wide[taken : taken + members]:
            shard[:, start : start + member.shape[1]] = member[...].astype(shard.dtype)
            start += member.shape[1]
        taken += members
    here.await_greetings()
    late = count - 1
    cuts = [halves(ref.shape[1]) for ref in shards]

    def block(which, shard):
        return wholes[which].at[shard]

    def piece_of(which, shard, way):
        return wholes[which].at[shard, :, cuts[which][way]]

    def send(source, target, which, arrived, device):
        pltpu.make_async_remote_copy(
            src_ref=source,
            dst_ref=target,
            send_sem=sent.at[which],
            recv_sem=arrived,
            device_id=device,
            device_id_type=MESH_ID,
        ).start()

    def awaited(ref, arrived):
        pltpu.make_async_copy(ref, ref, arrived).wait()

    own = here.shard(here.spot, here.core, here.layer)
    for which in range(late):
        send(shards[which], block(which, own), which, from_below.at[which, 0], here.up)
        for way in range(2):
            send(
                shards[which].at[:, cuts[which][way]],
                piece_of(which, own, way),
                which,
                from_ring.at[which, way, 0],
                (here.right, here.left)[way],
            )
    for way in range(2):
        part = shards[late].at[:, cuts[late][way]]
        piece = piece_of(late, own, way)
        send(part, piece, late, late_ring.at[way, 0], (here.right, here.left)[way])
        send(part, piece, late, late_below.at[way, 0], here.up)
    for which in range(count):
        send(shards[which], block(which, own), which, from_sibling.at[which], here.sibling)
        pltpu.make_async_copy(shards[which], block(which, own), kept.at[which]).start()

    def late_around(hop):
        for way in range(2):
            away = (chips - hop, hop)[way]
            piece = piece_of(late, here.shard((here.spot + away) % chips, here.core, here.layer), way)
            awaited(piece, late_ring.at[way, hop - 1])
            if hop < chips - 1:
                send(piece, piece, late, late_ring.at[way, hop], (here.right, here.left)[way])
            send(piece, piece, late, late_below.at[way, hop], here.up)
            send(piece, piece, late, from_sibling.at[late], here.sibling)

    def late_layer(layer_step, hop):
        layer = (here.layer + depth - layer_step) % depth
        for way in range(2):
            away = (chips - hop, hop)[way]
            piece = piece_of(late, here.shard((here.spot + away) % chips, here.core, layer), way)
            awaited(piece, late_below.at[way, (layer_step - 1) * chips + hop])

            @pl.when(layer_step < depth - 1)
            def _():
                send(piece, piece, late, late_below.at[way, layer_step * chips + hop], here.up)

            send(piece, piece, late, from_sibling.at[late], here.sibling)

    def late_step(layer_step, hop):
        if hop > 0:
            @pl.when(layer_step == 0)
            def _():
                late_around(hop)

        @pl.when(layer_step > 0)
        def _():
            late_layer(layer_step, hop)

    def around(hop, layer_step):
        layer = (here.layer + depth - layer_step) % depth
        for which in range(late):
            for way in range(2):
                away = (chips - hop, hop)[way]
                shard = here.shard((here.spot + away) % chips, here.core, layer)
                arrived = layer_step * (chips - 1) + hop - 1
                piece = piece_of(which, shard, way)
                awaited(piece, from_ring.at[which, way, arrived])
                if hop < chips - 1:
                    send(
                        piece,
                        piece,
                        which,
                        from_ring.at[which, way, arrived + 1],
                        (here.right, here.left)[way],
                    )
                send(piece, piece, which, from_sibling.at[which], here.sibling)

    def layer_arrives(layer_step):
        layer = (here.layer + depth - layer_step) % depth
        shard = here.shard(here.spot, here.core, layer)
        for which in range(late):
            whole = block(which, shard)
            awaited(whole, from_below.at[which, layer_step - 1])

            @pl.when(layer_step < depth - 1)
            def _():
                send(whole, whole, which, from_below.at[which, layer_step], here.up)

            for way in range(2):
                piece = piece_of(which, shard, way)
                send(
                    piece,
                    piece,
                    which,
                    from_ring.at[which, way, layer_step * (chips - 1)],
                    (here.right, here.left)[way],
                )
            send(whole, whole, which, from_sibling.at[which], here.sibling)

    @pl.loop(0, depth)
    def _(layer_step):
        late_step(layer_step, 0)
        for hop in range(1, chips - 1):
            around(hop, layer_step)
            late_step(layer_step, hop)

        @pl.when(layer_step < depth - 1)
        def _():
            layer_arrives(layer_step + 1)

        around(chips - 1, layer_step)
        late_step(layer_step, chips - 1)

    shard_count = 2 * chips * depth
    for which in range(count):
        pltpu.make_async_copy(shards[which], block(which, own), kept.at[which]).wait()
        awaited(wholes[which].at[pl.ds(0, shard_count // 2)], from_sibling.at[which])
        awaited(wholes[which].at[pl.ds(0, shard_count - 1)], sent.at[which])


def gather(chips, depth, *groups):
    count = len(groups)
    steps = depth * (chips - 1)
    shard_count = 2 * chips * depth
    shapes = [(g[0].shape[0], sum(x.shape[1] for x in g)) for g in groups]
    half = jnp.bfloat16
    return pl.pallas_call(
        functools.partial(gather_kernel, chips, depth, [len(g) for g in groups]),
        out_shape=[jax.ShapeDtypeStruct((shard_count,) + shape, half) for shape in shapes],
        in_specs=[pl.BlockSpec(memory_space=pl.ANY)] * sum(len(g) for g in groups),
        out_specs=[pl.BlockSpec(memory_space=pl.ANY)] * count,
        scratch_shapes=[pltpu.VMEM(shape, half) for shape in shapes]
        + [pltpu.VMEM(x.shape, x.dtype) for g in groups for x in g]
        + [
            pltpu.SemaphoreType.DMA((sum(len(g) for g in groups),)),
            pltpu.SemaphoreType.DMA((count,)),
            pltpu.SemaphoreType.DMA((count,)),
            pltpu.SemaphoreType.DMA((count, depth - 1)),
            pltpu.SemaphoreType.DMA((count, 2, steps)),
            pltpu.SemaphoreType.DMA((count,)),
            pltpu.SemaphoreType.DMA((2, chips - 1)),
            pltpu.SemaphoreType.DMA((2, chips * (depth - 1))),
        ],
        compiler_params=pltpu.CompilerParams(
            collective_id=0, has_side_effects=True, vmem_limit_bytes=VMEM_GATHER
        ),
        name="gather_weights",
    )(*[x for g in groups for x in g])


def scatter_kernel(chips, depth, count, *refs):
    grads = refs[:count]
    owned = refs[count : 2 * count]
    rest = refs[2 * count :]
    theirs = rest[:count]
    staged = rest[count : 2 * count]
    ringed = rest[2 * count : 3 * count]
    layered = rest[3 * count : 4 * count]
    sent, loaded, from_sibling, from_below, from_ring, late_below = rest[4 * count :]
    here = Place(chips, depth)
    late = count - 1
    cuts = [halves(ref.shape[1]) for ref in owned]
    f32 = jnp.float32

    def part(which, shard, way):
        if len(grads[which].shape) == 4:
            return grads[which].at[way, shard]
        return grads[which].at[shard, :, cuts[which][way]]

    def place(hop, way):
        away = (chips - hop, hop)[way]
        return (here.spot + away) % chips

    def layer_of(layer_step):
        return (here.layer + 2 * depth - 1 - layer_step) % depth

    def slot_of(layer_step, hop):
        return layer_step * chips + hop - 1

    def load(which, layer_step, hop, start):
        for way, cut in enumerate(cuts[which]):
            shard = here.shard(place(hop, way), here.core, layer_of(layer_step))
            copy = pltpu.make_async_copy(
                part(which, shard, way),
                staged[which].at[hop - 1, :, cut],
                loaded.at[which, way, hop - 1],
            )
            copy.start() if start else copy.wait()

    def hand_over(which, slot):
        layer_step = slot // chips
        hop = slot % chips + 1
        for way, cut in enumerate(cuts[which]):
            shard = here.shard(place(hop, way), 1 - here.core, layer_of(layer_step))
            pltpu.make_async_remote_copy(
                src_ref=part(which, shard, way),
                dst_ref=theirs[which].at[slot, :, cut],
                send_sem=sent.at[which],
                recv_sem=from_sibling.at[which, way, slot],
                device_id=here.sibling,
                device_id_type=MESH_ID,
            ).start()

    slots = chips * depth
    for hop in range(1, chips + 1):
        for which in range(count):
            load(which, 0, hop, True)
    here.greet()
    here.await_greetings()

    @pl.loop(0, slots)
    def _(slot):
        for which in range(count):
            hand_over(which, slot)

    def got(ref, semaphore):
        pltpu.make_async_copy(ref, ref, semaphore).wait()

    def step(layer_step, hop):
        slot = slot_of(layer_step, hop)
        for which in range(late):
            load(which, layer_step, hop, False)
            if hop == chips:
                @pl.when(layer_step > 0)
                def _():
                    ref = layered[which].at[layer_step - 1]
                    got(ref, from_below.at[which, layer_step - 1])

            for way, cut in enumerate(cuts[which]):
                mine = theirs[which].at[slot, :, cut]
                got(mine, from_sibling.at[which, way, slot])
                total = mine[...].astype(f32) + staged[which][hop - 1, :, cut].astype(f32)
                if hop > 1:
                    index = layer_step * (chips - 1) + hop - 2
                    arrived = ringed[which].at[index, :, cut]
                    got(arrived, from_ring.at[which, way, index])
                    total = total + arrived[...].astype(f32)
                if hop < chips:
                    index = layer_step * (chips - 1) + hop - 1
                    mine[...] = total.astype(mine.dtype)
                    pltpu.make_async_remote_copy(
                        src_ref=mine,
                        dst_ref=ringed[which].at[index, :, cut],
                        send_sem=sent.at[which],
                        recv_sem=from_ring.at[which, way, index],
                        device_id=(here.right, here.left)[way],
                        device_id_type=MESH_ID,
                    ).start()
                else:
                    owned[which][:, cut] = total

            if hop == chips:
                @pl.when(layer_step > 0)
                def _():
                    owned[which][...] += layered[which][layer_step - 1].astype(f32)

                @pl.when(layer_step < depth - 1)
                def _():
                    mine = theirs[which].at[slot]
                    mine[...] = owned[which][...].astype(mine.dtype)
                    pltpu.make_async_remote_copy(
                        src_ref=mine,
                        dst_ref=layered[which].at[layer_step],
                        send_sem=sent.at[which],
                        recv_sem=from_below.at[which, layer_step],
                        device_id=here.up,
                        device_id_type=MESH_ID,
                    ).start()

        @pl.when(layer_step < depth - 1)
        def _():
            for which in range(late):
                load(which, layer_step + 1, hop, True)

    def late_step(layer_step, hop):
        slot = slot_of(layer_step, hop)
        load(late, layer_step, hop, False)
        for way, cut in enumerate(cuts[late]):
            mine = theirs[late].at[slot, :, cut]
            got(mine, from_sibling.at[late, way, slot])
            total = mine[...].astype(f32) + staged[late][hop - 1, :, cut].astype(f32)
            mine[...] = total.astype(mine.dtype)

            @pl.when(layer_step > 0)
            def _():
                before = slot_of(layer_step - 1, hop)
                arrived = layered[late].at[before, :, cut]
                got(arrived, late_below.at[way, before])
                both = total + arrived[...].astype(f32)
                mine[...] = both.astype(mine.dtype)

            @pl.when(layer_step < depth - 1)
            def _():
                pltpu.make_async_remote_copy(
                    src_ref=mine,
                    dst_ref=layered[late].at[slot, :, cut],
                    send_sem=sent.at[late],
                    recv_sem=late_below.at[way, slot],
                    device_id=here.up,
                    device_id_type=MESH_ID,
                ).start()

            @pl.when(layer_step == depth - 1)
            def _():
                around = mine[...].astype(f32)
                if hop > 1:
                    arrived = ringed[late].at[hop - 2, :, cut]
                    got(arrived, from_ring.at[late, way, hop - 2])
                    around = around + arrived[...].astype(f32)
                if hop < chips:
                    mine[...] = around.astype(mine.dtype)
                    pltpu.make_async_remote_copy(
                        src_ref=mine,
                        dst_ref=ringed[late].at[hop - 1, :, cut],
                        send_sem=sent.at[late],
                        recv_sem=from_ring.at[late, way, hop - 1],
                        device_id=(here.right, here.left)[way],
                        device_id_type=MESH_ID,
                    ).start()
                else:
                    owned[late][:, cut] = around

        @pl.when(layer_step < depth - 1)
        def _():
            load(late, layer_step + 1, hop, True)

    for place_in_line in range(1, chips - 1):
        for layer_step in range(min(place_in_line, depth)):
            step(layer_step, place_in_line - layer_step)

    @pl.loop(0, depth)
    def _(layer_step):
        for hop in range(chips - 1, 0, -1):
            late_step(layer_step, chips - hop)
            ahead = chips - 1 - hop

            @pl.when(layer_step + ahead < depth)
            def _():
                step(layer_step + ahead, hop)

        late_step(layer_step, chips)
        step(layer_step, chips)

    for which in range(count):
        some = pl.ds(0, 2 * slots - 1)
        most = grads[which].at[:, some] if len(grads[which].shape) == 4 else grads[which].at[some]
        pltpu.make_async_copy(most, most, sent.at[which]).wait()


def scatter(chips, depth, *grads):
    count = len(grads)
    slots = chips * depth
    steps = depth * (chips - 1)
    shapes = [
        (g.shape[1], g.shape[2]) if g.ndim == 3 else (g.shape[2], 2 * g.shape[3]) for g in grads
    ]
    anywhere = pl.BlockSpec(memory_space=pl.ANY)
    inner = pl.BlockSpec(memory_space=pltpu.VMEM)

    def room(most, last):
        leading = [most] * (count - 1) + [last]
        return [pltpu.VMEM((n,) + x, jnp.bfloat16) for n, x in zip(leading, shapes)]

    return pl.pallas_call(
        functools.partial(scatter_kernel, chips, depth, count),
        out_shape=[jax.ShapeDtypeStruct(x, jnp.float32) for x in shapes],
        in_specs=[anywhere] * count,
        out_specs=[inner] * count,
        scratch_shapes=room(slots, slots)
        + room(chips, chips)
        + room(steps, chips - 1)
        + room(depth - 1, chips * (depth - 1))
        + [
            pltpu.SemaphoreType.DMA((count,)),
            pltpu.SemaphoreType.DMA((count, 2, chips)),
            pltpu.SemaphoreType.DMA((count, 2, slots)),
            pltpu.SemaphoreType.DMA((count, depth - 1)),
            pltpu.SemaphoreType.DMA((count, 2, steps)),
            pltpu.SemaphoreType.DMA((2, chips * (depth - 1))),
        ],
        compiler_params=pltpu.CompilerParams(
            collective_id=1, has_side_effects=True, vmem_limit_bytes=VMEM_SCATTER
        ),
        name="scatter_gradients",
    )(*grads)


def from_behind(value, axis, steps):
    count = lax.axis_size(axis)
    first, last = (max(0, -steps), min(count, count - steps))
    return lax.ppermute(value, axis, [(source, source + steps) for source in range(first, last)])


def matmul(left, right):
    return jnp.dot(left, right, preferred_element_type=jnp.float32)


def matmul_tn(left, right):
    return lax.dot_general(
        left, right, (((0,), (0,)), ((), ())), preferred_element_type=jnp.float32
    )


def matmul_nt(left, right):
    return lax.dot_general(
        left, right, (((1,), (1,)), ((), ())), preferred_element_type=jnp.float32
    )


def inverse_rms(values):
    return lax.rsqrt(jnp.mean(values * values, axis=-1, keepdims=True) + NORM_EPS)


def norm_backward(values, scale, gain, grad_normed):
    weighted = grad_normed * gain
    grad_gain = jnp.sum(grad_normed * values * scale, axis=0)
    cubed = scale * scale * scale
    grad_values = scale * weighted - values * cubed * jnp.mean(
        weighted * values, axis=-1, keepdims=True
    )
    return (grad_values, grad_gain)


def adamw_update(param, grad, first, second, rate, decay):
    first_new = BETA_ONE * first + (1.0 - BETA_ONE) * grad
    second_new = BETA_TWO * second + (1.0 - BETA_TWO) * grad * grad
    first_hat = first_new / (1.0 - BETA_ONE**STEP)
    second_hat = second_new / (1.0 - BETA_TWO**STEP)
    param_new = param - rate * (first_hat / (jnp.sqrt(second_hat) + ADAM_EPS) + decay * param)
    return (param_new, first_new, second_new)


def adamw_kernel(*refs):
    grads, state, outs = refs[:4], refs[4:22], refs[22:]
    side, lanes, width = grads[0], outs[0].shape[1], outs[3].shape[1]
    vectors = side[:8, width:]
    found = [vectors[:2, :lanes], vectors[2:5, :lanes], grads[1][...], side[:, :width]]
    found += [ref[...] for ref in grads[2:]]
    for index, grad in enumerate(found):
        rate, decay = (RATE_VECTOR, 0.0) if index < 2 else (RATE_MATRIX, DECAY)
        param, first, second = (state[6 * kind + index][...] for kind in range(3))
        new = adamw_update(param, grad, first, second, rate, decay)
        for kind, value in enumerate((grad,) + new):
            outs[6 * kind + index][...] = value


def adamw(grads, params, firsts, seconds):
    inner = pl.BlockSpec(memory_space=pltpu.VMEM)
    return pl.pallas_call(
        adamw_kernel,
        out_shape=[jax.ShapeDtypeStruct(p.shape, p.dtype) for p in params] * 4,
        in_specs=[inner] * 22,
        out_specs=[inner] * 24,
        compiler_params=pltpu.CompilerParams(vmem_limit_bytes=48 << 20),
        name="adamw",
    )(*grads, *params, *firsts, *seconds)


def feed_forward_kernel(
    normed, turned, resid, cot, gate, up, down, out, grad_normed, grad_down, grad_gate_up
):
    half = jnp.bfloat16

    @pl.when(pl.program_id(0) == 0)
    def _():
        out[...] = resid[...]
        grad_normed[...] = jnp.zeros_like(grad_normed)

    gate_pre = matmul(normed[...], gate[...])
    up_pre = matmul(normed[...], up[...])
    grad_act = matmul_nt(cot[...], down[...])
    sigmoid_gate = jax.nn.sigmoid(gate_pre)
    silu_gate = gate_pre * sigmoid_gate
    act = (silu_gate * up_pre).astype(half)
    grad_gate = grad_act * up_pre * sigmoid_gate * (1.0 + gate_pre * (1.0 - sigmoid_gate))
    grad_gate = grad_gate.astype(half)
    grad_up = (grad_act * silu_gate).astype(half)
    out[...] += matmul(act, down[...])
    grad_normed[...] += matmul_nt(grad_gate, gate[...]) + matmul_nt(grad_up, up[...])
    grad_down[...] = matmul_tn(act, cot[...]).astype(half)
    grad_gate_up[0] = matmul(turned[...], grad_gate).astype(half)
    grad_gate_up[1] = matmul(turned[...], grad_up).astype(half)


def feed_forward(normed, resid, cot, packed, down):
    tokens, width = normed.shape
    units = down.shape[0]
    tile = UNIT_TILE
    tiles = units // tile
    half, single = jnp.bfloat16, jnp.float32

    def fixed(rows, columns):
        return pl.BlockSpec((rows, columns), lambda i: (0, 0))

    flops = 2 * tokens * width * units * 9
    return pl.pallas_call(
        feed_forward_kernel,
        grid=(tiles,),
        out_shape=[
            jax.ShapeDtypeStruct((tokens, width), single),
            jax.ShapeDtypeStruct((tokens, width), single),
            jax.ShapeDtypeStruct((units, width), half),
            jax.ShapeDtypeStruct((2, width, units), half),
        ],
        in_specs=[
            fixed(tokens, width),
            fixed(width, tokens),
            fixed(tokens, width),
            fixed(tokens, width),
            pl.BlockSpec((width, tile), lambda i: (0, i)),
            pl.BlockSpec((width, tile), lambda i: (0, i + tiles)),
            pl.BlockSpec((tile, width), lambda i: (i, 0)),
        ],
        out_specs=[
            fixed(tokens, width),
            fixed(tokens, width),
            pl.BlockSpec((tile, width), lambda i: (i, 0)),
            pl.BlockSpec((2, width, tile), lambda i: (0, 0, i)),
        ],
        compiler_params=pltpu.CompilerParams(vmem_limit_bytes=48 << 20),
        cost_estimate=pl.CostEstimate(
            flops=flops, bytes_accessed=12 * width * units, transcendentals=tokens * units
        ),
        name="feed_forward",
    )(normed, normed.T, resid, cot, packed, packed, down)


def local(
    hidden_in,
    cotangent,
    doc_position,
    norm_gains,
    conv_taps,
    in_proj,
    out_proj,
    gate_up,
    down_proj,
    first_gains,
    first_taps,
    first_in,
    first_out,
    first_gate_up,
    first_down,
    second_gains,
    second_taps,
    second_in,
    second_out,
    second_gate_up,
    second_down,
):
    half = jnp.bfloat16
    single = jnp.float32
    row_count, length, width = hidden_in.shape
    tok_count = row_count * length
    chips, depth = lax.axis_size("ring"), lax.axis_size("fsdp")
    in_width = in_proj.shape[1]
    out_width = out_proj.shape[1]
    rows, unit_columns = gate_up.shape
    shards = 2 * chips * depth
    vectors = jnp.concatenate([norm_gains, conv_taps], axis=0)
    vector_count, lanes = vectors.shape
    corner = ((0, rows - vector_count), (0, LANES - lanes))
    packed_shards, down_shards = gather(
        chips, depth, (gate_up, in_proj, out_proj, jnp.pad(vectors, corner)), (down_proj,)
    )
    packed_full = packed_shards.reshape(width, -1)
    down_full = down_shards.reshape(-1, width)
    out_start = unit_columns + in_width
    in_full = packed_full[:, unit_columns:out_start]
    out_full = packed_full[:, out_start : out_start + out_width]
    vectors_full = packed_shards[:, :vector_count, -LANES:][:, :, :lanes].astype(single)
    vectors_full = vectors_full.transpose(1, 0, 2).reshape(vector_count, width)
    mixer_full = (None, None, in_full, out_full)
    gains_f = vectors_full[:2]
    taps_f = vectors_full[2:5]
    resid_one = hidden_in.reshape(tok_count, width).astype(single)
    scale_one = inverse_rms(resid_one)
    normed_one = (resid_one * scale_one * gains_f[0]).astype(half)
    projected = matmul(normed_one, mixer_full[2])
    b_branch = projected[:, :width]
    c_branch = projected[:, width : 2 * width]
    x_branch = projected[:, 2 * width :]
    gated_input = (b_branch * x_branch).astype(half)
    gated_rows = gated_input.reshape(row_count, length, width)
    carried = from_behind(gated_rows[:, length - 2 :, :], SEQ, 1)
    extended = jnp.concatenate([carried, gated_rows], axis=1).astype(single)
    gated_f = extended[:, 2:].reshape(tok_count, width)
    prev_one = extended[:, 1 : length + 1].reshape(tok_count, width)
    prev_two = extended[:, :length].reshape(tok_count, width)
    positions = doc_position.reshape(tok_count)
    mask_one = (positions >= 1).astype(single)[:, None]
    mask_two = (positions >= 2).astype(single)[:, None]
    conv_out = (
        taps_f[0] * gated_f + mask_one * taps_f[1] * prev_one + mask_two * taps_f[2] * prev_two
    )
    mixer_act = (c_branch * conv_out).astype(half)
    resid_two = resid_one + matmul(mixer_act, mixer_full[3])
    scale_two = inverse_rms(resid_two)
    normed_two = (resid_two * scale_two * gains_f[1]).astype(half)
    cot_rows = cotangent.reshape(tok_count, width)
    block_out, grad_normed, grad_down, grad_gate_up = feed_forward(
        normed_two, resid_two, cot_rows, packed_full, down_full
    )
    norm_part, gain_two_grad = norm_backward(resid_two, scale_two, gains_f[1], grad_normed)
    grad_resid = cot_rows.astype(single) + norm_part
    resid_cast = grad_resid.astype(half)
    grad_mixer = matmul_nt(resid_cast, mixer_full[3])
    grad_cbranch = grad_mixer * conv_out
    grad_conv = grad_mixer * c_branch
    masked_one = mask_one * grad_conv
    masked_two = mask_two * grad_conv
    grad_taps = jnp.stack(
        [
            jnp.sum(grad_conv * gated_f, axis=0),
            jnp.sum(masked_one * prev_one, axis=0),
            jnp.sum(masked_two * prev_two, axis=0),
        ]
    )
    one_rows = masked_one.reshape(row_count, length, width)
    two_rows = masked_two.reshape(row_count, length, width)
    leading = from_behind((one_rows[:, :2, :], two_rows[:, :2, :]), SEQ, -1)
    ext_one = jnp.concatenate([one_rows, leading[0]], axis=1)
    ext_two = jnp.concatenate([two_rows, leading[1]], axis=1)
    next_one = ext_one[:, 1 : length + 1].reshape(tok_count, width)
    next_two = ext_two[:, 2 : length + 2].reshape(tok_count, width)
    grad_gated = taps_f[0] * grad_conv + taps_f[1] * next_one + taps_f[2] * next_two
    grad_proj = jnp.concatenate(
        [grad_gated * x_branch, grad_cbranch, grad_gated * b_branch], axis=1
    ).astype(half)
    grad_normone = matmul_nt(grad_proj, mixer_full[2])
    first_part, gain_one_grad = norm_backward(resid_one, scale_one, gains_f[0], grad_normone)
    grad_hidden = grad_resid + first_part
    grad_gains = jnp.stack([gain_one_grad, gain_two_grad])
    grad_in = matmul_tn(normed_one, grad_proj)
    grad_out = matmul_tn(mixer_act, resid_cast)
    vector_grads = jnp.concatenate([grad_gains, grad_taps], axis=0)
    vector_shards = vector_grads.reshape(vector_count, shards, lanes).transpose(1, 0, 2)
    vector_shards = jnp.pad(vector_shards.astype(half), ((0, 0),) + corner)
    grad_side = jnp.concatenate(
        [grad_out.astype(half).reshape(shards, rows, out_width), vector_shards], axis=2
    )
    gate_owned, in_owned, side_owned, down_owned = scatter(
        chips,
        depth,
        grad_gate_up.reshape(2, shards, rows, -1),
        grad_in.astype(half).reshape(shards, rows, in_width),
        grad_side,
        grad_down.reshape(shards, -1, width),
    )
    params = (norm_gains, conv_taps, in_proj, out_proj, gate_up, down_proj)
    firsts = (first_gains, first_taps, first_in, first_out, first_gate_up, first_down)
    seconds = (second_gains, second_taps, second_in, second_out, second_gate_up, second_down)
    owned = (side_owned, in_owned, gate_owned, down_owned)
    results = adamw(owned, params, firsts, seconds)
    out_rows = block_out.reshape(row_count, length, width)
    grad_rows = grad_hidden.reshape(row_count, length, width)
    return (
        out_rows,
        grad_rows,
        *results,
    )


def solution(mesh):
    tokens, depth = mesh.devices.shape
    chip_mesh = Mesh(mesh.devices.reshape(tokens // 2, 2, depth), ALL)
    in_specs = (
        P("fsdp", SEQ, None),
        P("fsdp", SEQ, None),
        P("fsdp", SEQ),
        P(None, ALL),
        P(None, ALL),
        P(ALL, None),
        P(ALL, None),
        P(ALL, None),
        P(ALL, None),
        P(None, ALL),
        P(None, ALL),
        P(ALL, None),
        P(ALL, None),
        P(ALL, None),
        P(ALL, None),
        P(None, ALL),
        P(None, ALL),
        P(ALL, None),
        P(ALL, None),
        P(ALL, None),
        P(ALL, None),
    )
    out_specs = (
        P("fsdp", SEQ, None),
        P("fsdp", SEQ, None),
        P(None, ALL),
        P(None, ALL),
        P(ALL, None),
        P(ALL, None),
        P(ALL, None),
        P(ALL, None),
        P(None, ALL),
        P(None, ALL),
        P(ALL, None),
        P(ALL, None),
        P(ALL, None),
        P(ALL, None),
        P(None, ALL),
        P(None, ALL),
        P(ALL, None),
        P(ALL, None),
        P(ALL, None),
        P(ALL, None),
        P(None, ALL),
        P(None, ALL),
        P(ALL, None),
        P(ALL, None),
        P(ALL, None),
        P(ALL, None),
    )
    return jax.shard_map(local, mesh=chip_mesh, in_specs=in_specs, out_specs=out_specs, check_vma=False)
```

```python
import functools

import jax
import jax.numpy as jnp
from jax import lax
from jax.experimental import pallas as pl
from jax.experimental.pallas import tpu as pltpu
from jax.sharding import Mesh
from jax.sharding import PartitionSpec as P

STEP = 3


NORM_EPS = 1e-05
BETA_ONE = 0.9
BETA_TWO = 0.999
ADAM_EPS = 1e-08
RATE_MATRIX = 0.005
RATE_VECTOR = 0.2
DECAY = 0.1
LANES = 128
VMEM_SCATTER = 46 << 20
VMEM_GATHER = 60 << 20
UNIT_TILE = 512
MESH_ID = pl.DeviceIdType.MESH
SEQ = ("ring", "core")
ALL = ("ring", "core", "fsdp")


def snake(index):
    return 2 * (index // 2) + (index % 2 + index // 2) % 2


def halves(columns):
    first = (columns // 2 + LANES - 1) // LANES * LANES
    return (pl.ds(0, first), pl.ds(first, columns - first))


class Place:
    def __init__(self, chips, depth):
        self.chips, self.depth = chips, depth
        self.core = lax.axis_index("core")
        self.layer = lax.axis_index("fsdp")
        self.spot = snake(lax.axis_index("ring"))
        self.own = lax.axis_index("ring")
        self.right = self.device(snake((self.spot + 1) % chips), self.core, self.layer)
        self.left = self.device(snake((self.spot + chips - 1) % chips), self.core, self.layer)
        self.up = self.device(self.own, self.core, (self.layer + 1) % depth)
        self.down = self.device(self.own, self.core, (self.layer + depth - 1) % depth)
        self.sibling = self.device(self.own, 1 - self.core, self.layer)

    def device(self, ring, core, layer):
        return (ring, core, layer)

    def shard(self, spot, core, layer):
        return (snake(spot) * 2 + core) * self.depth + layer

    def greet(self):
        for device in (self.right, self.left, self.up, self.down, self.sibling):
            pl.semaphore_signal(
                pltpu.get_barrier_semaphore(), inc=1, device_id=device, device_id_type=MESH_ID
            )

    def await_greetings(self):
        pl.semaphore_wait(pltpu.get_barrier_semaphore(), 5)


def gather_kernel(chips, depth, groups, *refs):
    count, inputs = len(groups), sum(groups)
    wholes = refs[inputs : inputs + count]
    shards = refs[inputs + count : inputs + 2 * count]
    wide = refs[inputs + 2 * count : 2 * inputs + 2 * count]
    loaded, sent, from_sibling, from_below, from_ring, kept, late_ring, late_below = refs[
        2 * inputs + 2 * count :
    ]
    loads = [
        pltpu.make_async_copy(refs[index], wide[index], loaded.at[index])
        for index in range(inputs)
    ]
    for load in loads:
        load.start()
    here = Place(chips, depth)
    here.greet()
    for load in loads:
        load.wait()
    taken = 0
    for shard, members in zip(shards, groups):
        start = 0
        for member in wide[taken : taken + members]:
            shard[:, start : start + member.shape[1]] = member[...].astype(shard.dtype)
            start += member.shape[1]
        taken += members
    here.await_greetings()
    late = count - 1
    cuts = [halves(ref.shape[1]) for ref in shards]

    def block(which, shard):
        return wholes[which].at[shard]

    def piece_of(which, shard, way):
        return wholes[which].at[shard, :, cuts[which][way]]

    def send(source, target, which, arrived, device):
        pltpu.make_async_remote_copy(
            src_ref=source,
            dst_ref=target,
            send_sem=sent.at[which],
            recv_sem=arrived,
            device_id=device,
            device_id_type=MESH_ID,
        ).start()

    def awaited(ref, arrived):
        pltpu.make_async_copy(ref, ref, arrived).wait()

    own = here.shard(here.spot, here.core, here.layer)
    for which in range(late):
        send(shards[which], block(which, own), which, from_below.at[which, 0], here.up)
        for way in range(2):
            send(
                shards[which].at[:, cuts[which][way]],
                piece_of(which, own, way),
                which,
                from_ring.at[which, way, 0],
                (here.right, here.left)[way],
            )
    for way in range(2):
        part = shards[late].at[:, cuts[late][way]]
        piece = piece_of(late, own, way)
        send(part, piece, late, late_ring.at[way, 0], (here.right, here.left)[way])
        send(part, piece, late, late_below.at[way, 0], here.up)
    for which in range(count):
        send(shards[which], block(which, own), which, from_sibling.at[which], here.sibling)
        pltpu.make_async_copy(shards[which], block(which, own), kept.at[which]).start()

    def late_around(hop):
        for way in range(2):
            away = (chips - hop, hop)[way]
            piece = piece_of(late, here.shard((here.spot + away) % chips, here.core, here.layer), way)
            awaited(piece, late_ring.at[way, hop - 1])
            if hop < chips - 1:
                send(piece, piece, late, late_ring.at[way, hop], (here.right, here.left)[way])
            send(piece, piece, late, late_below.at[way, hop], here.up)
            send(piece, piece, late, from_sibling.at[late], here.sibling)

    def late_layer(layer_step, hop):
        layer = (here.layer + depth - layer_step) % depth
        for way in range(2):
            away = (chips - hop, hop)[way]
            piece = piece_of(late, here.shard((here.spot + away) % chips, here.core, layer), way)
            awaited(piece, late_below.at[way, (layer_step - 1) * chips + hop])

            @pl.when(layer_step < depth - 1)
            def _():
                send(piece, piece, late, late_below.at[way, layer_step * chips + hop], here.up)

            send(piece, piece, late, from_sibling.at[late], here.sibling)

    def late_step(layer_step, hop):
        if hop > 0:
            @pl.when(layer_step == 0)
            def _():
                late_around(hop)

        @pl.when(layer_step > 0)
        def _():
            late_layer(layer_step, hop)

    def around(hop, layer_step):
        layer = (here.layer + depth - layer_step) % depth
        for which in range(late):
            for way in range(2):
                away = (chips - hop, hop)[way]
                shard = here.shard((here.spot + away) % chips, here.core, layer)
                arrived = layer_step * (chips - 1) + hop - 1
                piece = piece_of(which, shard, way)
                awaited(piece, from_ring.at[which, way, arrived])
                if hop < chips - 1:
                    send(
                        piece,
                        piece,
                        which,
                        from_ring.at[which, way, arrived + 1],
                        (here.right, here.left)[way],
                    )
                send(piece, piece, which, from_sibling.at[which], here.sibling)

    def layer_arrives(layer_step):
        layer = (here.layer + depth - layer_step) % depth
        shard = here.shard(here.spot, here.core, layer)
        for which in range(late):
            whole = block(which, shard)
            awaited(whole, from_below.at[which, layer_step - 1])

            @pl.when(layer_step < depth - 1)
            def _():
                send(whole, whole, which, from_below.at[which, layer_step], here.up)

            for way in range(2):
                piece = piece_of(which, shard, way)
                send(
                    piece,
                    piece,
                    which,
                    from_ring.at[which, way, layer_step * (chips - 1)],
                    (here.right, here.left)[way],
                )
            send(whole, whole, which, from_sibling.at[which], here.sibling)

    @pl.loop(0, depth)
    def _(layer_step):
        late_step(layer_step, 0)
        for hop in range(1, chips - 1):
            around(hop, layer_step)
            late_step(layer_step, hop)

        @pl.when(layer_step < depth - 1)
        def _():
            layer_arrives(layer_step + 1)

        around(chips - 1, layer_step)
        late_step(layer_step, chips - 1)

    shard_count = 2 * chips * depth
    for which in range(count):
        pltpu.make_async_copy(shards[which], block(which, own), kept.at[which]).wait()
        awaited(wholes[which].at[pl.ds(0, shard_count // 2)], from_sibling.at[which])
        awaited(wholes[which].at[pl.ds(0, shard_count - 1)], sent.at[which])


def gather(chips, depth, *groups):
    count = len(groups)
    steps = depth * (chips - 1)
    shard_count = 2 * chips * depth
    shapes = [(g[0].shape[0], sum(x.shape[1] for x in g)) for g in groups]
    half = jnp.bfloat16
    return pl.pallas_call(
        functools.partial(gather_kernel, chips, depth, [len(g) for g in groups]),
        out_shape=[jax.ShapeDtypeStruct((shard_count,) + shape, half) for shape in shapes],
        in_specs=[pl.BlockSpec(memory_space=pl.ANY)] * sum(len(g) for g in groups),
        out_specs=[pl.BlockSpec(memory_space=pl.ANY)] * count,
        scratch_shapes=[pltpu.VMEM(shape, half) for shape in shapes]
        + [pltpu.VMEM(x.shape, x.dtype) for g in groups for x in g]
        + [
            pltpu.SemaphoreType.DMA((sum(len(g) for g in groups),)),
            pltpu.SemaphoreType.DMA((count,)),
            pltpu.SemaphoreType.DMA((count,)),
            pltpu.SemaphoreType.DMA((count, depth - 1)),
            pltpu.SemaphoreType.DMA((count, 2, steps)),
            pltpu.SemaphoreType.DMA((count,)),
            pltpu.SemaphoreType.DMA((2, chips - 1)),
            pltpu.SemaphoreType.DMA((2, chips * (depth - 1))),
        ],
        compiler_params=pltpu.CompilerParams(
            collective_id=0, has_side_effects=True, vmem_limit_bytes=VMEM_GATHER
        ),
        name="gather_weights",
    )(*[x for g in groups for x in g])


def scatter_kernel(chips, depth, count, *refs):
    grads = refs[:count]
    owned = refs[count : 2 * count]
    rest = refs[2 * count :]
    theirs = rest[:count]
    staged = rest[count : 2 * count]
    ringed = rest[2 * count : 3 * count]
    layered = rest[3 * count : 4 * count]
    sent, loaded, from_sibling, from_below, from_ring, late_below = rest[4 * count :]
    here = Place(chips, depth)
    late = count - 1
    cuts = [halves(ref.shape[1]) for ref in owned]
    f32 = jnp.float32

    def part(which, shard, way):
        if len(grads[which].shape) == 4:
            return grads[which].at[way, shard]
        return grads[which].at[shard, :, cuts[which][way]]

    def place(hop, way):
        away = (chips - hop, hop)[way]
        return (here.spot + away) % chips

    def layer_of(layer_step):
        return (here.layer + 2 * depth - 1 - layer_step) % depth

    def slot_of(layer_step, hop):
        return layer_step * chips + hop - 1

    def load(which, layer_step, hop, start):
        for way, cut in enumerate(cuts[which]):
            shard = here.shard(place(hop, way), here.core, layer_of(layer_step))
            copy = pltpu.make_async_copy(
                part(which, shard, way),
                staged[which].at[hop - 1, :, cut],
                loaded.at[which, way, hop - 1],
            )
            copy.start() if start else copy.wait()

    def hand_over(which, slot):
        layer_step = slot // chips
        hop = slot % chips + 1
        for way, cut in enumerate(cuts[which]):
            shard = here.shard(place(hop, way), 1 - here.core, layer_of(layer_step))
            pltpu.make_async_remote_copy(
                src_ref=part(which, shard, way),
                dst_ref=theirs[which].at[slot, :, cut],
                send_sem=sent.at[which],
                recv_sem=from_sibling.at[which, way, slot],
                device_id=here.sibling,
                device_id_type=MESH_ID,
            ).start()

    slots = chips * depth
    for hop in range(1, chips + 1):
        for which in range(count):
            load(which, 0, hop, True)
    here.greet()
    here.await_greetings()

    @pl.loop(0, slots)
    def _(slot):
        for which in reversed(range(count)):
            hand_over(which, slot)

    def got(ref, semaphore):
        pltpu.make_async_copy(ref, ref, semaphore).wait()

    def step(layer_step, hop):
        slot = slot_of(layer_step, hop)
        for which in range(late):
            load(which, layer_step, hop, False)
            if hop == chips:
                @pl.when(layer_step > 0)
                def _():
                    ref = layered[which].at[layer_step - 1]
                    got(ref, from_below.at[which, layer_step - 1])

            for way, cut in enumerate(cuts[which]):
                mine = theirs[which].at[slot, :, cut]
                got(mine, from_sibling.at[which, way, slot])
                total = mine[...].astype(f32) + staged[which][hop - 1, :, cut].astype(f32)
                if hop > 1:
                    index = layer_step * (chips - 1) + hop - 2
                    arrived = ringed[which].at[index, :, cut]
                    got(arrived, from_ring.at[which, way, index])
                    total = total + arrived[...].astype(f32)
                if hop < chips:
                    index = layer_step * (chips - 1) + hop - 1
                    mine[...] = total.astype(mine.dtype)
                    pltpu.make_async_remote_copy(
                        src_ref=mine,
                        dst_ref=ringed[which].at[index, :, cut],
                        send_sem=sent.at[which],
                        recv_sem=from_ring.at[which, way, index],
                        device_id=(here.right, here.left)[way],
                        device_id_type=MESH_ID,
                    ).start()
                else:
                    owned[which][:, cut] = total

            if hop == chips:
                @pl.when(layer_step > 0)
                def _():
                    owned[which][...] += layered[which][layer_step - 1].astype(f32)

                @pl.when(layer_step < depth - 1)
                def _():
                    mine = theirs[which].at[slot]
                    mine[...] = owned[which][...].astype(mine.dtype)
                    pltpu.make_async_remote_copy(
                        src_ref=mine,
                        dst_ref=layered[which].at[layer_step],
                        send_sem=sent.at[which],
                        recv_sem=from_below.at[which, layer_step],
                        device_id=here.up,
                        device_id_type=MESH_ID,
                    ).start()

        @pl.when(layer_step < depth - 1)
        def _():
            for which in range(late):
                load(which, layer_step + 1, hop, True)

    def late_step(layer_step, hop):
        slot = slot_of(layer_step, hop)
        load(late, layer_step, hop, False)
        for way, cut in enumerate(cuts[late]):
            mine = theirs[late].at[slot, :, cut]
            got(mine, from_sibling.at[late, way, slot])
            total = mine[...].astype(f32) + staged[late][hop - 1, :, cut].astype(f32)
            mine[...] = total.astype(mine.dtype)

            @pl.when(layer_step > 0)
            def _():
                before = slot_of(layer_step - 1, hop)
                arrived = layered[late].at[before, :, cut]
                got(arrived, late_below.at[way, before])
                both = total + arrived[...].astype(f32)
                mine[...] = both.astype(mine.dtype)

            @pl.when(layer_step < depth - 1)
            def _():
                pltpu.make_async_remote_copy(
                    src_ref=mine,
                    dst_ref=layered[late].at[slot, :, cut],
                    send_sem=sent.at[late],
                    recv_sem=late_below.at[way, slot],
                    device_id=here.up,
                    device_id_type=MESH_ID,
                ).start()

            @pl.when(layer_step == depth - 1)
            def _():
                around = mine[...].astype(f32)
                if hop > 1:
                    arrived = ringed[late].at[hop - 2, :, cut]
                    got(arrived, from_ring.at[late, way, hop - 2])
                    around = around + arrived[...].astype(f32)
                if hop < chips:
                    mine[...] = around.astype(mine.dtype)
                    pltpu.make_async_remote_copy(
                        src_ref=mine,
                        dst_ref=ringed[late].at[hop - 1, :, cut],
                        send_sem=sent.at[late],
                        recv_sem=from_ring.at[late, way, hop - 1],
                        device_id=(here.right, here.left)[way],
                        device_id_type=MESH_ID,
                    ).start()
                else:
                    owned[late][:, cut] = around

        @pl.when(layer_step < depth - 1)
        def _():
            load(late, layer_step + 1, hop, True)

    late_step(0, 1)
    step(0, 1)
    for hop in range(2, chips + 1):
        late_step(0, hop)

    @pl.loop(0, depth)
    def _(layer_step):
        def late_ahead(hop):
            @pl.when(layer_step < depth - 1)
            def _():
                late_step(layer_step + 1, hop)

        for hop in range(2, chips):
            step(layer_step, hop)
            late_ahead(hop - 1)

        @pl.when(layer_step < depth - 1)
        def _():
            step(layer_step + 1, 1)

        late_ahead(chips - 1)
        step(layer_step, chips)
        late_ahead(chips)

    for which in range(count):
        some = pl.ds(0, 2 * slots - 1)
        most = grads[which].at[:, some] if len(grads[which].shape) == 4 else grads[which].at[some]
        pltpu.make_async_copy(most, most, sent.at[which]).wait()


def scatter(chips, depth, *grads):
    count = len(grads)
    slots = chips * depth
    steps = depth * (chips - 1)
    shapes = [
        (g.shape[1], g.shape[2]) if g.ndim == 3 else (g.shape[2], 2 * g.shape[3]) for g in grads
    ]
    anywhere = pl.BlockSpec(memory_space=pl.ANY)
    inner = pl.BlockSpec(memory_space=pltpu.VMEM)

    def room(most, last):
        leading = [most] * (count - 1) + [last]
        return [pltpu.VMEM((n,) + x, jnp.bfloat16) for n, x in zip(leading, shapes)]

    return pl.pallas_call(
        functools.partial(scatter_kernel, chips, depth, count),
        out_shape=[jax.ShapeDtypeStruct(x, jnp.float32) for x in shapes],
        in_specs=[anywhere] * count,
        out_specs=[inner] * count,
        scratch_shapes=room(slots, slots)
        + room(chips, chips)
        + room(steps, chips - 1)
        + room(depth - 1, chips * (depth - 1))
        + [
            pltpu.SemaphoreType.DMA((count,)),
            pltpu.SemaphoreType.DMA((count, 2, chips)),
            pltpu.SemaphoreType.DMA((count, 2, slots)),
            pltpu.SemaphoreType.DMA((count, depth - 1)),
            pltpu.SemaphoreType.DMA((count, 2, steps)),
            pltpu.SemaphoreType.DMA((2, chips * (depth - 1))),
        ],
        compiler_params=pltpu.CompilerParams(
            collective_id=1, has_side_effects=True, vmem_limit_bytes=VMEM_SCATTER
        ),
        name="scatter_gradients",
    )(*grads)


def from_behind(value, axis, steps):
    count = lax.axis_size(axis)
    first, last = (max(0, -steps), min(count, count - steps))
    return lax.ppermute(value, axis, [(source, source + steps) for source in range(first, last)])


def matmul(left, right):
    return jnp.dot(left, right, preferred_element_type=jnp.float32)


def matmul_tn(left, right):
    return lax.dot_general(
        left, right, (((0,), (0,)), ((), ())), preferred_element_type=jnp.float32
    )


def matmul_nt(left, right):
    return lax.dot_general(
        left, right, (((1,), (1,)), ((), ())), preferred_element_type=jnp.float32
    )


def inverse_rms(values):
    return lax.rsqrt(jnp.mean(values * values, axis=-1, keepdims=True) + NORM_EPS)


def norm_backward(values, scale, gain, grad_normed):
    weighted = grad_normed * gain
    grad_gain = jnp.sum(grad_normed * values * scale, axis=0)
    cubed = scale * scale * scale
    grad_values = scale * weighted - values * cubed * jnp.mean(
        weighted * values, axis=-1, keepdims=True
    )
    return (grad_values, grad_gain)


def adamw_update(param, grad, first, second, rate, decay):
    first_new = BETA_ONE * first + (1.0 - BETA_ONE) * grad
    second_new = BETA_TWO * second + (1.0 - BETA_TWO) * grad * grad
    first_hat = first_new / (1.0 - BETA_ONE**STEP)
    second_hat = second_new / (1.0 - BETA_TWO**STEP)
    param_new = param - rate * (first_hat / (jnp.sqrt(second_hat) + ADAM_EPS) + decay * param)
    return (param_new, first_new, second_new)


def adamw_kernel(*refs):
    grads, state, outs = refs[:4], refs[4:22], refs[22:]
    side, lanes, width = grads[0], outs[0].shape[1], outs[3].shape[1]
    vectors = side[:8, width:]
    found = [vectors[:2, :lanes], vectors[2:5, :lanes], grads[1][...], side[:, :width]]
    found += [ref[...] for ref in grads[2:]]
    for index, grad in enumerate(found):
        rate, decay = (RATE_VECTOR, 0.0) if index < 2 else (RATE_MATRIX, DECAY)
        param, first, second = (state[6 * kind + index][...] for kind in range(3))
        new = adamw_update(param, grad, first, second, rate, decay)
        for kind, value in enumerate((grad,) + new):
            outs[6 * kind + index][...] = value


def adamw(grads, params, firsts, seconds):
    inner = pl.BlockSpec(memory_space=pltpu.VMEM)
    return pl.pallas_call(
        adamw_kernel,
        out_shape=[jax.ShapeDtypeStruct(p.shape, p.dtype) for p in params] * 4,
        in_specs=[inner] * 22,
        out_specs=[inner] * 24,
        compiler_params=pltpu.CompilerParams(vmem_limit_bytes=48 << 20),
        name="adamw",
    )(*grads, *params, *firsts, *seconds)


def feed_forward_kernel(
    normed, resid, cot, gate, up, down, out, grad_normed, grad_down, grad_gate_up, turned
):
    half = jnp.bfloat16

    @pl.when(pl.program_id(0) == 0)
    def _():
        turned[...] = normed[...].T
        out[...] = resid[...]
        grad_normed[...] = jnp.zeros_like(grad_normed)

    gate_pre = matmul(normed[...], gate[...])
    up_pre = matmul(normed[...], up[...])
    grad_act = matmul_nt(cot[...], down[...])
    sigmoid_gate = jax.nn.sigmoid(gate_pre)
    silu_gate = gate_pre * sigmoid_gate
    act = (silu_gate * up_pre).astype(half)
    grad_gate = grad_act * up_pre * sigmoid_gate * (1.0 + gate_pre * (1.0 - sigmoid_gate))
    grad_gate = grad_gate.astype(half)
    grad_up = (grad_act * silu_gate).astype(half)
    out[...] += matmul(act, down[...])
    grad_normed[...] += matmul_nt(grad_gate, gate[...]) + matmul_nt(grad_up, up[...])
    grad_down[...] = matmul_tn(act, cot[...]).astype(half)
    grad_gate_up[0] = matmul(turned[...], grad_gate).astype(half)
    grad_gate_up[1] = matmul(turned[...], grad_up).astype(half)


def feed_forward(normed, resid, cot, packed, down):
    tokens, width = normed.shape
    units = down.shape[0]
    tile = UNIT_TILE
    tiles = units // tile
    half, single = jnp.bfloat16, jnp.float32

    def fixed(rows, columns):
        return pl.BlockSpec((rows, columns), lambda i: (0, 0))

    flops = 2 * tokens * width * units * 9
    return pl.pallas_call(
        feed_forward_kernel,
        grid=(tiles,),
        out_shape=[
            jax.ShapeDtypeStruct((tokens, width), single),
            jax.ShapeDtypeStruct((tokens, width), single),
            jax.ShapeDtypeStruct((units, width), half),
            jax.ShapeDtypeStruct((2, width, units), half),
        ],
        in_specs=[
            fixed(tokens, width),
            fixed(tokens, width),
            fixed(tokens, width),
            pl.BlockSpec((width, tile), lambda i: (0, i)),
            pl.BlockSpec((width, tile), lambda i: (0, i + tiles)),
            pl.BlockSpec((tile, width), lambda i: (i, 0)),
        ],
        out_specs=[
            fixed(tokens, width),
            fixed(tokens, width),
            pl.BlockSpec((tile, width), lambda i: (i, 0)),
            pl.BlockSpec((2, width, tile), lambda i: (0, 0, i)),
        ],
        scratch_shapes=[pltpu.VMEM((width, tokens), half)],
        compiler_params=pltpu.CompilerParams(vmem_limit_bytes=48 << 20),
        cost_estimate=pl.CostEstimate(
            flops=flops, bytes_accessed=12 * width * units, transcendentals=tokens * units
        ),
        name="feed_forward",
    )(normed, resid, cot, packed, packed, down)


def local(
    hidden_in,
    cotangent,
    doc_position,
    norm_gains,
    conv_taps,
    in_proj,
    out_proj,
    gate_up,
    down_proj,
    first_gains,
    first_taps,
    first_in,
    first_out,
    first_gate_up,
    first_down,
    second_gains,
    second_taps,
    second_in,
    second_out,
    second_gate_up,
    second_down,
):
    half = jnp.bfloat16
    single = jnp.float32
    row_count, length, width = hidden_in.shape
    tok_count = row_count * length
    chips, depth = lax.axis_size("ring"), lax.axis_size("fsdp")
    in_width = in_proj.shape[1]
    out_width = out_proj.shape[1]
    rows, unit_columns = gate_up.shape
    shards = 2 * chips * depth
    vectors = jnp.concatenate([norm_gains, conv_taps], axis=0)
    vector_count, lanes = vectors.shape
    corner = ((0, rows - vector_count), (0, LANES - lanes))
    packed_shards, down_shards = gather(
        chips, depth, (gate_up, in_proj, out_proj, jnp.pad(vectors, corner)), (down_proj,)
    )
    packed_full = packed_shards.reshape(width, -1)
    down_full = down_shards.reshape(-1, width)
    out_start = unit_columns + in_width
    in_full = packed_full[:, unit_columns:out_start]
    out_full = packed_full[:, out_start : out_start + out_width]
    vectors_full = packed_shards[:, :vector_count, -LANES:][:, :, :lanes].astype(single)
    vectors_full = vectors_full.transpose(1, 0, 2).reshape(vector_count, width)
    mixer_full = (None, None, in_full, out_full)
    gains_f = vectors_full[:2]
    taps_f = vectors_full[2:5]
    resid_one = hidden_in.reshape(tok_count, width).astype(single)
    scale_one = inverse_rms(resid_one)
    normed_one = (resid_one * scale_one * gains_f[0]).astype(half)
    projected = matmul(normed_one, mixer_full[2])
    b_branch = projected[:, :width]
    c_branch = projected[:, width : 2 * width]
    x_branch = projected[:, 2 * width :]
    gated_input = (b_branch * x_branch).astype(half)
    gated_rows = gated_input.reshape(row_count, length, width)
    carried = from_behind(gated_rows[:, length - 2 :, :], SEQ, 1)
    extended = jnp.concatenate([carried, gated_rows], axis=1).astype(single)
    gated_f = extended[:, 2:].reshape(tok_count, width)
    prev_one = extended[:, 1 : length + 1].reshape(tok_count, width)
    prev_two = extended[:, :length].reshape(tok_count, width)
    positions = doc_position.reshape(tok_count)
    mask_one = (positions >= 1).astype(single)[:, None]
    mask_two = (positions >= 2).astype(single)[:, None]
    conv_out = (
        taps_f[0] * gated_f + mask_one * taps_f[1] * prev_one + mask_two * taps_f[2] * prev_two
    )
    mixer_act = (c_branch * conv_out).astype(half)
    resid_two = resid_one + matmul(mixer_act, mixer_full[3])
    scale_two = inverse_rms(resid_two)
    normed_two = (resid_two * scale_two * gains_f[1]).astype(half)
    cot_rows = cotangent.reshape(tok_count, width)
    block_out, grad_normed, grad_down, grad_gate_up = feed_forward(
        normed_two, resid_two, cot_rows, packed_full, down_full
    )
    norm_part, gain_two_grad = norm_backward(resid_two, scale_two, gains_f[1], grad_normed)
    grad_resid = cot_rows.astype(single) + norm_part
    resid_cast = grad_resid.astype(half)
    grad_mixer = matmul_nt(resid_cast, mixer_full[3])
    grad_cbranch = grad_mixer * conv_out
    grad_conv = grad_mixer * c_branch
    masked_one = mask_one * grad_conv
    masked_two = mask_two * grad_conv
    grad_taps = jnp.stack(
        [
            jnp.sum(grad_conv * gated_f, axis=0),
            jnp.sum(masked_one * prev_one, axis=0),
            jnp.sum(masked_two * prev_two, axis=0),
        ]
    )
    one_rows = masked_one.reshape(row_count, length, width)
    two_rows = masked_two.reshape(row_count, length, width)
    leading = from_behind((one_rows[:, :2, :], two_rows[:, :2, :]), SEQ, -1)
    ext_one = jnp.concatenate([one_rows, leading[0]], axis=1)
    ext_two = jnp.concatenate([two_rows, leading[1]], axis=1)
    next_one = ext_one[:, 1 : length + 1].reshape(tok_count, width)
    next_two = ext_two[:, 2 : length + 2].reshape(tok_count, width)
    grad_gated = taps_f[0] * grad_conv + taps_f[1] * next_one + taps_f[2] * next_two
    grad_proj = jnp.concatenate(
        [grad_gated * x_branch, grad_cbranch, grad_gated * b_branch], axis=1
    ).astype(half)
    grad_normone = matmul_nt(grad_proj, mixer_full[2])
    first_part, gain_one_grad = norm_backward(resid_one, scale_one, gains_f[0], grad_normone)
    grad_hidden = grad_resid + first_part
    grad_gains = jnp.stack([gain_one_grad, gain_two_grad])
    grad_in = matmul_tn(normed_one, grad_proj)
    grad_out = matmul_tn(mixer_act, resid_cast)
    vector_grads = jnp.concatenate([grad_gains, grad_taps], axis=0)
    vector_shards = vector_grads.reshape(vector_count, shards, lanes).transpose(1, 0, 2)
    vector_shards = jnp.pad(vector_shards.astype(half), ((0, 0),) + corner)
    grad_side = jnp.concatenate(
        [grad_out.astype(half).reshape(shards, rows, out_width), vector_shards], axis=2
    )
    gate_owned, in_owned, side_owned, down_owned = scatter(
        chips,
        depth,
        grad_gate_up.reshape(2, shards, rows, -1),
        grad_in.astype(half).reshape(shards, rows, in_width),
        grad_side,
        grad_down.reshape(shards, -1, width),
    )
    params = (norm_gains, conv_taps, in_proj, out_proj, gate_up, down_proj)
    firsts = (first_gains, first_taps, first_in, first_out, first_gate_up, first_down)
    seconds = (second_gains, second_taps, second_in, second_out, second_gate_up, second_down)
    owned = (side_owned, in_owned, gate_owned, down_owned)
    results = adamw(owned, params, firsts, seconds)
    out_rows = block_out.reshape(row_count, length, width)
    grad_rows = grad_hidden.reshape(row_count, length, width)
    return (
        out_rows,
        grad_rows,
        *results,
    )


def solution(mesh):
    tokens, depth = mesh.devices.shape
    chip_mesh = Mesh(mesh.devices.reshape(tokens // 2, 2, depth), ALL)
    in_specs = (
        P("fsdp", SEQ, None),
        P("fsdp", SEQ, None),
        P("fsdp", SEQ),
        P(None, ALL),
        P(None, ALL),
        P(ALL, None),
        P(ALL, None),
        P(ALL, None),
        P(ALL, None),
        P(None, ALL),
        P(None, ALL),
        P(ALL, None),
        P(ALL, None),
        P(ALL, None),
        P(ALL, None),
        P(None, ALL),
        P(None, ALL),
        P(ALL, None),
        P(ALL, None),
        P(ALL, None),
        P(ALL, None),
    )
    out_specs = (
        P("fsdp", SEQ, None),
        P("fsdp", SEQ, None),
        P(None, ALL),
        P(None, ALL),
        P(ALL, None),
        P(ALL, None),
        P(ALL, None),
        P(ALL, None),
        P(None, ALL),
        P(None, ALL),
        P(ALL, None),
        P(ALL, None),
        P(ALL, None),
        P(ALL, None),
        P(None, ALL),
        P(None, ALL),
        P(ALL, None),
        P(ALL, None),
        P(ALL, None),
        P(ALL, None),
        P(None, ALL),
        P(None, ALL),
        P(ALL, None),
        P(ALL, None),
        P(ALL, None),
        P(ALL, None),
    )
    return jax.shard_map(local, mesh=chip_mesh, in_specs=in_specs, out_specs=out_specs, check_vma=False)
```

```python
import functools

import jax
import jax.numpy as jnp
from jax import lax
from jax.experimental import pallas as pl
from jax.experimental.pallas import tpu as pltpu
from jax.sharding import Mesh
from jax.sharding import PartitionSpec as P

STEP = 3


NORM_EPS = 1e-05
BETA_ONE = 0.9
BETA_TWO = 0.999
ADAM_EPS = 1e-08
RATE_MATRIX = 0.005
RATE_VECTOR = 0.2
DECAY = 0.1
LANES = 128
VMEM_SCATTER = 46 << 20
VMEM_GATHER = 60 << 20
UNIT_TILE = 512
MESH_ID = pl.DeviceIdType.MESH
SEQ = ("ring", "core")
ALL = ("ring", "core", "fsdp")


def snake(index):
    return 2 * (index // 2) + (index % 2 + index // 2) % 2


def halves(columns):
    first = (columns // 2 + LANES - 1) // LANES * LANES
    return (pl.ds(0, first), pl.ds(first, columns - first))


class Place:
    def __init__(self, chips, depth):
        self.chips, self.depth = chips, depth
        self.core = lax.axis_index("core")
        self.layer = lax.axis_index("fsdp")
        self.spot = snake(lax.axis_index("ring"))
        self.own = lax.axis_index("ring")
        self.right = self.device(snake((self.spot + 1) % chips), self.core, self.layer)
        self.left = self.device(snake((self.spot + chips - 1) % chips), self.core, self.layer)
        self.up = self.device(self.own, self.core, (self.layer + 1) % depth)
        self.down = self.device(self.own, self.core, (self.layer + depth - 1) % depth)
        self.sibling = self.device(self.own, 1 - self.core, self.layer)

    def device(self, ring, core, layer):
        return (ring, core, layer)

    def shard(self, spot, core, layer):
        return (snake(spot) * 2 + core) * self.depth + layer

    def greet(self):
        for device in (self.right, self.left, self.up, self.down, self.sibling):
            pl.semaphore_signal(
                pltpu.get_barrier_semaphore(), inc=1, device_id=device, device_id_type=MESH_ID
            )

    def await_greetings(self):
        pl.semaphore_wait(pltpu.get_barrier_semaphore(), 5)


def gather_kernel(chips, depth, groups, *refs):
    count, inputs = len(groups), sum(groups)
    wholes = refs[inputs : inputs + count]
    shards = refs[inputs + count : inputs + 2 * count]
    wide = refs[inputs + 2 * count : 2 * inputs + 2 * count]
    loaded, sent, from_sibling, from_below, from_ring, kept, late_ring, late_below = refs[
        2 * inputs + 2 * count :
    ]
    loads = [
        pltpu.make_async_copy(refs[index], wide[index], loaded.at[index])
        for index in range(inputs)
    ]
    for load in loads:
        load.start()
    here = Place(chips, depth)
    here.greet()
    for load in loads:
        load.wait()
    taken = 0
    for shard, members in zip(shards, groups):
        start = 0
        for member in wide[taken : taken + members]:
            shard[:, start : start + member.shape[1]] = member[...].astype(shard.dtype)
            start += member.shape[1]
        taken += members
    here.await_greetings()
    late = count - 1
    cuts = [halves(ref.shape[1]) for ref in shards]

    def block(which, shard):
        return wholes[which].at[shard]

    def piece_of(which, shard, way):
        return wholes[which].at[shard, :, cuts[which][way]]

    def send(source, target, which, arrived, device):
        pltpu.make_async_remote_copy(
            src_ref=source,
            dst_ref=target,
            send_sem=sent.at[which],
            recv_sem=arrived,
            device_id=device,
            device_id_type=MESH_ID,
        ).start()

    def awaited(ref, arrived):
        pltpu.make_async_copy(ref, ref, arrived).wait()

    own = here.shard(here.spot, here.core, here.layer)
    for which in range(late):
        send(shards[which], block(which, own), which, from_below.at[which, 0], here.up)
        for way in range(2):
            send(
                shards[which].at[:, cuts[which][way]],
                piece_of(which, own, way),
                which,
                from_ring.at[which, way, 0],
                (here.right, here.left)[way],
            )
    for way in range(2):
        part = shards[late].at[:, cuts[late][way]]
        piece = piece_of(late, own, way)
        send(part, piece, late, late_ring.at[way, 0], (here.right, here.left)[way])
        send(part, piece, late, late_below.at[way, 0], here.up)
    for which in range(count):
        send(shards[which], block(which, own), which, from_sibling.at[which], here.sibling)
        pltpu.make_async_copy(shards[which], block(which, own), kept.at[which]).start()

    def late_around(hop):
        for way in range(2):
            away = (chips - hop, hop)[way]
            piece = piece_of(late, here.shard((here.spot + away) % chips, here.core, here.layer), way)
            awaited(piece, late_ring.at[way, hop - 1])
            if hop < chips - 1:
                send(piece, piece, late, late_ring.at[way, hop], (here.right, here.left)[way])
            send(piece, piece, late, late_below.at[way, hop], here.up)
            send(piece, piece, late, from_sibling.at[late], here.sibling)

    def late_layer(layer_step, hop):
        layer = (here.layer + depth - layer_step) % depth
        for way in range(2):
            away = (chips - hop, hop)[way]
            piece = piece_of(late, here.shard((here.spot + away) % chips, here.core, layer), way)
            awaited(piece, late_below.at[way, (layer_step - 1) * chips + hop])

            @pl.when(layer_step < depth - 1)
            def _():
                send(piece, piece, late, late_below.at[way, layer_step * chips + hop], here.up)

            send(piece, piece, late, from_sibling.at[late], here.sibling)

    def late_step(layer_step, hop):
        if hop > 0:
            @pl.when(layer_step == 0)
            def _():
                late_around(hop)

        @pl.when(layer_step > 0)
        def _():
            late_layer(layer_step, hop)

    def around(hop, layer_step):
        layer = (here.layer + depth - layer_step) % depth
        for which in range(late):
            for way in range(2):
                away = (chips - hop, hop)[way]
                shard = here.shard((here.spot + away) % chips, here.core, layer)
                arrived = layer_step * (chips - 1) + hop - 1
                piece = piece_of(which, shard, way)
                awaited(piece, from_ring.at[which, way, arrived])
                if hop < chips - 1:
                    send(
                        piece,
                        piece,
                        which,
                        from_ring.at[which, way, arrived + 1],
                        (here.right, here.left)[way],
                    )
                send(piece, piece, which, from_sibling.at[which], here.sibling)

    def layer_arrives(layer_step):
        layer = (here.layer + depth - layer_step) % depth
        shard = here.shard(here.spot, here.core, layer)
        for which in range(late):
            whole = block(which, shard)
            awaited(whole, from_below.at[which, layer_step - 1])

            @pl.when(layer_step < depth - 1)
            def _():
                send(whole, whole, which, from_below.at[which, layer_step], here.up)

            for way in range(2):
                piece = piece_of(which, shard, way)
                send(
                    piece,
                    piece,
                    which,
                    from_ring.at[which, way, layer_step * (chips - 1)],
                    (here.right, here.left)[way],
                )
            send(whole, whole, which, from_sibling.at[which], here.sibling)

    @pl.loop(0, depth)
    def _(layer_step):
        for hop in range(1, chips - 1):
            around(hop, layer_step)
            late_step(layer_step, hop - 1)

        @pl.when(layer_step < depth - 1)
        def _():
            layer_arrives(layer_step + 1)

        around(chips - 1, layer_step)
        late_step(layer_step, chips - 2)
        late_step(layer_step, chips - 1)

    shard_count = 2 * chips * depth
    for which in range(count):
        pltpu.make_async_copy(shards[which], block(which, own), kept.at[which]).wait()
        awaited(wholes[which].at[pl.ds(0, shard_count // 2)], from_sibling.at[which])
        awaited(wholes[which].at[pl.ds(0, shard_count - 1)], sent.at[which])


def gather(chips, depth, *groups):
    count = len(groups)
    steps = depth * (chips - 1)
    shard_count = 2 * chips * depth
    shapes = [(g[0].shape[0], sum(x.shape[1] for x in g)) for g in groups]
    half = jnp.bfloat16
    return pl.pallas_call(
        functools.partial(gather_kernel, chips, depth, [len(g) for g in groups]),
        out_shape=[jax.ShapeDtypeStruct((shard_count,) + shape, half) for shape in shapes],
        in_specs=[pl.BlockSpec(memory_space=pl.ANY)] * sum(len(g) for g in groups),
        out_specs=[pl.BlockSpec(memory_space=pl.ANY)] * count,
        scratch_shapes=[pltpu.VMEM(shape, half) for shape in shapes]
        + [pltpu.VMEM(x.shape, x.dtype) for g in groups for x in g]
        + [
            pltpu.SemaphoreType.DMA((sum(len(g) for g in groups),)),
            pltpu.SemaphoreType.DMA((count,)),
            pltpu.SemaphoreType.DMA((count,)),
            pltpu.SemaphoreType.DMA((count, depth - 1)),
            pltpu.SemaphoreType.DMA((count, 2, steps)),
            pltpu.SemaphoreType.DMA((count,)),
            pltpu.SemaphoreType.DMA((2, chips - 1)),
            pltpu.SemaphoreType.DMA((2, chips * (depth - 1))),
        ],
        compiler_params=pltpu.CompilerParams(
            collective_id=0, has_side_effects=True, vmem_limit_bytes=VMEM_GATHER
        ),
        name="gather_weights",
    )(*[x for g in groups for x in g])


def scatter_kernel(chips, depth, count, *refs):
    grads = refs[:count]
    owned = refs[count : 2 * count]
    rest = refs[2 * count :]
    theirs = rest[:count]
    staged = rest[count : 2 * count]
    ringed = rest[2 * count : 3 * count]
    layered = rest[3 * count : 4 * count]
    sent, loaded, from_sibling, from_below, from_ring, late_below = rest[4 * count :]
    here = Place(chips, depth)
    late = count - 1
    cuts = [halves(ref.shape[1]) for ref in owned]
    f32 = jnp.float32

    def part(which, shard, way):
        if len(grads[which].shape) == 4:
            return grads[which].at[way, shard]
        return grads[which].at[shard, :, cuts[which][way]]

    def place(hop, way):
        away = (chips - hop, hop)[way]
        return (here.spot + away) % chips

    def layer_of(layer_step):
        return (here.layer + 2 * depth - 1 - layer_step) % depth

    def slot_of(layer_step, hop):
        return layer_step * chips + hop - 1

    def load(which, layer_step, hop, start):
        for way, cut in enumerate(cuts[which]):
            shard = here.shard(place(hop, way), here.core, layer_of(layer_step))
            copy = pltpu.make_async_copy(
                part(which, shard, way),
                staged[which].at[hop - 1, :, cut],
                loaded.at[which, way, hop - 1],
            )
            copy.start() if start else copy.wait()

    def hand_over(which, slot):
        layer_step = slot // chips
        hop = slot % chips + 1
        for way, cut in enumerate(cuts[which]):
            shard = here.shard(place(hop, way), 1 - here.core, layer_of(layer_step))
            pltpu.make_async_remote_copy(
                src_ref=part(which, shard, way),
                dst_ref=theirs[which].at[slot, :, cut],
                send_sem=sent.at[which],
                recv_sem=from_sibling.at[which, way, slot],
                device_id=here.sibling,
                device_id_type=MESH_ID,
            ).start()

    slots = chips * depth
    for hop in range(1, chips + 1):
        for which in range(count):
            load(which, 0, hop, True)
    here.greet()
    here.await_greetings()

    @pl.loop(0, slots)
    def _(slot):
        for which in reversed(range(count)):
            hand_over(which, slot)

    def got(ref, semaphore):
        pltpu.make_async_copy(ref, ref, semaphore).wait()

    def step(layer_step, hop):
        slot = slot_of(layer_step, hop)
        for which in range(late):
            load(which, layer_step, hop, False)
            if hop == chips:
                @pl.when(layer_step > 0)
                def _():
                    ref = layered[which].at[layer_step - 1]
                    got(ref, from_below.at[which, layer_step - 1])

            for way, cut in enumerate(cuts[which]):
                mine = theirs[which].at[slot, :, cut]
                got(mine, from_sibling.at[which, way, slot])
                total = mine[...].astype(f32) + staged[which][hop - 1, :, cut].astype(f32)
                if hop > 1:
                    index = layer_step * (chips - 1) + hop - 2
                    arrived = ringed[which].at[index, :, cut]
                    got(arrived, from_ring.at[which, way, index])
                    total = total + arrived[...].astype(f32)
                if hop < chips:
                    index = layer_step * (chips - 1) + hop - 1
                    mine[...] = total.astype(mine.dtype)
                    pltpu.make_async_remote_copy(
                        src_ref=mine,
                        dst_ref=ringed[which].at[index, :, cut],
                        send_sem=sent.at[which],
                        recv_sem=from_ring.at[which, way, index],
                        device_id=(here.right, here.left)[way],
                        device_id_type=MESH_ID,
                    ).start()
                else:
                    owned[which][:, cut] = total

            if hop == chips:
                @pl.when(layer_step > 0)
                def _():
                    owned[which][...] += layered[which][layer_step - 1].astype(f32)

                @pl.when(layer_step < depth - 1)
                def _():
                    mine = theirs[which].at[slot]
                    mine[...] = owned[which][...].astype(mine.dtype)
                    pltpu.make_async_remote_copy(
                        src_ref=mine,
                        dst_ref=layered[which].at[layer_step],
                        send_sem=sent.at[which],
                        recv_sem=from_below.at[which, layer_step],
                        device_id=here.up,
                        device_id_type=MESH_ID,
                    ).start()

        @pl.when(layer_step < depth - 1)
        def _():
            for which in range(late):
                load(which, layer_step + 1, hop, True)

    def late_step(layer_step, hop):
        slot = slot_of(layer_step, hop)
        load(late, layer_step, hop, False)
        for way, cut in enumerate(cuts[late]):
            mine = theirs[late].at[slot, :, cut]
            got(mine, from_sibling.at[late, way, slot])
            total = mine[...].astype(f32) + staged[late][hop - 1, :, cut].astype(f32)
            mine[...] = total.astype(mine.dtype)

            @pl.when(layer_step > 0)
            def _():
                before = slot_of(layer_step - 1, hop)
                arrived = layered[late].at[before, :, cut]
                got(arrived, late_below.at[way, before])
                both = total + arrived[...].astype(f32)
                mine[...] = both.astype(mine.dtype)

            @pl.when(layer_step < depth - 1)
            def _():
                pltpu.make_async_remote_copy(
                    src_ref=mine,
                    dst_ref=layered[late].at[slot, :, cut],
                    send_sem=sent.at[late],
                    recv_sem=late_below.at[way, slot],
                    device_id=here.up,
                    device_id_type=MESH_ID,
                ).start()

            @pl.when(layer_step == depth - 1)
            def _():
                around = mine[...].astype(f32)
                if hop > 1:
                    arrived = ringed[late].at[hop - 2, :, cut]
                    got(arrived, from_ring.at[late, way, hop - 2])
                    around = around + arrived[...].astype(f32)
                if hop < chips:
                    mine[...] = around.astype(mine.dtype)
                    pltpu.make_async_remote_copy(
                        src_ref=mine,
                        dst_ref=ringed[late].at[hop - 1, :, cut],
                        send_sem=sent.at[late],
                        recv_sem=from_ring.at[late, way, hop - 1],
                        device_id=(here.right, here.left)[way],
                        device_id_type=MESH_ID,
                    ).start()
                else:
                    owned[late][:, cut] = around

        @pl.when(layer_step < depth - 1)
        def _():
            load(late, layer_step + 1, hop, True)

    late_step(0, 1)
    step(0, 1)
    for hop in range(2, chips + 1):
        late_step(0, hop)

    @pl.loop(0, depth)
    def _(layer_step):
        def late_ahead(hop):
            @pl.when(layer_step < depth - 1)
            def _():
                late_step(layer_step + 1, hop)

        for hop in range(2, chips):
            step(layer_step, hop)
            late_ahead(hop - 1)

        @pl.when(layer_step < depth - 1)
        def _():
            step(layer_step + 1, 1)

        late_ahead(chips - 1)
        step(layer_step, chips)
        late_ahead(chips)

    for which in range(count):
        some = pl.ds(0, 2 * slots - 1)
        most = grads[which].at[:, some] if len(grads[which].shape) == 4 else grads[which].at[some]
        pltpu.make_async_copy(most, most, sent.at[which]).wait()


def scatter(chips, depth, *grads):
    count = len(grads)
    slots = chips * depth
    steps = depth * (chips - 1)
    shapes = [
        (g.shape[1], g.shape[2]) if g.ndim == 3 else (g.shape[2], 2 * g.shape[3]) for g in grads
    ]
    anywhere = pl.BlockSpec(memory_space=pl.ANY)
    inner = pl.BlockSpec(memory_space=pltpu.VMEM)

    def room(most, last):
        leading = [most] * (count - 1) + [last]
        return [pltpu.VMEM((n,) + x, jnp.bfloat16) for n, x in zip(leading, shapes)]

    return pl.pallas_call(
        functools.partial(scatter_kernel, chips, depth, count),
        out_shape=[jax.ShapeDtypeStruct(x, jnp.float32) for x in shapes],
        in_specs=[anywhere] * count,
        out_specs=[inner] * count,
        scratch_shapes=room(slots, slots)
        + room(chips, chips)
        + room(steps, chips - 1)
        + room(depth - 1, chips * (depth - 1))
        + [
            pltpu.SemaphoreType.DMA((count,)),
            pltpu.SemaphoreType.DMA((count, 2, chips)),
            pltpu.SemaphoreType.DMA((count, 2, slots)),
            pltpu.SemaphoreType.DMA((count, depth - 1)),
            pltpu.SemaphoreType.DMA((count, 2, steps)),
            pltpu.SemaphoreType.DMA((2, chips * (depth - 1))),
        ],
        compiler_params=pltpu.CompilerParams(
            collective_id=1, has_side_effects=True, vmem_limit_bytes=VMEM_SCATTER
        ),
        name="scatter_gradients",
    )(*grads)


def from_behind(value, axis, steps):
    count = lax.axis_size(axis)
    first, last = (max(0, -steps), min(count, count - steps))
    return lax.ppermute(value, axis, [(source, source + steps) for source in range(first, last)])


def matmul(left, right):
    return jnp.dot(left, right, preferred_element_type=jnp.float32)


def matmul_tn(left, right):
    return lax.dot_general(
        left, right, (((0,), (0,)), ((), ())), preferred_element_type=jnp.float32
    )


def matmul_nt(left, right):
    return lax.dot_general(
        left, right, (((1,), (1,)), ((), ())), preferred_element_type=jnp.float32
    )


def inverse_rms(values):
    return lax.rsqrt(jnp.mean(values * values, axis=-1, keepdims=True) + NORM_EPS)


def norm_backward(values, scale, gain, grad_normed):
    weighted = grad_normed * gain
    grad_gain = jnp.sum(grad_normed * values * scale, axis=0)
    cubed = scale * scale * scale
    grad_values = scale * weighted - values * cubed * jnp.mean(
        weighted * values, axis=-1, keepdims=True
    )
    return (grad_values, grad_gain)


def adamw_update(param, grad, first, second, rate, decay):
    first_new = BETA_ONE * first + (1.0 - BETA_ONE) * grad
    second_new = BETA_TWO * second + (1.0 - BETA_TWO) * grad * grad
    first_hat = first_new / (1.0 - BETA_ONE**STEP)
    second_hat = second_new / (1.0 - BETA_TWO**STEP)
    param_new = param - rate * (first_hat / (jnp.sqrt(second_hat) + ADAM_EPS) + decay * param)
    return (param_new, first_new, second_new)


def adamw_kernel(*refs):
    grads, state, outs = refs[:4], refs[4:22], refs[22:]
    side, lanes, width = grads[0], outs[0].shape[1], outs[3].shape[1]
    vectors = side[:8, width:]
    found = [vectors[:2, :lanes], vectors[2:5, :lanes], grads[1][...], side[:, :width]]
    found += [ref[...] for ref in grads[2:]]
    for index, grad in enumerate(found):
        rate, decay = (RATE_VECTOR, 0.0) if index < 2 else (RATE_MATRIX, DECAY)
        param, first, second = (state[6 * kind + index][...] for kind in range(3))
        new = adamw_update(param, grad, first, second, rate, decay)
        for kind, value in enumerate((grad,) + new):
            outs[6 * kind + index][...] = value


def adamw(grads, params, firsts, seconds):
    inner = pl.BlockSpec(memory_space=pltpu.VMEM)
    return pl.pallas_call(
        adamw_kernel,
        out_shape=[jax.ShapeDtypeStruct(p.shape, p.dtype) for p in params] * 4,
        in_specs=[inner] * 22,
        out_specs=[inner] * 24,
        compiler_params=pltpu.CompilerParams(vmem_limit_bytes=48 << 20),
        name="adamw",
    )(*grads, *params, *firsts, *seconds)


def feed_forward_kernel(
    normed, resid, cot, gate, up, down, out, grad_normed, grad_down, grad_gate_up, turned
):
    half = jnp.bfloat16

    @pl.when(pl.program_id(0) == 0)
    def _():
        turned[...] = normed[...].T
        out[...] = resid[...]
        grad_normed[...] = jnp.zeros_like(grad_normed)

    gate_pre = matmul(normed[...], gate[...])
    up_pre = matmul(normed[...], up[...])
    grad_act = matmul_nt(cot[...], down[...])
    sigmoid_gate = jax.nn.sigmoid(gate_pre)
    silu_gate = gate_pre * sigmoid_gate
    act = (silu_gate * up_pre).astype(half)
    grad_gate = grad_act * up_pre * sigmoid_gate * (1.0 + gate_pre * (1.0 - sigmoid_gate))
    grad_gate = grad_gate.astype(half)
    grad_up = (grad_act * silu_gate).astype(half)
    out[...] += matmul(act, down[...])
    grad_normed[...] += matmul_nt(grad_gate, gate[...]) + matmul_nt(grad_up, up[...])
    grad_down[...] = matmul_tn(act, cot[...]).astype(half)
    grad_gate_up[0] = matmul(turned[...], grad_gate).astype(half)
    grad_gate_up[1] = matmul(turned[...], grad_up).astype(half)


def feed_forward(normed, resid, cot, gate_up, down):
    tokens, width = normed.shape
    units = down.shape[0]
    tile = UNIT_TILE
    tiles = units // tile
    half, single = jnp.bfloat16, jnp.float32

    def fixed(rows, columns):
        return pl.BlockSpec((rows, columns), lambda i: (0, 0))

    flops = 2 * tokens * width * units * 9
    return pl.pallas_call(
        feed_forward_kernel,
        grid=(tiles,),
        out_shape=[
            jax.ShapeDtypeStruct((tokens, width), single),
            jax.ShapeDtypeStruct((tokens, width), single),
            jax.ShapeDtypeStruct((units, width), half),
            jax.ShapeDtypeStruct((2, width, units), half),
        ],
        in_specs=[
            fixed(tokens, width),
            fixed(tokens, width),
            fixed(tokens, width),
            pl.BlockSpec((width, tile), lambda i: (0, i)),
            pl.BlockSpec((width, tile), lambda i: (0, i + tiles)),
            pl.BlockSpec((tile, width), lambda i: (i, 0)),
        ],
        out_specs=[
            fixed(tokens, width),
            fixed(tokens, width),
            pl.BlockSpec((tile, width), lambda i: (i, 0)),
            pl.BlockSpec((2, width, tile), lambda i: (0, 0, i)),
        ],
        scratch_shapes=[pltpu.VMEM((width, tokens), half)],
        compiler_params=pltpu.CompilerParams(vmem_limit_bytes=48 << 20),
        cost_estimate=pl.CostEstimate(
            flops=flops, bytes_accessed=12 * width * units, transcendentals=tokens * units
        ),
        name="feed_forward",
    )(normed, resid, cot, gate_up, gate_up, down)


def local(
    hidden_in,
    cotangent,
    doc_position,
    norm_gains,
    conv_taps,
    in_proj,
    out_proj,
    gate_up,
    down_proj,
    first_gains,
    first_taps,
    first_in,
    first_out,
    first_gate_up,
    first_down,
    second_gains,
    second_taps,
    second_in,
    second_out,
    second_gate_up,
    second_down,
):
    half = jnp.bfloat16
    single = jnp.float32
    row_count, length, width = hidden_in.shape
    tok_count = row_count * length
    chips, depth = lax.axis_size("ring"), lax.axis_size("fsdp")
    in_width = in_proj.shape[1]
    out_width = out_proj.shape[1]
    rows = gate_up.shape[0]
    shards = 2 * chips * depth
    vectors = jnp.concatenate([norm_gains, conv_taps], axis=0)
    vector_count, lanes = vectors.shape
    corner = ((0, rows - vector_count), (0, LANES - lanes))
    gate_shards, down_shards, mixer_shards = gather(
        chips, depth, (gate_up,), (down_proj,), (in_proj, out_proj, jnp.pad(vectors, corner))
    )
    gate_full = gate_shards.reshape(width, -1)
    down_full = down_shards.reshape(-1, width)
    mixer_columns = mixer_shards.reshape(width, -1)
    in_full = mixer_columns[:, :in_width]
    out_full = mixer_columns[:, in_width : in_width + out_width]
    vectors_full = mixer_shards[:, :vector_count, -LANES:][:, :, :lanes].astype(single)
    vectors_full = vectors_full.transpose(1, 0, 2).reshape(vector_count, width)
    mixer_full = (None, None, in_full, out_full)
    gains_f = vectors_full[:2]
    taps_f = vectors_full[2:5]
    resid_one = hidden_in.reshape(tok_count, width).astype(single)
    scale_one = inverse_rms(resid_one)
    normed_one = (resid_one * scale_one * gains_f[0]).astype(half)
    projected = matmul(normed_one, mixer_full[2])
    b_branch = projected[:, :width]
    c_branch = projected[:, width : 2 * width]
    x_branch = projected[:, 2 * width :]
    gated_input = (b_branch * x_branch).astype(half)
    gated_rows = gated_input.reshape(row_count, length, width)
    carried = from_behind(gated_rows[:, length - 2 :, :], SEQ, 1)
    extended = jnp.concatenate([carried, gated_rows], axis=1).astype(single)
    gated_f = extended[:, 2:].reshape(tok_count, width)
    prev_one = extended[:, 1 : length + 1].reshape(tok_count, width)
    prev_two = extended[:, :length].reshape(tok_count, width)
    positions = doc_position.reshape(tok_count)
    mask_one = (positions >= 1).astype(single)[:, None]
    mask_two = (positions >= 2).astype(single)[:, None]
    conv_out = (
        taps_f[0] * gated_f + mask_one * taps_f[1] * prev_one + mask_two * taps_f[2] * prev_two
    )
    mixer_act = (c_branch * conv_out).astype(half)
    resid_two = resid_one + matmul(mixer_act, mixer_full[3])
    scale_two = inverse_rms(resid_two)
    normed_two = (resid_two * scale_two * gains_f[1]).astype(half)
    cot_rows = cotangent.reshape(tok_count, width)
    block_out, grad_normed, grad_down, grad_gate_up = feed_forward(
        normed_two, resid_two, cot_rows, gate_full, down_full
    )
    norm_part, gain_two_grad = norm_backward(resid_two, scale_two, gains_f[1], grad_normed)
    grad_resid = cot_rows.astype(single) + norm_part
    resid_cast = grad_resid.astype(half)
    grad_mixer = matmul_nt(resid_cast, mixer_full[3])
    grad_cbranch = grad_mixer * conv_out
    grad_conv = grad_mixer * c_branch
    masked_one = mask_one * grad_conv
    masked_two = mask_two * grad_conv
    grad_taps = jnp.stack(
        [
            jnp.sum(grad_conv * gated_f, axis=0),
            jnp.sum(masked_one * prev_one, axis=0),
            jnp.sum(masked_two * prev_two, axis=0),
        ]
    )
    one_rows = masked_one.reshape(row_count, length, width)
    two_rows = masked_two.reshape(row_count, length, width)
    leading = from_behind((one_rows[:, :2, :], two_rows[:, :2, :]), SEQ, -1)
    ext_one = jnp.concatenate([one_rows, leading[0]], axis=1)
    ext_two = jnp.concatenate([two_rows, leading[1]], axis=1)
    next_one = ext_one[:, 1 : length + 1].reshape(tok_count, width)
    next_two = ext_two[:, 2 : length + 2].reshape(tok_count, width)
    grad_gated = taps_f[0] * grad_conv + taps_f[1] * next_one + taps_f[2] * next_two
    grad_proj = jnp.concatenate(
        [grad_gated * x_branch, grad_cbranch, grad_gated * b_branch], axis=1
    ).astype(half)
    grad_normone = matmul_nt(grad_proj, mixer_full[2])
    first_part, gain_one_grad = norm_backward(resid_one, scale_one, gains_f[0], grad_normone)
    grad_hidden = grad_resid + first_part
    grad_gains = jnp.stack([gain_one_grad, gain_two_grad])
    grad_in = matmul_tn(normed_one, grad_proj)
    grad_out = matmul_tn(mixer_act, resid_cast)
    vector_grads = jnp.concatenate([grad_gains, grad_taps], axis=0)
    vector_shards = vector_grads.reshape(vector_count, shards, lanes).transpose(1, 0, 2)
    vector_shards = jnp.pad(vector_shards.astype(half), ((0, 0),) + corner)
    grad_side = jnp.concatenate(
        [grad_out.astype(half).reshape(shards, rows, out_width), vector_shards], axis=2
    )
    gate_owned, in_owned, side_owned, down_owned = scatter(
        chips,
        depth,
        grad_gate_up.reshape(2, shards, rows, -1),
        grad_in.astype(half).reshape(shards, rows, in_width),
        grad_side,
        grad_down.reshape(shards, -1, width),
    )
    params = (norm_gains, conv_taps, in_proj, out_proj, gate_up, down_proj)
    firsts = (first_gains, first_taps, first_in, first_out, first_gate_up, first_down)
    seconds = (second_gains, second_taps, second_in, second_out, second_gate_up, second_down)
    owned = (side_owned, in_owned, gate_owned, down_owned)
    results = adamw(owned, params, firsts, seconds)
    out_rows = block_out.reshape(row_count, length, width)
    grad_rows = grad_hidden.reshape(row_count, length, width)
    return (
        out_rows,
        grad_rows,
        *results,
    )


def solution(mesh):
    tokens, depth = mesh.devices.shape
    chip_mesh = Mesh(mesh.devices.reshape(tokens // 2, 2, depth), ALL)
    in_specs = (
        P("fsdp", SEQ, None),
        P("fsdp", SEQ, None),
        P("fsdp", SEQ),
        P(None, ALL),
        P(None, ALL),
        P(ALL, None),
        P(ALL, None),
        P(ALL, None),
        P(ALL, None),
        P(None, ALL),
        P(None, ALL),
        P(ALL, None),
        P(ALL, None),
        P(ALL, None),
        P(ALL, None),
        P(None, ALL),
        P(None, ALL),
        P(ALL, None),
        P(ALL, None),
        P(ALL, None),
        P(ALL, None),
    )
    out_specs = (
        P("fsdp", SEQ, None),
        P("fsdp", SEQ, None),
        P(None, ALL),
        P(None, ALL),
        P(ALL, None),
        P(ALL, None),
        P(ALL, None),
        P(ALL, None),
        P(None, ALL),
        P(None, ALL),
        P(ALL, None),
        P(ALL, None),
        P(ALL, None),
        P(ALL, None),
        P(None, ALL),
        P(None, ALL),
        P(ALL, None),
        P(ALL, None),
        P(ALL, None),
        P(ALL, None),
        P(None, ALL),
        P(None, ALL),
        P(ALL, None),
        P(ALL, None),
        P(ALL, None),
        P(ALL, None),
    )
    return jax.shard_map(local, mesh=chip_mesh, in_specs=in_specs, out_specs=out_specs, check_vma=False)
```

```python
import functools

import jax
import jax.numpy as jnp
from jax import lax
from jax.experimental import pallas as pl
from jax.experimental.pallas import tpu as pltpu
from jax.sharding import Mesh
from jax.sharding import PartitionSpec as P

STEP = 3


NORM_EPS = 1e-05
BETA_ONE = 0.9
BETA_TWO = 0.999
ADAM_EPS = 1e-08
RATE_MATRIX = 0.005
RATE_VECTOR = 0.2
DECAY = 0.1
LANES = 128
VMEM_SCATTER = 46 << 20
VMEM_GATHER = 60 << 20
UNIT_TILE = 512
MESH_ID = pl.DeviceIdType.MESH
SEQ = ("ring", "core")
ALL = ("ring", "core", "fsdp")


def snake(index):
    return 2 * (index // 2) + (index % 2 + index // 2) % 2


def halves(columns):
    first = (columns // 2 + LANES - 1) // LANES * LANES
    return (pl.ds(0, first), pl.ds(first, columns - first))


class Place:
    def __init__(self, chips, depth):
        self.chips, self.depth = chips, depth
        self.core = lax.axis_index("core")
        self.layer = lax.axis_index("fsdp")
        self.spot = snake(lax.axis_index("ring"))
        self.own = lax.axis_index("ring")
        self.right = self.device(snake((self.spot + 1) % chips), self.core, self.layer)
        self.left = self.device(snake((self.spot + chips - 1) % chips), self.core, self.layer)
        self.up = self.device(self.own, self.core, (self.layer + 1) % depth)
        self.down = self.device(self.own, self.core, (self.layer + depth - 1) % depth)
        self.sibling = self.device(self.own, 1 - self.core, self.layer)

    def device(self, ring, core, layer):
        return (ring, core, layer)

    def shard(self, spot, core, layer):
        return (snake(spot) * 2 + core) * self.depth + layer

    def greet(self):
        for device in (self.right, self.left, self.up, self.down, self.sibling):
            pl.semaphore_signal(
                pltpu.get_barrier_semaphore(), inc=1, device_id=device, device_id_type=MESH_ID
            )

    def await_greetings(self):
        pl.semaphore_wait(pltpu.get_barrier_semaphore(), 5)


def gather_kernel(chips, depth, groups, *refs):
    count, inputs = len(groups), sum(groups)
    wholes = refs[inputs : inputs + count]
    shards = refs[inputs + count : inputs + 2 * count]
    wide = refs[inputs + 2 * count : 2 * inputs + 2 * count]
    loaded, sent, from_sibling, from_below, from_ring, kept, late_ring, late_below = refs[
        2 * inputs + 2 * count :
    ]
    loads = [
        pltpu.make_async_copy(refs[index], wide[index], loaded.at[index])
        for index in range(inputs)
    ]
    for load in loads:
        load.start()
    here = Place(chips, depth)
    here.greet()
    for load in loads:
        load.wait()
    taken = 0
    for shard, members in zip(shards, groups):
        start = 0
        for member in wide[taken : taken + members]:
            shard[:, start : start + member.shape[1]] = member[...].astype(shard.dtype)
            start += member.shape[1]
        taken += members
    here.await_greetings()
    late = count - 1
    cuts = [halves(ref.shape[1]) for ref in shards]

    def block(which, shard):
        return wholes[which].at[shard]

    def piece_of(which, shard, way):
        return wholes[which].at[shard, :, cuts[which][way]]

    def send(source, target, which, arrived, device):
        pltpu.make_async_remote_copy(
            src_ref=source,
            dst_ref=target,
            send_sem=sent.at[which],
            recv_sem=arrived,
            device_id=device,
            device_id_type=MESH_ID,
        ).start()

    def awaited(ref, arrived):
        pltpu.make_async_copy(ref, ref, arrived).wait()

    own = here.shard(here.spot, here.core, here.layer)
    for which in range(late):
        send(shards[which], block(which, own), which, from_below.at[which, 0], here.up)
        for way in range(2):
            send(
                shards[which].at[:, cuts[which][way]],
                piece_of(which, own, way),
                which,
                from_ring.at[which, way, 0],
                (here.right, here.left)[way],
            )
    for way in range(2):
        part = shards[late].at[:, cuts[late][way]]
        piece = piece_of(late, own, way)
        send(part, piece, late, late_ring.at[way, 0], (here.right, here.left)[way])
        send(part, piece, late, late_below.at[way, 0], here.up)
    for which in range(count):
        send(shards[which], block(which, own), which, from_sibling.at[which], here.sibling)
        pltpu.make_async_copy(shards[which], block(which, own), kept.at[which]).start()

    def late_around(hop):
        for way in range(2):
            away = (chips - hop, hop)[way]
            piece = piece_of(late, here.shard((here.spot + away) % chips, here.core, here.layer), way)
            awaited(piece, late_ring.at[way, hop - 1])
            if hop < chips - 1:
                send(piece, piece, late, late_ring.at[way, hop], (here.right, here.left)[way])
            send(piece, piece, late, late_below.at[way, hop], here.up)
            send(piece, piece, late, from_sibling.at[late], here.sibling)

    def late_layer(layer_step, hop):
        layer = (here.layer + depth - layer_step) % depth
        for way in range(2):
            away = (chips - hop, hop)[way]
            piece = piece_of(late, here.shard((here.spot + away) % chips, here.core, layer), way)
            awaited(piece, late_below.at[way, (layer_step - 1) * chips + hop])

            @pl.when(layer_step < depth - 1)
            def _():
                send(piece, piece, late, late_below.at[way, layer_step * chips + hop], here.up)

            send(piece, piece, late, from_sibling.at[late], here.sibling)

    def late_step(layer_step, hop):
        if hop > 0:
            @pl.when(layer_step == 0)
            def _():
                late_around(hop)

        @pl.when(layer_step > 0)
        def _():
            late_layer(layer_step, hop)

    def around(hop, layer_step):
        layer = (here.layer + depth - layer_step) % depth
        for which in range(late):
            for way in range(2):
                away = (chips - hop, hop)[way]
                shard = here.shard((here.spot + away) % chips, here.core, layer)
                arrived = layer_step * (chips - 1) + hop - 1
                piece = piece_of(which, shard, way)
                awaited(piece, from_ring.at[which, way, arrived])
                if hop < chips - 1:
                    send(
                        piece,
                        piece,
                        which,
                        from_ring.at[which, way, arrived + 1],
                        (here.right, here.left)[way],
                    )
                send(piece, piece, which, from_sibling.at[which], here.sibling)

    def layer_arrives(layer_step):
        layer = (here.layer + depth - layer_step) % depth
        shard = here.shard(here.spot, here.core, layer)
        for which in range(late):
            whole = block(which, shard)
            awaited(whole, from_below.at[which, layer_step - 1])

            @pl.when(layer_step < depth - 1)
            def _():
                send(whole, whole, which, from_below.at[which, layer_step], here.up)

            for way in range(2):
                piece = piece_of(which, shard, way)
                send(
                    piece,
                    piece,
                    which,
                    from_ring.at[which, way, layer_step * (chips - 1)],
                    (here.right, here.left)[way],
                )
            send(whole, whole, which, from_sibling.at[which], here.sibling)

    @pl.loop(0, depth)
    def _(layer_step):
        for hop in range(1, chips - 1):
            around(hop, layer_step)
            late_step(layer_step, hop - 1)

        @pl.when(layer_step < depth - 1)
        def _():
            layer_arrives(layer_step + 1)

        around(chips - 1, layer_step)
        late_step(layer_step, chips - 2)
        late_step(layer_step, chips - 1)

    shard_count = 2 * chips * depth
    for which in range(count):
        pltpu.make_async_copy(shards[which], block(which, own), kept.at[which]).wait()
        awaited(wholes[which].at[pl.ds(0, shard_count // 2)], from_sibling.at[which])
        awaited(wholes[which].at[pl.ds(0, shard_count - 1)], sent.at[which])


def gather(chips, depth, *groups):
    count = len(groups)
    steps = depth * (chips - 1)
    shard_count = 2 * chips * depth
    shapes = [(g[0].shape[0], sum(x.shape[1] for x in g)) for g in groups]
    half = jnp.bfloat16
    return pl.pallas_call(
        functools.partial(gather_kernel, chips, depth, [len(g) for g in groups]),
        out_shape=[jax.ShapeDtypeStruct((shard_count,) + shape, half) for shape in shapes],
        in_specs=[pl.BlockSpec(memory_space=pl.ANY)] * sum(len(g) for g in groups),
        out_specs=[pl.BlockSpec(memory_space=pl.ANY)] * count,
        scratch_shapes=[pltpu.VMEM(shape, half) for shape in shapes]
        + [pltpu.VMEM(x.shape, x.dtype) for g in groups for x in g]
        + [
            pltpu.SemaphoreType.DMA((sum(len(g) for g in groups),)),
            pltpu.SemaphoreType.DMA((count,)),
            pltpu.SemaphoreType.DMA((count,)),
            pltpu.SemaphoreType.DMA((count, depth - 1)),
            pltpu.SemaphoreType.DMA((count, 2, steps)),
            pltpu.SemaphoreType.DMA((count,)),
            pltpu.SemaphoreType.DMA((2, chips - 1)),
            pltpu.SemaphoreType.DMA((2, chips * (depth - 1))),
        ],
        compiler_params=pltpu.CompilerParams(
            collective_id=0, has_side_effects=True, vmem_limit_bytes=VMEM_GATHER
        ),
        name="gather_weights",
    )(*[x for g in groups for x in g])


def scatter_kernel(chips, depth, count, *refs):
    grads = refs[:count]
    owned = refs[count : 2 * count]
    rest = refs[2 * count :]
    theirs = rest[:count]
    staged = rest[count : 2 * count]
    ringed = rest[2 * count : 3 * count]
    layered = rest[3 * count : 4 * count]
    sent, loaded, from_sibling, from_below, from_ring, late_below = rest[4 * count :]
    here = Place(chips, depth)
    late = count - 1
    cuts = [halves(ref.shape[1]) for ref in owned]
    f32 = jnp.float32

    def part(which, shard, way):
        if len(grads[which].shape) == 4:
            return grads[which].at[way, shard]
        return grads[which].at[shard, :, cuts[which][way]]

    def place(hop, way):
        away = (chips - hop, hop)[way]
        return (here.spot + away) % chips

    def layer_of(layer_step):
        return (here.layer + 2 * depth - 1 - layer_step) % depth

    def slot_of(layer_step, hop):
        return layer_step * chips + hop - 1

    def load(which, layer_step, hop, start):
        for way, cut in enumerate(cuts[which]):
            shard = here.shard(place(hop, way), here.core, layer_of(layer_step))
            copy = pltpu.make_async_copy(
                part(which, shard, way),
                staged[which].at[hop - 1, :, cut],
                loaded.at[which, way, hop - 1],
            )
            copy.start() if start else copy.wait()

    def hand_over(which, slot):
        layer_step = slot // chips
        hop = slot % chips + 1
        for way, cut in enumerate(cuts[which]):
            shard = here.shard(place(hop, way), 1 - here.core, layer_of(layer_step))
            pltpu.make_async_remote_copy(
                src_ref=part(which, shard, way),
                dst_ref=theirs[which].at[slot, :, cut],
                send_sem=sent.at[which],
                recv_sem=from_sibling.at[which, way, slot],
                device_id=here.sibling,
                device_id_type=MESH_ID,
            ).start()

    slots = chips * depth
    for hop in range(1, chips + 1):
        for which in range(count):
            load(which, 0, hop, True)
    here.greet()
    here.await_greetings()

    @pl.loop(0, slots)
    def _(slot):
        for which in reversed(range(count)):
            hand_over(which, slot)

    def got(ref, semaphore):
        pltpu.make_async_copy(ref, ref, semaphore).wait()

    def step(layer_step, hop):
        slot = slot_of(layer_step, hop)
        for which in range(late):
            load(which, layer_step, hop, False)
            if hop == chips:
                @pl.when(layer_step > 0)
                def _():
                    ref = layered[which].at[layer_step - 1]
                    got(ref, from_below.at[which, layer_step - 1])

            for way, cut in enumerate(cuts[which]):
                mine = theirs[which].at[slot, :, cut]
                got(mine, from_sibling.at[which, way, slot])
                total = mine[...].astype(f32) + staged[which][hop - 1, :, cut].astype(f32)
                if hop > 1:
                    index = layer_step * (chips - 1) + hop - 2
                    arrived = ringed[which].at[index, :, cut]
                    got(arrived, from_ring.at[which, way, index])
                    total = total + arrived[...].astype(f32)
                if hop < chips:
                    index = layer_step * (chips - 1) + hop - 1
                    mine[...] = total.astype(mine.dtype)
                    pltpu.make_async_remote_copy(
                        src_ref=mine,
                        dst_ref=ringed[which].at[index, :, cut],
                        send_sem=sent.at[which],
                        recv_sem=from_ring.at[which, way, index],
                        device_id=(here.right, here.left)[way],
                        device_id_type=MESH_ID,
                    ).start()
                else:
                    owned[which][:, cut] = total

            if hop == chips:
                @pl.when(layer_step > 0)
                def _():
                    owned[which][...] += layered[which][layer_step - 1].astype(f32)

                @pl.when(layer_step < depth - 1)
                def _():
                    mine = theirs[which].at[slot]
                    mine[...] = owned[which][...].astype(mine.dtype)
                    pltpu.make_async_remote_copy(
                        src_ref=mine,
                        dst_ref=layered[which].at[layer_step],
                        send_sem=sent.at[which],
                        recv_sem=from_below.at[which, layer_step],
                        device_id=here.up,
                        device_id_type=MESH_ID,
                    ).start()

        @pl.when(layer_step < depth - 1)
        def _():
            for which in range(late):
                load(which, layer_step + 1, hop, True)

    def late_step(layer_step, hop):
        slot = slot_of(layer_step, hop)
        load(late, layer_step, hop, False)
        for way, cut in enumerate(cuts[late]):
            mine = theirs[late].at[slot, :, cut]
            got(mine, from_sibling.at[late, way, slot])
            total = mine[...].astype(f32) + staged[late][hop - 1, :, cut].astype(f32)
            mine[...] = total.astype(mine.dtype)

            @pl.when(layer_step > 0)
            def _():
                before = slot_of(layer_step - 1, hop)
                arrived = layered[late].at[before, :, cut]
                got(arrived, late_below.at[way, before])
                both = total + arrived[...].astype(f32)
                mine[...] = both.astype(mine.dtype)

            @pl.when(layer_step < depth - 1)
            def _():
                pltpu.make_async_remote_copy(
                    src_ref=mine,
                    dst_ref=layered[late].at[slot, :, cut],
                    send_sem=sent.at[late],
                    recv_sem=late_below.at[way, slot],
                    device_id=here.up,
                    device_id_type=MESH_ID,
                ).start()

            @pl.when(layer_step == depth - 1)
            def _():
                around = mine[...].astype(f32)
                if hop > 1:
                    arrived = ringed[late].at[hop - 2, :, cut]
                    got(arrived, from_ring.at[late, way, hop - 2])
                    around = around + arrived[...].astype(f32)
                if hop < chips:
                    mine[...] = around.astype(mine.dtype)
                    pltpu.make_async_remote_copy(
                        src_ref=mine,
                        dst_ref=ringed[late].at[hop - 1, :, cut],
                        send_sem=sent.at[late],
                        recv_sem=from_ring.at[late, way, hop - 1],
                        device_id=(here.right, here.left)[way],
                        device_id_type=MESH_ID,
                    ).start()
                else:
                    owned[late][:, cut] = around

        @pl.when(layer_step < depth - 1)
        def _():
            load(late, layer_step + 1, hop, True)

    late_step(0, 1)
    step(0, 1)
    for hop in range(2, chips + 1):
        late_step(0, hop)

    @pl.loop(0, depth)
    def _(layer_step):
        def late_ahead(hop):
            @pl.when(layer_step < depth - 1)
            def _():
                late_step(layer_step + 1, hop)

        step(layer_step, 2)
        for hop in range(3, chips):
            step(layer_step, hop)
            late_ahead(hop - 2)

        @pl.when(layer_step < depth - 1)
        def _():
            step(layer_step + 1, 1)

        late_ahead(chips - 2)
        step(layer_step, chips)
        late_ahead(chips - 1)
        late_ahead(chips)

    for which in range(count):
        some = pl.ds(0, 2 * slots - 1)
        most = grads[which].at[:, some] if len(grads[which].shape) == 4 else grads[which].at[some]
        pltpu.make_async_copy(most, most, sent.at[which]).wait()


def scatter(chips, depth, *grads):
    count = len(grads)
    slots = chips * depth
    steps = depth * (chips - 1)
    shapes = [
        (g.shape[1], g.shape[2]) if g.ndim == 3 else (g.shape[2], 2 * g.shape[3]) for g in grads
    ]
    anywhere = pl.BlockSpec(memory_space=pl.ANY)
    inner = pl.BlockSpec(memory_space=pltpu.VMEM)

    def room(most, last):
        leading = [most] * (count - 1) + [last]
        return [pltpu.VMEM((n,) + x, jnp.bfloat16) for n, x in zip(leading, shapes)]

    return pl.pallas_call(
        functools.partial(scatter_kernel, chips, depth, count),
        out_shape=[jax.ShapeDtypeStruct(x, jnp.float32) for x in shapes],
        in_specs=[anywhere] * count,
        out_specs=[inner] * count,
        scratch_shapes=room(slots, slots)
        + room(chips, chips)
        + room(steps, chips - 1)
        + room(depth - 1, chips * (depth - 1))
        + [
            pltpu.SemaphoreType.DMA((count,)),
            pltpu.SemaphoreType.DMA((count, 2, chips)),
            pltpu.SemaphoreType.DMA((count, 2, slots)),
            pltpu.SemaphoreType.DMA((count, depth - 1)),
            pltpu.SemaphoreType.DMA((count, 2, steps)),
            pltpu.SemaphoreType.DMA((2, chips * (depth - 1))),
        ],
        compiler_params=pltpu.CompilerParams(
            collective_id=1, has_side_effects=True, vmem_limit_bytes=VMEM_SCATTER
        ),
        name="scatter_gradients",
    )(*grads)


def from_behind(value, axis, steps):
    count = lax.axis_size(axis)
    first, last = (max(0, -steps), min(count, count - steps))
    return lax.ppermute(value, axis, [(source, source + steps) for source in range(first, last)])


def matmul(left, right):
    return jnp.dot(left, right, preferred_element_type=jnp.float32)


def matmul_tn(left, right):
    return lax.dot_general(
        left, right, (((0,), (0,)), ((), ())), preferred_element_type=jnp.float32
    )


def matmul_nt(left, right):
    return lax.dot_general(
        left, right, (((1,), (1,)), ((), ())), preferred_element_type=jnp.float32
    )


def inverse_rms(values):
    return lax.rsqrt(jnp.mean(values * values, axis=-1, keepdims=True) + NORM_EPS)


def norm_backward(values, scale, gain, grad_normed):
    weighted = grad_normed * gain
    grad_gain = jnp.sum(grad_normed * values * scale, axis=0)
    cubed = scale * scale * scale
    grad_values = scale * weighted - values * cubed * jnp.mean(
        weighted * values, axis=-1, keepdims=True
    )
    return (grad_values, grad_gain)


def adamw_update(param, grad, first, second, rate, decay):
    first_new = BETA_ONE * first + (1.0 - BETA_ONE) * grad
    second_new = BETA_TWO * second + (1.0 - BETA_TWO) * grad * grad
    first_hat = first_new / (1.0 - BETA_ONE**STEP)
    second_hat = second_new / (1.0 - BETA_TWO**STEP)
    param_new = param - rate * (first_hat / (jnp.sqrt(second_hat) + ADAM_EPS) + decay * param)
    return (param_new, first_new, second_new)


def adamw_kernel(*refs):
    grads, state, outs = refs[:4], refs[4:22], refs[22:]
    side, lanes, width = grads[0], outs[0].shape[1], outs[3].shape[1]
    vectors = side[:8, width:]
    found = [vectors[:2, :lanes], vectors[2:5, :lanes], grads[1][...], side[:, :width]]
    found += [ref[...] for ref in grads[2:]]
    for index, grad in enumerate(found):
        rate, decay = (RATE_VECTOR, 0.0) if index < 2 else (RATE_MATRIX, DECAY)
        param, first, second = (state[6 * kind + index][...] for kind in range(3))
        new = adamw_update(param, grad, first, second, rate, decay)
        for kind, value in enumerate((grad,) + new):
            outs[6 * kind + index][...] = value


def adamw(grads, params, firsts, seconds):
    inner = pl.BlockSpec(memory_space=pltpu.VMEM)
    return pl.pallas_call(
        adamw_kernel,
        out_shape=[jax.ShapeDtypeStruct(p.shape, p.dtype) for p in params] * 4,
        in_specs=[inner] * 22,
        out_specs=[inner] * 24,
        compiler_params=pltpu.CompilerParams(vmem_limit_bytes=48 << 20),
        name="adamw",
    )(*grads, *params, *firsts, *seconds)


def feed_forward_kernel(
    normed, resid, cot, gate, up, down, out, grad_normed, grad_down, grad_gate_up, turned
):
    half = jnp.bfloat16

    @pl.when(pl.program_id(0) == 0)
    def _():
        turned[...] = normed[...].T
        out[...] = resid[...]
        grad_normed[...] = jnp.zeros_like(grad_normed)

    gate_pre = matmul(normed[...], gate[...])
    up_pre = matmul(normed[...], up[...])
    grad_act = matmul_nt(cot[...], down[...])
    sigmoid_gate = jax.nn.sigmoid(gate_pre)
    silu_gate = gate_pre * sigmoid_gate
    act = (silu_gate * up_pre).astype(half)
    grad_gate = grad_act * up_pre * sigmoid_gate * (1.0 + gate_pre * (1.0 - sigmoid_gate))
    grad_gate = grad_gate.astype(half)
    grad_up = (grad_act * silu_gate).astype(half)
    out[...] += matmul(act, down[...])
    grad_normed[...] += matmul_nt(grad_gate, gate[...]) + matmul_nt(grad_up, up[...])
    grad_down[...] = matmul_tn(act, cot[...]).astype(half)
    grad_gate_up[0] = matmul(turned[...], grad_gate).astype(half)
    grad_gate_up[1] = matmul(turned[...], grad_up).astype(half)


def feed_forward(normed, resid, cot, gate_up, down):
    tokens, width = normed.shape
    units = down.shape[0]
    tile = UNIT_TILE
    tiles = units // tile
    half, single = jnp.bfloat16, jnp.float32

    def fixed(rows, columns):
        return pl.BlockSpec((rows, columns), lambda i: (0, 0))

    flops = 2 * tokens * width * units * 9
    return pl.pallas_call(
        feed_forward_kernel,
        grid=(tiles,),
        out_shape=[
            jax.ShapeDtypeStruct((tokens, width), single),
            jax.ShapeDtypeStruct((tokens, width), single),
            jax.ShapeDtypeStruct((units, width), half),
            jax.ShapeDtypeStruct((2, width, units), half),
        ],
        in_specs=[
            fixed(tokens, width),
            fixed(tokens, width),
            fixed(tokens, width),
            pl.BlockSpec((width, tile), lambda i: (0, i)),
            pl.BlockSpec((width, tile), lambda i: (0, i + tiles)),
            pl.BlockSpec((tile, width), lambda i: (i, 0)),
        ],
        out_specs=[
            fixed(tokens, width),
            fixed(tokens, width),
            pl.BlockSpec((tile, width), lambda i: (i, 0)),
            pl.BlockSpec((2, width, tile), lambda i: (0, 0, i)),
        ],
        scratch_shapes=[pltpu.VMEM((width, tokens), half)],
        compiler_params=pltpu.CompilerParams(vmem_limit_bytes=48 << 20),
        cost_estimate=pl.CostEstimate(
            flops=flops, bytes_accessed=12 * width * units, transcendentals=tokens * units
        ),
        name="feed_forward",
    )(normed, resid, cot, gate_up, gate_up, down)


def local(
    hidden_in,
    cotangent,
    doc_position,
    norm_gains,
    conv_taps,
    in_proj,
    out_proj,
    gate_up,
    down_proj,
    first_gains,
    first_taps,
    first_in,
    first_out,
    first_gate_up,
    first_down,
    second_gains,
    second_taps,
    second_in,
    second_out,
    second_gate_up,
    second_down,
):
    half = jnp.bfloat16
    single = jnp.float32
    row_count, length, width = hidden_in.shape
    tok_count = row_count * length
    chips, depth = lax.axis_size("ring"), lax.axis_size("fsdp")
    in_width = in_proj.shape[1]
    out_width = out_proj.shape[1]
    rows = gate_up.shape[0]
    shards = 2 * chips * depth
    vectors = jnp.concatenate([norm_gains, conv_taps], axis=0)
    vector_count, lanes = vectors.shape
    corner = ((0, rows - vector_count), (0, LANES - lanes))
    gate_shards, down_shards, mixer_shards = gather(
        chips, depth, (gate_up,), (down_proj,), (in_proj, out_proj, jnp.pad(vectors, corner))
    )
    gate_full = gate_shards.reshape(width, -1)
    down_full = down_shards.reshape(-1, width)
    mixer_columns = mixer_shards.reshape(width, -1)
    in_full = mixer_columns[:, :in_width]
    out_full = mixer_columns[:, in_width : in_width + out_width]
    vectors_full = mixer_shards[:, :vector_count, -LANES:][:, :, :lanes].astype(single)
    vectors_full = vectors_full.transpose(1, 0, 2).reshape(vector_count, width)
    mixer_full = (None, None, in_full, out_full)
    gains_f = vectors_full[:2]
    taps_f = vectors_full[2:5]
    resid_one = hidden_in.reshape(tok_count, width).astype(single)
    scale_one = inverse_rms(resid_one)
    normed_one = (resid_one * scale_one * gains_f[0]).astype(half)
    projected = matmul(normed_one, mixer_full[2])
    b_branch = projected[:, :width]
    c_branch = projected[:, width : 2 * width]
    x_branch = projected[:, 2 * width :]
    gated_input = (b_branch * x_branch).astype(half)
    gated_rows = gated_input.reshape(row_count, length, width)
    carried = from_behind(gated_rows[:, length - 2 :, :], SEQ, 1)
    extended = jnp.concatenate([carried, gated_rows], axis=1).astype(single)
    gated_f = extended[:, 2:].reshape(tok_count, width)
    prev_one = extended[:, 1 : length + 1].reshape(tok_count, width)
    prev_two = extended[:, :length].reshape(tok_count, width)
    positions = doc_position.reshape(tok_count)
    mask_one = (positions >= 1).astype(single)[:, None]
    mask_two = (positions >= 2).astype(single)[:, None]
    conv_out = (
        taps_f[0] * gated_f + mask_one * taps_f[1] * prev_one + mask_two * taps_f[2] * prev_two
    )
    mixer_act = (c_branch * conv_out).astype(half)
    resid_two = resid_one + matmul(mixer_act, mixer_full[3])
    scale_two = inverse_rms(resid_two)
    normed_two = (resid_two * scale_two * gains_f[1]).astype(half)
    cot_rows = cotangent.reshape(tok_count, width)
    block_out, grad_normed, grad_down, grad_gate_up = feed_forward(
        normed_two, resid_two, cot_rows, gate_full, down_full
    )
    norm_part, gain_two_grad = norm_backward(resid_two, scale_two, gains_f[1], grad_normed)
    grad_resid = cot_rows.astype(single) + norm_part
    resid_cast = grad_resid.astype(half)
    grad_mixer = matmul_nt(resid_cast, mixer_full[3])
    grad_cbranch = grad_mixer * conv_out
    grad_conv = grad_mixer * c_branch
    masked_one = mask_one * grad_conv
    masked_two = mask_two * grad_conv
    grad_taps = jnp.stack(
        [
            jnp.sum(grad_conv * gated_f, axis=0),
            jnp.sum(masked_one * prev_one, axis=0),
            jnp.sum(masked_two * prev_two, axis=0),
        ]
    )
    one_rows = masked_one.reshape(row_count, length, width)
    two_rows = masked_two.reshape(row_count, length, width)
    leading = from_behind((one_rows[:, :2, :], two_rows[:, :2, :]), SEQ, -1)
    ext_one = jnp.concatenate([one_rows, leading[0]], axis=1)
    ext_two = jnp.concatenate([two_rows, leading[1]], axis=1)
    next_one = ext_one[:, 1 : length + 1].reshape(tok_count, width)
    next_two = ext_two[:, 2 : length + 2].reshape(tok_count, width)
    grad_gated = taps_f[0] * grad_conv + taps_f[1] * next_one + taps_f[2] * next_two
    grad_proj = jnp.concatenate(
        [grad_gated * x_branch, grad_cbranch, grad_gated * b_branch], axis=1
    ).astype(half)
    grad_normone = matmul_nt(grad_proj, mixer_full[2])
    first_part, gain_one_grad = norm_backward(resid_one, scale_one, gains_f[0], grad_normone)
    grad_hidden = grad_resid + first_part
    grad_gains = jnp.stack([gain_one_grad, gain_two_grad])
    grad_in = matmul_tn(normed_one, grad_proj)
    grad_out = matmul_tn(mixer_act, resid_cast)
    vector_grads = jnp.concatenate([grad_gains, grad_taps], axis=0)
    vector_shards = vector_grads.reshape(vector_count, shards, lanes).transpose(1, 0, 2)
    vector_shards = jnp.pad(vector_shards.astype(half), ((0, 0),) + corner)
    grad_side = jnp.concatenate(
        [grad_out.astype(half).reshape(shards, rows, out_width), vector_shards], axis=2
    )
    gate_owned, in_owned, side_owned, down_owned = scatter(
        chips,
        depth,
        grad_gate_up.reshape(2, shards, rows, -1),
        grad_in.astype(half).reshape(shards, rows, in_width),
        grad_side,
        grad_down.reshape(shards, -1, width),
    )
    params = (norm_gains, conv_taps, in_proj, out_proj, gate_up, down_proj)
    firsts = (first_gains, first_taps, first_in, first_out, first_gate_up, first_down)
    seconds = (second_gains, second_taps, second_in, second_out, second_gate_up, second_down)
    owned = (side_owned, in_owned, gate_owned, down_owned)
    results = adamw(owned, params, firsts, seconds)
    out_rows = block_out.reshape(row_count, length, width)
    grad_rows = grad_hidden.reshape(row_count, length, width)
    return (
        out_rows,
        grad_rows,
        *results,
    )


def solution(mesh):
    tokens, depth = mesh.devices.shape
    chip_mesh = Mesh(mesh.devices.reshape(tokens // 2, 2, depth), ALL)
    in_specs = (
        P("fsdp", SEQ, None),
        P("fsdp", SEQ, None),
        P("fsdp", SEQ),
        P(None, ALL),
        P(None, ALL),
        P(ALL, None),
        P(ALL, None),
        P(ALL, None),
        P(ALL, None),
        P(None, ALL),
        P(None, ALL),
        P(ALL, None),
        P(ALL, None),
        P(ALL, None),
        P(ALL, None),
        P(None, ALL),
        P(None, ALL),
        P(ALL, None),
        P(ALL, None),
        P(ALL, None),
        P(ALL, None),
    )
    out_specs = (
        P("fsdp", SEQ, None),
        P("fsdp", SEQ, None),
        P(None, ALL),
        P(None, ALL),
        P(ALL, None),
        P(ALL, None),
        P(ALL, None),
        P(ALL, None),
        P(None, ALL),
        P(None, ALL),
        P(ALL, None),
        P(ALL, None),
        P(ALL, None),
        P(ALL, None),
        P(None, ALL),
        P(None, ALL),
        P(ALL, None),
        P(ALL, None),
        P(ALL, None),
        P(ALL, None),
        P(None, ALL),
        P(None, ALL),
        P(ALL, None),
        P(ALL, None),
        P(ALL, None),
        P(ALL, None),
    )
    return jax.shard_map(local, mesh=chip_mesh, in_specs=in_specs, out_specs=out_specs, check_vma=False)
```
